32 devices in a mesh: groups: 2 (over y), seq: 4 (over z), head: 2 (over x), dp: 2 (over core).
Axes of the slice: x: 2, y: 2, z: 4, core: 2. Of those that a mesh axis runs over, the one named last changes fastest.
Arguments:
- x_input: bfloat16 [4, 1024, 5120], P(('groups', 'dp'), 'seq', 'head'), parts along dimension 0, may hold values from -6 to 6
- bc_input: bfloat16 [4, 1024, 256], P(('groups', 'dp'), 'seq'), parts along dimension 0, may hold values from -6 to 6
- decays: float32 [4, 80, 1024], P(('groups', 'dp'), 'head', 'seq'), parts along dimension 0, may hold values from 0.5 to 1, as said below
- conv_x: float32 [4, 5120], P(None, 'head'), may hold values from -3 to 3
- conv_bc: float32 [4, 256], replicated, may hold values from -3 to 3
- skip_gain: float32 [80], P('head'), may hold values from 0.5 to 2
- grad_out: bfloat16 [4, 1024, 5120], P(('groups', 'dp'), 'seq', 'head'), parts along dimension 0, may hold values from -6 to 6
Outputs:
- y_output: bfloat16 [4, 1024, 5120], P(('groups', 'dp'), 'seq', 'head'), parts along dimension 0
- grad_x: bfloat16 [4, 1024, 5120], P(('groups', 'dp'), 'seq', 'head'), parts along dimension 0
- grad_bc: bfloat16 [4, 1024, 256], P(('groups', 'dp'), 'seq'), parts along dimension 0
- grad_conv_x: float32 [8, 5120], P('groups', 'head'), parts along dimension 0
- grad_conv_bc: float32 [8, 256], P('groups'), parts along dimension 0
- grad_skip: float32 [160], P(('groups', 'head')), parts along dimension 0
The draws below stay inside these ranges and needn't reach their ends.
There are 2 independent parts, one for each index of `groups`. The reference program is written for one: setup_inputs(seed, part) draws one part's arguments, and reference() takes and returns one part's arrays. A program takes and returns all parts, laid end to end along the dimension named above; an argument that names none is the same for every part. Nothing has to cross between parts.
Inputs may be any that keep to these rules, and one draw needn't show every extreme that they name: `decays`: every decay is strictly below 1.
All inputs are finite; a program needn't handle non-finite values.
Results may differ from the reference program's by a relative error of at most 0.009.
Values may be sent and summed in bfloat16 or wider, within the bound.
A program may use at most 64 MiB of HBM per device.

```python
import math
import jax
import jax.numpy as jnp
from jax import lax

NUMBER_OF_HEADS = 80
HEAD_DIM = 64
STATE_DIM = 128
BLOCK_LEN = 256
CONV_WIDTH = 4
INNER_DIM = 5120
SEQUENCE_LENGTH = 1024
GROUP_SEQUENCES = 2


def draw_decays(key, part):
    random_subkeys = jax.random.split(key, 7)
    position = jnp.arange(SEQUENCE_LENGTH, dtype=jnp.float32)[None, None, :]
    fast_share = 0.5
    head_shape = (GROUP_SEQUENCES, NUMBER_OF_HEADS, 1)
    full_shape = (GROUP_SEQUENCES, NUMBER_OF_HEADS, SEQUENCE_LENGTH)
    is_fast = jax.random.uniform(random_subkeys[0], head_shape) < fast_share
    memory = jnp.exp(jax.random.uniform(random_subkeys[1], head_shape, minval=math.log(30.0), maxval=math.log(50.0)))
    slow_rate = jnp.exp(jax.random.uniform(random_subkeys[2], head_shape, minval=math.log(0.05), maxval=math.log(0.6))) / SEQUENCE_LENGTH
    base_rate = jnp.where(is_fast, 1.0 / memory, slow_rate)
    jitter = jnp.exp(jax.random.uniform(random_subkeys[3], full_shape, minval=-0.7, maxval=0.7))
    phase_shift = jax.random.uniform(random_subkeys[4], head_shape, minval=0.0, maxval=2.0 * math.pi)
    wave_factor = jnp.exp(0.7 * jnp.sin(2.0 * math.pi * 3.0 * position / SEQUENCE_LENGTH + phase_shift))
    every_rate = base_rate * jitter * wave_factor
    spike_position = jax.random.randint(random_subkeys[5], (GROUP_SEQUENCES, NUMBER_OF_HEADS, 2), 0, SEQUENCE_LENGTH)
    spike_flag = jnp.any(jnp.arange(SEQUENCE_LENGTH)[None, None, :, None] == spike_position[:, :, None, :], axis=-1)
    retained_values = jax.random.uniform(random_subkeys[6], full_shape, minval=0.5, maxval=0.8)
    logarithm_decay = jnp.where(spike_flag, jnp.log(retained_values), -every_rate)
    return jnp.exp(logarithm_decay).astype(jnp.float32)


def block_scale(own_key, shape, shards, least, top_value):
    gain, own = 1.0, jax.random.fold_in(own_key, 6)
    for axis_at, parts in shards:
        heights = jnp.exp(jax.random.uniform(jax.random.fold_in(own, axis_at), (parts,), jnp.float32, least / len(shards), top_value / len(shards)))
        gain = gain * jnp.repeat(heights, shape[axis_at] // parts).reshape([-1 if axis == axis_at else 1 for axis in range(len(shape))])
    return gain


def normal_values(key, shape, width, most, cuts=(), held_as=jnp.bfloat16):
    level = block_scale(key, shape, cuts, -0.22, 0.18) if cuts else 1.0
    array = jax.random.normal(key, shape, jnp.float32) * width * level
    return jnp.minimum(jnp.maximum(array, -most), most).astype(held_as)


def setup_inputs(seed: int = 0, part: int = 0) -> dict:
    splits = jax.random.split(jax.random.key(seed), 8)
    part_keys = jax.random.split(jax.random.fold_in(splits[7], part), 8)
    return {
        "x_input": normal_values(part_keys[0], (GROUP_SEQUENCES, SEQUENCE_LENGTH, INNER_DIM), 1.0, 6.0, ((0, 2), (1, 4), (2, 2))),
        "bc_input": normal_values(part_keys[1], (GROUP_SEQUENCES, SEQUENCE_LENGTH, 2 * STATE_DIM), 1.0, 6.0, ((0, 2), (1, 4))),
        "decays": draw_decays(jax.random.fold_in(jax.random.fold_in(splits[7], part), 71), part),
        "conv_x": normal_values(splits[3], (CONV_WIDTH, INNER_DIM), CONV_WIDTH ** -0.5, 3.0, ((1, 2),), jnp.float32),
        "conv_bc": normal_values(splits[4], (CONV_WIDTH, 2 * STATE_DIM), CONV_WIDTH ** -0.5, 3.0, (), jnp.float32),
        "skip_gain": jnp.clip(jnp.exp(math.log(2.0) - 1.3862944 * jax.random.uniform(splits[5], (NUMBER_OF_HEADS,), jnp.float32) ** block_scale(splits[5], (NUMBER_OF_HEADS,), ((0, 2),), -0.2, 0.2)), 0.5, 2.0),
        "grad_out": normal_values(part_keys[6], (GROUP_SEQUENCES, SEQUENCE_LENGTH, INNER_DIM), 1.0, 6.0, ((0, 2), (1, 4), (2, 2))),
    }


highest = lax.Precision.HIGHEST

def silu_grad(pre):
    sigma = jax.nn.sigmoid(pre)
    return sigma * (1.0 + pre * (1.0 - sigma))

def conv_forward(padded, weight, length):
    total = jnp.zeros((length, weight.shape[1]), jnp.float32)
    for shift in range(weight.shape[0]):
        total = total + weight[shift][None, :] * padded[shift:shift + length].astype(jnp.float32)
    return total

def conv_backward(pregrad, weight):
    taps = weight.shape[0]
    length = pregrad.shape[0]
    padded = jnp.concatenate([pregrad, jnp.zeros((taps - 1, pregrad.shape[1]), jnp.float32)], axis=0)
    total = jnp.zeros(pregrad.shape, jnp.float32)
    for shift in range(taps):
        total = total + weight[shift][None, :] * padded[taps - 1 - shift:taps - 1 - shift + length]
    return total

def conv_weight_grad(pregrad, padded, taps):
    length = pregrad.shape[0]
    return jnp.stack([lax.optimization_barrier(jnp.sum(pregrad * padded[shift:shift + length].astype(jnp.float32), axis=0)) for shift in range(taps)])

def decay_matrix(cum_block):
    size = cum_block.shape[-1]
    rows = jnp.arange(size)
    lower = (rows[:, None] >= rows[None, :])[None]
    diff = cum_block[:, :, None] - cum_block[:, None, :]
    return jnp.where(lower, jnp.exp(jnp.where(lower, diff, 0.0)), 0.0)

def one_row(x_row, bc_row, decay_row, conv_x, conv_bc, skip_gain, grad_row):
    length = x_row.shape[0]
    scale = STATE_DIM ** (-0.5)
    taps = CONV_WIDTH
    x_pad = jnp.concatenate([jnp.zeros((taps - 1, INNER_DIM), jnp.bfloat16), x_row], axis=0)
    bc_pad = jnp.concatenate([jnp.zeros((taps - 1, 2 * STATE_DIM), jnp.bfloat16), bc_row], axis=0)
    pre_x = conv_forward(x_pad, conv_x, length)
    pre_bc = conv_forward(bc_pad, conv_bc, length)
    inner = jax.nn.silu(pre_x).astype(jnp.bfloat16)
    mapped = jax.nn.silu(pre_bc).astype(jnp.bfloat16)
    b_mat = mapped[:, :STATE_DIM]
    c_mat = mapped[:, STATE_DIM:]
    logarithm_decay = jnp.log(decay_row)
    input_gain = jnp.sqrt(-jnp.expm1(2.0 * logarithm_decay))
    inner_heads = inner.astype(jnp.float32).reshape(length, NUMBER_OF_HEADS, HEAD_DIM)
    weighted = (inner_heads * input_gain.T[:, :, None]).astype(jnp.bfloat16)
    blocks = length // BLOCK_LEN
    cum = jnp.cumsum(logarithm_decay.reshape(NUMBER_OF_HEADS, blocks, BLOCK_LEN), axis=-1).transpose(1, 0, 2)
    w_blocks = weighted.reshape(blocks, BLOCK_LEN, NUMBER_OF_HEADS, HEAD_DIM)
    b_blocks = b_mat.reshape(blocks, BLOCK_LEN, STATE_DIM)
    c_blocks = c_mat.reshape(blocks, BLOCK_LEN, STATE_DIM)
    g_blocks = grad_row.reshape(blocks, BLOCK_LEN, NUMBER_OF_HEADS, HEAD_DIM)

    def forward_step(state, item):
        cum_b, w_b, b_b, c_b = item
        sim = jnp.dot(c_b, b_b.T, preferred_element_type=jnp.float32)
        mixing = (decay_matrix(cum_b) * sim[None]).astype(jnp.bfloat16)
        intra = jnp.einsum('hij,jhp->ihp', mixing.astype(jnp.float32), w_b.astype(jnp.float32))
        inter = jnp.exp(cum_b).T[:, :, None] * jnp.einsum('in,hpn->ihp', c_b.astype(jnp.float32), state, precision=highest)
        tail = jnp.exp(cum_b[:, -1:] - cum_b)
        update = jnp.einsum('jhp,jn->hpn', w_b.astype(jnp.float32) * tail.T[:, :, None], b_b.astype(jnp.float32), precision=highest)
        return (jnp.exp(cum_b[:, -1])[:, None, None] * state + update, (intra + inter, state))
    zero_state = jnp.zeros((NUMBER_OF_HEADS, HEAD_DIM, STATE_DIM), jnp.float32)
    final_state, (mixed, prior) = lax.scan(forward_step, zero_state, (cum, w_blocks, b_blocks, c_blocks))
    skip_rep = jnp.repeat(skip_gain, HEAD_DIM)[None, :]
    y_row = (scale * mixed.reshape(length, INNER_DIM) + skip_rep * inner.astype(jnp.float32)).astype(jnp.bfloat16)

    def backward_step(grad, item):
        cum_b, w_b, b_b, c_b, g_b, prior_b = item
        sim = jnp.dot(c_b, b_b.T, preferred_element_type=jnp.float32)
        decay_b = decay_matrix(cum_b)
        mixing = (decay_b * sim[None]).astype(jnp.bfloat16)
        g_f = g_b.astype(jnp.float32)
        w_f = w_b.astype(jnp.float32)
        tail = jnp.exp(cum_b[:, -1:] - cum_b)
        d_w = scale * jnp.einsum('hij,ihp->jhp', mixing.astype(jnp.float32), g_f)
        d_w = d_w + tail.T[:, :, None] * jnp.einsum('jn,hpn->jhp', b_b.astype(jnp.float32), grad, precision=highest)
        d_mix = scale * jnp.einsum('ihp,jhp->hij', g_f, w_f)
        d_sim = lax.optimization_barrier(jnp.sum(d_mix * decay_b, axis=0))
        lead = scale * g_f * jnp.exp(cum_b).T[:, :, None]
        d_c = jnp.dot(d_sim, b_b.astype(jnp.float32), precision=highest)
        d_c = d_c + jnp.einsum('ihp,hpn->in', lead, prior_b, precision=highest)
        d_b = jnp.dot(d_sim.T, c_b.astype(jnp.float32), precision=highest)
        d_b = d_b + jnp.einsum('jhp,hpn->jn', w_f * tail.T[:, :, None], grad, precision=highest)
        new_grad = jnp.exp(cum_b[:, -1])[:, None, None] * grad + jnp.einsum('ihp,in->hpn', lead, c_b.astype(jnp.float32), precision=highest)
        return (new_grad, (d_w, d_b, d_c))
    start_grad, (d_weighted, d_bmat, d_cmat) = lax.scan(backward_step, zero_state, (cum, w_blocks, b_blocks, c_blocks, g_blocks, prior), reverse=True)
    d_weighted = d_weighted.reshape(length, NUMBER_OF_HEADS, HEAD_DIM)
    d_inner = (input_gain.T[:, :, None] * d_weighted).reshape(length, INNER_DIM) + skip_rep * grad_row.astype(jnp.float32)
    d_pre_x = d_inner * silu_grad(pre_x)
    d_mapped = jnp.concatenate([d_bmat.reshape(length, STATE_DIM), d_cmat.reshape(length, STATE_DIM)], axis=1)
    d_pre_bc = d_mapped * silu_grad(pre_bc)
    grad_x = conv_backward(d_pre_x, conv_x).astype(jnp.bfloat16)
    grad_bc = conv_backward(d_pre_bc, conv_bc).astype(jnp.bfloat16)
    taps_x = conv_weight_grad(d_pre_x, x_pad, taps)
    taps_bc = conv_weight_grad(d_pre_bc, bc_pad, taps)
    skip_term = lax.optimization_barrier(jnp.sum((grad_row.astype(jnp.float32) * inner.astype(jnp.float32)).reshape(length, NUMBER_OF_HEADS, HEAD_DIM), axis=(0, 2)))
    return (y_row, grad_x, grad_bc, taps_x, taps_bc, skip_term)

def reference(x_input, bc_input, decays, conv_x, conv_bc, skip_gain, grad_out):
    outputs = [one_row(x_input[row], bc_input[row], decays[row], conv_x, conv_bc, skip_gain, grad_out[row]) for row in range(GROUP_SEQUENCES)]
    y_output = jnp.stack([item[0] for item in outputs])
    grad_x = jnp.stack([item[1] for item in outputs])
    grad_bc = jnp.stack([item[2] for item in outputs])
    norm_tokens = float(GROUP_SEQUENCES * SEQUENCE_LENGTH) ** (-0.5)
    norm_skip = float(GROUP_SEQUENCES * SEQUENCE_LENGTH * HEAD_DIM) ** (-0.5)
    grad_conv_x = sum((item[3] for item in outputs)) * norm_tokens
    grad_conv_bc = sum((item[4] for item in outputs)) * norm_tokens
    grad_skip = sum((item[5] for item in outputs)) * norm_skip
    return (y_output, grad_x, grad_bc, grad_conv_x, grad_conv_bc, grad_skip)
```

```python
import functools

import jax
import jax.numpy as jnp
from jax import lax
from jax.experimental import pallas as pl
from jax.experimental.pallas import tpu as pltpu
from jax.sharding import PartitionSpec as P

MESH = pl.DeviceIdType.MESH
f32 = jnp.float32
bf16 = jnp.bfloat16
LAG = 2


def dot(a, b, ca, cb):
    return lax.dot_general(a, b, (((ca,), (cb,)), ((), ())), preferred_element_type=f32)


def ones_where(mask):
    return mask.astype(f32).astype(bf16)


def iota(shape, axis):
    return lax.broadcasted_iota(jnp.int32, shape, axis)


def conv_taps(pad_ref, weight, first, tokens):
    total = weight[0:1, :] * pad_ref[pl.ds(first, tokens), :]
    for k in range(1, weight.shape[0]):
        total = total + weight[k : k + 1, :] * pad_ref[pl.ds(first + k, tokens), :]
    return total


def silu_parts(pre):
    sigma = 0.5 * jnp.tanh(0.5 * pre) + 0.5
    return pre * sigma, sigma * (1.0 + pre * (1.0 - sigma))


def main_kernel(
    head_dim, scale, sizes, lag,
    x_hbm, bc_hbm, d_hbm, cw_hbm, cbc_hbm, skip_hbm, g_hbm,
    y_ref, gx_ref, gbc_ref, sums_ref, bsum_ref,
    xv, gv, bcv, dv, cwv, cbcv, skip_ref,
    w_all, in_all, ds_all, lg_all, tw_all, ya, da, s_all, u_all, p_all, q_all, et, fac, cum_all,
    cum_r, cum_t, halo, halo_b, mapped, mapped_t, dsbc, bp, xp, dp, sim, dsim, dbc,
    tails, edges, next_x, parts, ride_in, core_in, tot, dbc_out, head_in, next_bc, dbp, bct, bct_in,
    load_x, load_g, load_small, halo_send, halo_recv, send_f, recv_f, send_b, recv_b,
    edge_send, edge_recv, ride_send, ride_recv, core_send, core_recv, tot_send, tot_recv,
    head_send, head_recv, nbc_send, nbc_recv, bct_send, bct_recv,
):
    groups, tokens, columns = xv.shape
    width = columns // head_dim
    count = groups * width
    n = mapped.shape[1] // 2
    taps = cwv.shape[0]
    first = 9 - taps
    seq, heads, cores = sizes
    peers = seq * heads * cores
    me = lax.axis_index("seq")
    back = seq - 1 - me
    hd = lax.axis_index("head")
    co = lax.axis_index("dp")
    rank = (me * heads + hd) * cores + co

    def copy(src, dst, send, recv, device):
        return pltpu.make_async_remote_copy(
            src_ref=src, dst_ref=dst, send_sem=send, recv_sem=recv, device_id=device,
            device_id_type=MESH,
        )

    def peer(o):
        at = lax.rem(rank + o, peers)
        high = at // cores
        return at, {"seq": high // heads, "head": lax.rem(high, heads), "dp": lax.rem(at, cores)}

    def lanes(c):
        return pl.ds(pl.multiple_of(c * columns, columns), columns)

    def x_load(c):
        return pltpu.make_async_copy(x_hbm.at[:, lanes(c)], xv.at[c], load_x.at[c])

    def g_load(c):
        return pltpu.make_async_copy(g_hbm.at[:, lanes(c)], gv.at[c], load_g.at[c])

    def halo_x():
        return copy(
            x_hbm.at[tokens - 16 : tokens], halo, halo_send.at[0], halo_recv.at[0], {"seq": me + 1}
        )

    def halo_bc():
        return copy(
            bc_hbm.at[tokens - 16 : tokens], halo_b, halo_send.at[1], halo_recv.at[1],
            {"seq": me + 1},
        )

    def forward(c):
        return copy(s_all.at[c], p_all.at[c], send_f.at[c], recv_f.at[c], {"seq": me + 1})

    def backward(c):
        return copy(u_all.at[c], q_all.at[c], send_b.at[c], recv_b.at[c], {"seq": me - 1})

    def edge_copy(c):
        return copy(edges.at[c], next_x.at[c], edge_send.at[c], edge_recv.at[c], {"seq": me - 1})

    def ride_copy(c):
        return copy(parts.at[c], ride_in.at[c], ride_send.at[c], ride_recv.at[c], {"seq": me - 1})

    def core_copy(c):
        return copy(
            parts.at[c], core_in.at[c], core_send.at[c], core_recv.at[c],
            {"dp": lax.rem(co + 1, cores)},
        )

    def tot_copy(c, z):
        return copy(tot.at[c], tot.at[c], tot_send.at[c, z], tot_recv.at[c], {"seq": z})

    def head_copy(half, o):
        return copy(
            dbc_out.at[half], head_in.at[half, hd], head_send.at[half, o],
            head_recv.at[half, hd], {"head": lax.rem(hd + o, heads)},
        )

    def nbc_copy(half, o):
        return copy(
            dbc_out.at[half, 0:16], next_bc.at[half, hd], nbc_send.at[half, o],
            nbc_recv.at[half, hd], {"head": lax.rem(hd + o, heads), "seq": me - 1},
        )

    def bct_copy(o):
        return copy(bct, bct_in.at[rank], bct_send.at[o], bct_recv.at[rank], peer(o)[1])

    def arrived(dst, sem, source):
        copy(source, dst, sem, sem, peer(1)[1]).wait_recv()

    small = [
        pltpu.make_async_copy(src, dst, load_small.at[i])
        for i, (src, dst) in enumerate(
            ((d_hbm, dv), (bc_hbm, bcv), (cbc_hbm, cbcv), (cw_hbm, cwv), (skip_hbm, skip_ref))
        )
    ]
    for load in small:
        load.start()

    @pl.loop(0, groups)
    def _(c):
        g_load(c).start()
        x_load(c).start()

    barrier = pltpu.get_barrier_semaphore()

    @pl.loop(1, peers)
    def _(o):
        pl.semaphore_signal(barrier, inc=1, device_id=peer(o)[1], device_id_type=MESH)

    pl.semaphore_wait(barrier, peers - 1)

    @pl.when(me < seq - 1)
    def _():
        halo_bc().start()
        halo_x().start()

    @pl.when(me == 0)
    def _():
        halo_b[...] = jnp.zeros(halo_b.shape, bf16)
        halo[...] = jnp.zeros(halo.shape, bf16)

    small[0].wait()
    d = dv[...]
    rest = jnp.log(d)
    upto = ones_where(iota((tokens, tokens), 0) <= iota((tokens, tokens), 1))
    rows = jnp.zeros(d.shape, f32)
    for _ in range(3):
        piece = rest.astype(bf16)
        rest = rest - piece.astype(f32)
        rows = rows + dot(piece, upto, 1, 0)
    cum_all[...] = rows
    last = rows[:, tokens - 1 :]
    factors = jnp.concatenate(
        [jnp.sqrt((1.0 - d) * (1.0 + d)), jnp.exp(rows), jnp.exp(last - rows)], axis=1
    )
    high = factors.astype(bf16).astype(f32)
    both = jnp.concatenate([high, factors - high], axis=0).astype(bf16)
    same = ones_where(iota((2 * count, 2 * count), 0) == iota((2 * count, 2 * count), 1))
    fac[...] = dot(both, same, 0, 0).astype(bf16)

    for load in small[1:]:
        load.wait()

    @pl.when(me > 0)
    def _():
        halo_bc().wait_recv()

    bp[0:8, :] = halo_b[...].astype(f32)[8:]
    bp[8:, :] = bcv[...].astype(f32)
    value, slope = silu_parts(conv_taps(bp, cbcv[...], first, tokens))
    mapped[...] = value.astype(bf16)
    dsbc[...] = slope
    unit = ones_where(iota((tokens, tokens), 0) == iota((tokens, tokens), 1))
    mapped_t[...] = dot(mapped[...], unit, 0, 0).astype(bf16)

    @pl.when(me > 0)
    def _():
        halo_x().wait_recv()

    def spread(c, start, stop):
        pick = iota((2 * count, columns), 0) % count == c * width + iota(
            (2 * count, columns), 1
        ) // head_dim
        return dot(fac[start * tokens : stop * tokens, :], ones_where(pick), 1, 0)

    def skip_row(c):
        lane = iota((1, columns), 1) // head_dim
        skip = jnp.zeros((1, columns), f32)
        for j in range(width):
            skip = jnp.where(lane == j, skip_ref[c * width + j], skip)
        return skip

    def phase_a(c):
        g_load(c).wait()
        factor = spread(c, 0, 3)
        et[c] = factor[2 * tokens - 1 : 2 * tokens]
        lead = (gv[c].astype(f32) * factor[tokens : 2 * tokens]).astype(bf16)
        lg_all[c] = lead
        u_all[c] = dot(mapped_t[n:, :], lead, 1, 0).astype(bf16)
        x_load(c).wait()
        xp[0:8, :] = halo[:, lanes(c)].astype(f32)[8:]
        xp[8:, :] = xv[c].astype(f32)
        value, slope = silu_parts(conv_taps(xp, cwv[:, lanes(c)], first, tokens))
        inner = value.astype(bf16)
        in_all[c] = inner
        ds_all[c] = slope.astype(bf16)
        w = (inner.astype(f32) * factor[:tokens]).astype(bf16)
        w_all[c] = w
        tail = (w.astype(f32) * factor[2 * tokens :]).astype(bf16)
        tw_all[c] = tail
        s_all[c] = dot(mapped_t[:n, :], tail, 1, 0).astype(bf16)

    def advance(c, hops, make, own, incoming):
        @pl.when(hops == 0)
        def _():
            incoming[c] = jnp.zeros(incoming.shape[1:], bf16)

        @pl.when(hops > 0)
        def _():
            make(c).wait_recv()

            @pl.when(hops < seq - 1)
            def _():
                own[c] = (incoming[c].astype(f32) * et[c] + own[c].astype(f32)).astype(bf16)

        @pl.when(hops < seq - 1)
        def _():
            make(c).start()

    def setup_b():
        turned = jnp.zeros((tokens, count), f32)
        rest = jnp.log(dv[...])
        upto = ones_where(iota((tokens, tokens), 0) <= iota((tokens, tokens), 1))
        for _ in range(3):
            piece = rest.astype(bf16)
            rest = rest - piece.astype(f32)
            turned = turned + dot(upto, piece, 0, 1)
        for c in range(groups):
            cum_t[c] = turned[:, c * width : (c + 1) * width]
            cum_r[c] = cum_all[c * width : (c + 1) * width, :]
        sim[...] = dot(mapped[:, n:], mapped[:, :n], 1, 1)
        dsim[...] = jnp.zeros_like(dsim)
        dbc[...] = jnp.zeros_like(dbc)

    def phase_b(c):
        lower = iota((tokens, tokens), 0) >= iota((tokens, tokens), 1)
        pair = 2 * head_dim
        side = iota((1, pair), 1) < head_dim
        for j in range(width // 2):
            cols = slice(j * pair, (j + 1) * pair)
            w_pair = w_all[c, :, cols]
            g_pair = gv[c, :, cols]
            found = []
            for e in range(2):
                h = 2 * j + e
                diff = cum_t[c, :, h : h + 1] - cum_r[c, h : h + 1, :]
                decay = jnp.exp(jnp.where(lower, diff, -1e30))
                mix = (decay * sim[...]).astype(bf16)
                mine = side if e == 0 else jnp.logical_not(side)
                g_own = jnp.where(mine, g_pair.astype(f32), 0.0).astype(bf16)
                dsim[...] += decay * dot(g_own, w_pair, 1, 1)
                found.append((dot(mix, w_pair, 1, 0), dot(mix, g_pair, 0, 0)))
            ya[c, :, cols] = jnp.where(side, found[0][0], found[1][0])
            da[c, :, cols] = jnp.where(side, found[0][1], found[1][1])

    def phase_p(c):
        p = p_all[c]
        lead = spread(c, 1, 2)
        y = scale * (ya[c] + lead * dot(mapped[:, n:], p, 1, 0))
        y_ref[:, lanes(c)] = (y + skip_row(c) * in_all[c].astype(f32)).astype(bf16)
        dbc[1] += dot(lg_all[c], p, 1, 1)

    def phase_q(c):
        q = q_all[c]
        g = gv[c].astype(f32)
        gain = spread(c, 0, 1)
        tail = spread(c, 2, 3)
        d_w = scale * (da[c] + tail * dot(mapped[:, :n], q, 1, 0))
        d_pre = (gain * d_w + skip_row(c) * g) * ds_all[c].astype(f32)
        dbc[0] += dot(tw_all[c], q, 1, 1)
        dp[0:tokens, :] = d_pre
        dp[tokens:, :] = jnp.zeros((8, columns), f32)
        edge = d_pre[0:8]
        for j in range(columns // 128):
            edges[c, j * (taps - 1) : (j + 1) * (taps - 1), :] = edge[
                0 : taps - 1, j * 128 : (j + 1) * 128
            ]

        @pl.when(me > 0)
        def _():
            edge_copy(c).start()

        x = xv[c].astype(f32)
        old = halo[:, lanes(c)].astype(f32)
        total = jnp.zeros((tokens, columns), f32)
        sums = []
        for k in range(taps):
            moved = dp[pl.ds(taps - 1 - k, tokens), :]
            total = total + cwv[k : k + 1, lanes(c)] * moved
            part = jnp.sum(x * moved, axis=0, keepdims=True)
            for t in range(taps - 1 - k):
                at = 16 - (taps - 1 - k) + t
                part = part + old[at : at + 1] * edge[t : t + 1]
            sums.append(part)
        gx_ref[:, lanes(c)] = total.astype(bf16)
        tails[c] = total[tokens - 16 :]
        sums.append(jnp.sum(g * in_all[c].astype(f32), axis=0, keepdims=True))
        sums.append(jnp.zeros((8 - taps - 1, columns), f32))
        parts[c] = jnp.concatenate(sums, axis=0)

        @pl.when(me < seq - 1)
        def _():
            ride_copy(c).wait_recv()
            parts[c] = parts[c] + ride_in[c]

        @pl.when(me > 0)
        def _():
            ride_copy(c).start()

        @pl.when(me == 0)
        def _():
            core_copy(c).start()

    def send_total(c):
        core_copy(c).wait_recv()
        tot[c] = parts[c] + core_in[c]
        for z in range(1, seq):
            tot_copy(c, z).start()

    def finish(half):
        other = mapped[:, n:] if half == 0 else mapped[:, :n]
        side = 0 if half == 0 else 1
        cols = slice(half * n, (half + 1) * n)
        whole = dbc[half] + dot(dsim[...].astype(bf16), other, side, 0)
        whole = scale * whole * dsbc[:, cols]
        dbc_out[half] = whole.astype(bf16)
        for o in range(1, heads):
            head_copy(half, o).start()

        @pl.when(me > 0)
        def _():
            for o in range(heads):
                nbc_copy(half, o).start()

        head_in[half, hd] = dbc_out[half]
        for k in range(taps):
            bct[half * taps + k : half * taps + k + 1, :] = jnp.sum(
                whole * bp[pl.ds(first + k, tokens), cols], axis=0, keepdims=True
            )

    @pl.loop(0, groups + lag * (seq - 1))
    def _(s):
        @pl.when(s < groups)
        def _():
            phase_a(s)

        cf = s - lag * me
        cb = s - lag * back

        @pl.when((cf >= 0) & (cf < groups))
        def _():
            advance(cf, me, forward, s_all, p_all)

        @pl.when((cb >= 0) & (cb < groups))
        def _():
            advance(cb, back, backward, u_all, q_all)

        @pl.when(s == 0)
        def _():
            setup_b()

        @pl.when(s < groups)
        def _():
            phase_b(s)

        @pl.when((me == 0) & (cb >= 1) & (cb < groups))
        def _():
            send_total(cb - 1)

        @pl.when((cb >= 0) & (cb < groups))
        def _():
            phase_q(cb)

            @pl.when(cb == groups - 1)
            def _():
                finish(0)

        @pl.when((cf >= 0) & (cf < groups))
        def _():
            phase_p(cf)

            @pl.when(cf == groups - 1)
            def _():
                finish(1)

    @pl.loop(1, peers)
    def _(o):
        bct_copy(o).start()

    @pl.when(me == 0)
    def _():
        send_total(groups - 1)

    bct_in[rank] = bct[...]

    @pl.when(me < seq - 1)
    def _():
        at = iota((16, 1), 0)
        for c in range(groups):
            edge_copy(c).wait_recv()
            fixed = tails[c]
            for r in range(taps - 1):
                cells = []
                for j in range(columns // 128):
                    lo = c * columns + j * 128
                    cell = jnp.zeros((1, 128), f32)
                    for k in range(r + 1):
                        e = j * (taps - 1) + r - k
                        cell = cell + cwv[k : k + 1, lo : lo + 128] * next_x[c, e : e + 1, :]
                    cells.append(cell)
                row = jnp.concatenate(cells, axis=1)
                fixed = fixed + jnp.where(at == 16 - (taps - 1) + r, row, 0.0)
            gx_ref[tokens - 16 :, c * columns : (c + 1) * columns] = fixed.astype(bf16)

    for half in range(2):
        for o in range(1, heads):
            at = lax.rem(hd + o, heads)
            arrived(head_in.at[half, at], head_recv.at[half, at], dbc_out.at[half])
        cols = slice(half * n, (half + 1) * n)
        full = head_in[half, 0].astype(f32)
        for h in range(1, heads):
            full = full + head_in[half, h].astype(f32)
        dbp[0:tokens, cols] = full

        @pl.when(me == seq - 1)
        def _():
            dbp[tokens:, cols] = jnp.zeros((8, n), f32)

        @pl.when(me < seq - 1)
        def _():
            for h in range(heads):
                arrived(next_bc.at[half, h], nbc_recv.at[half, h], dbc_out.at[half, 0:16])
            rows = next_bc[half, 0].astype(f32)
            for h in range(1, heads):
                rows = rows + next_bc[half, h].astype(f32)
            dbp[tokens:, cols] = rows[0:8]

    grad = jnp.zeros((tokens, 2 * n), f32)
    for k in range(taps):
        grad = grad + cbcv[k : k + 1, :] * dbp[pl.ds(taps - 1 - k, tokens), :]
    gbc_ref[...] = grad.astype(bf16)

    @pl.loop(1, peers)
    def _(o):
        at = lax.rem(rank + o, peers)
        arrived(bct_in.at[at], bct_recv.at[at], bct)

    bsum = bct_in[0]
    for i in range(1, peers):
        bsum = bsum + bct_in[i]
    bsum_ref[...] = bsum

    @pl.when(me > 0)
    def _():
        @pl.loop(0, groups)
        def _(c):
            arrived(tot.at[c], tot_recv.at[c], tot.at[c])

    sums_ref[...] = tot[...]

    for half in range(2):
        for o in range(1, heads):
            head_copy(half, o).wait_send()

    @pl.loop(1, peers)
    def _(o):
        bct_copy(o).wait_send()

    @pl.when(me < seq - 1)
    def _():
        halo_bc().wait_send()
        halo_x().wait_send()

        @pl.loop(0, groups)
        def _(c):
            forward(c).wait_send()

    @pl.when(me > 0)
    def _():
        for half in range(2):
            for o in range(heads):
                nbc_copy(half, o).wait_send()

        @pl.loop(0, groups)
        def _(c):
            backward(c).wait_send()
            edge_copy(c).wait_send()
            ride_copy(c).wait_send()

    @pl.when(me == 0)
    def _():
        @pl.loop(0, groups)
        def _(c):
            core_copy(c).wait_send()
            for z in range(1, seq):
                tot_copy(c, z).wait_send()


def final_kernel(
    head_dim, norm, pieces, y_in, gx_in, gbc_in, tot, bsum, y_out, gx_out, gbc_out, sums_out, bsum_out,
    skip_out, sem,
):
    tokens = y_in.shape[0]
    groups, _, columns = tot.shape
    taps = sums_out.shape[0]
    count = skip_out.shape[1]
    width = columns // head_dim
    block = tokens // pieces
    moves = []
    for i in range(pieces):
        at = pl.ds(i * block, block)
        moves.append(pltpu.make_async_copy(y_in.at[at], y_out.at[at], sem.at[0, i]))
        moves.append(pltpu.make_async_copy(gx_in.at[at], gx_out.at[at], sem.at[1, i]))
    moves.append(pltpu.make_async_copy(gbc_in, gbc_out, sem.at[2, 0]))
    for move in moves:
        move.start()
    rows = []
    for c in range(groups):
        sums_out[:, c * columns : (c + 1) * columns] = tot[c, 0:taps] * norm
        rows.append(tot[c, taps : taps + 1])
    rest = jnp.concatenate(rows, axis=0)
    pick = ones_where(
        iota((columns, count), 0) // head_dim == iota((columns, count), 1) % width
    )
    heads = jnp.zeros((groups, count), f32)
    for _ in range(3):
        piece = rest.astype(bf16)
        rest = rest - piece.astype(f32)
        heads = heads + dot(piece, pick, 1, 0)
    own = iota((groups, count), 1) // width == iota((groups, count), 0)
    skip_out[...] = jnp.sum(jnp.where(own, heads, 0.0), axis=0, keepdims=True) * (
        norm * float(head_dim) ** (-0.5)
    )
    half = bsum.shape[1]
    bsum_out[:, :half] = bsum[0:taps] * norm
    bsum_out[:, half:] = bsum[taps:] * norm
    for move in moves:
        move.wait()


def local(x_input, bc_input, decays, conv_x, conv_bc, skip_gain, grad_out):
    x = x_input[0]
    bc = bc_input[0]
    d = decays[0]
    g = grad_out[0]
    tokens, channels = x.shape
    taps = conv_x.shape[0]
    count = d.shape[0]
    head_dim = channels // count
    n = bc.shape[1] // 2
    scale = float(n) ** (-0.5)
    seq = lax.axis_size("seq")
    heads = lax.axis_size("head")
    cores = lax.axis_size("dp")
    peers = seq * heads * cores
    width = next(k for k in (4, 2) if count % k == 0)
    groups = count // width
    columns = width * head_dim
    norm = float(tokens * seq * cores) ** (-0.5)
    sizes = (seq, heads, cores)

    held = pltpu.with_memory_space_constraint

    def out(shape, dtype):
        return jax.ShapeDtypeStruct(shape, dtype)

    dma = pltpu.SemaphoreType.DMA
    vmem = pltpu.VMEM
    anywhere = pl.BlockSpec(memory_space=pl.ANY)
    inside = pl.BlockSpec(memory_space=vmem)
    wide = (groups, tokens, columns)
    state = (groups, n, columns)
    part = (groups, 8, columns)
    y, gx, gbc, sums, bsum = pl.pallas_call(
        functools.partial(main_kernel, head_dim, scale, sizes, LAG),
        in_specs=[anywhere] * 7,
        out_specs=[inside] * 5,
        out_shape=[
            vmem((tokens, channels), bf16), vmem((tokens, channels), bf16),
            vmem((tokens, 2 * n), bf16), vmem(part, f32), vmem((8, n), f32),
        ],
        scratch_shapes=[
            vmem(wide, bf16), vmem(wide, bf16), vmem((tokens, 2 * n), bf16),
            vmem((count, tokens), f32), vmem((taps, channels), f32), vmem((taps, 2 * n), f32), pltpu.SMEM((count,), f32),
            vmem(wide, bf16), vmem(wide, bf16), vmem(wide, bf16), vmem(wide, bf16),
            vmem(wide, bf16), vmem(wide, f32), vmem(wide, f32),
            vmem(state, bf16), vmem(state, bf16), vmem(state, bf16), vmem(state, bf16),
            vmem((groups, 1, columns), f32), vmem((3 * tokens, 2 * count), bf16),
            vmem((count, tokens), f32),
            vmem((groups, width, tokens), f32), vmem((groups, tokens, width), f32),
            vmem((16, channels), bf16), vmem((16, 2 * n), bf16),
            vmem((tokens, 2 * n), bf16), vmem((2 * n, tokens), bf16),
            vmem((tokens, 2 * n), f32), vmem((tokens + 8, 2 * n), f32),
            vmem((tokens + 8, columns), f32), vmem((tokens + 8, columns), f32),
            vmem((tokens, tokens), f32), vmem((tokens, tokens), f32),
            vmem((2, tokens, n), f32),
            vmem((groups, 16, columns), f32), vmem((groups, 8, 128), f32),
            vmem((groups, 8, 128), f32), vmem(part, f32), vmem(part, f32), vmem(part, f32),
            vmem(part, f32), vmem((2, tokens, n), bf16), vmem((2, heads, tokens, n), bf16),
            vmem((2, heads, 16, n), bf16), vmem((tokens + 8, 2 * n), f32),
            vmem((8, n), f32), vmem((peers, 8, n), f32),
            dma((groups,)), dma((groups,)), dma((5,)), dma((2,)), dma((2,)),
            dma((groups,)), dma((groups,)), dma((groups,)), dma((groups,)),
            dma((groups,)), dma((groups,)), dma((groups,)), dma((groups,)),
            dma((groups,)), dma((groups,)), dma((groups, seq)), dma((groups,)),
            dma((2, heads)), dma((2, heads)), dma((2, heads)), dma((2, heads)),
            dma((peers,)), dma((peers,)),
        ],
        compiler_params=pltpu.CompilerParams(
            vmem_limit_bytes=44 * 1024 * 1024, collective_id=0, has_side_effects=True,
        ),
        name="main",
    )(*(held(a, pltpu.HBM) for a in (x, bc, d, conv_x, conv_bc, skip_gain, g)))

    pieces = 8
    y, gx, gbc, taps_x, taps_bc, skips = pl.pallas_call(
        functools.partial(final_kernel, head_dim, norm, pieces),
        in_specs=[inside] * 5,
        out_specs=[anywhere] * 3 + [inside] * 3,
        out_shape=[
            out((tokens, channels), bf16), out((tokens, channels), bf16),
            out((tokens, 2 * n), bf16), out((taps, channels), f32), out((taps, 2 * n), f32),
            out((1, count), f32),
        ],
        scratch_shapes=[dma((3, pieces))],
        compiler_params=pltpu.CompilerParams(vmem_limit_bytes=16 * 1024 * 1024),
        name="final",
    )(y, gx, gbc, sums, bsum)
    return y[None], gx[None], gbc[None], taps_x, taps_bc, skips.reshape(count)


def solution(mesh):
    return jax.shard_map(
        local,
        mesh=mesh,
        in_specs=(
            P(("groups", "dp"), "seq", "head"),
            P(("groups", "dp"), "seq", None),
            P(("groups", "dp"), "head", "seq"),
            P(None, "head"),
            P(),
            P("head"),
            P(("groups", "dp"), "seq", "head"),
        ),
        out_specs=(
            P(("groups", "dp"), "seq", "head"),
            P(("groups", "dp"), "seq", "head"),
            P(("groups", "dp"), "seq", None),
            P("groups", "head"),
            P("groups", None),
            P(("groups", "head")),
        ),
        check_vma=False,
    )
```

```python
import functools

import jax
import jax.numpy as jnp
from jax import lax
from jax.experimental import pallas as pl
from jax.experimental.pallas import tpu as pltpu
from jax.sharding import PartitionSpec as P

MESH = pl.DeviceIdType.MESH
f32 = jnp.float32
bf16 = jnp.bfloat16
STRIP = 64


def dot(a, b, ca, cb):
    return lax.dot_general(a, b, (((ca,), (cb,)), ((), ())), preferred_element_type=f32)


def ones_where(mask):
    return mask.astype(f32).astype(bf16)


def iota(shape, axis):
    return lax.broadcasted_iota(jnp.int32, shape, axis)


def conv_taps(pad_ref, weight, first, tokens):
    total = weight[0:1, :] * pad_ref[pl.ds(first, tokens), :]
    for k in range(1, weight.shape[0]):
        total = total + weight[k : k + 1, :] * pad_ref[pl.ds(first + k, tokens), :]
    return total


def fold(a):
    return jnp.sum(a.reshape(a.shape[0] // 8, 8, a.shape[1]), axis=0)


def silu_parts(pre):
    sigma = 0.5 * jnp.tanh(0.5 * pre) + 0.5
    return pre * sigma, sigma * (1.0 + pre * (1.0 - sigma))


def main_kernel(
    head_dim, scale, sizes,
    x_hbm, bc_hbm, d_hbm, cw_hbm, cbc_hbm, skip_hbm, g_hbm,
    y_ref, gx_ref, gbc_ref, sums_ref, bsum_ref,
    xv, gv, bcv, dv, cwv, cbcv, skip_ref,
    in_all, ds_all, lead_all, gt_all, lg_all, tw_all, ya, da, s_all, u_all, p_all, q_all, et, fac, cum_all,
    cum_r, cum_t, halo, halo_b, mapped, mapped_t, dsbc, bp, xp, sim, dsim, dbc,
    tails, edges, next_x, parts, ride_in, core_in, tot, dbc_out, head_in, next_bc, dbp, bct, bct_in,
    load_x, load_g, load_small, halo_send, halo_recv, send_f, recv_f, send_b, recv_b,
    edge_send, edge_recv, ride_send, ride_recv, core_send, core_recv, tot_send, tot_recv,
    head_send, head_recv, nbc_send, nbc_recv, bct_send, bct_recv,
):
    groups, tokens, columns = xv.shape
    width = columns // head_dim
    count = groups * width
    n = mapped.shape[1] // 2
    taps = cwv.shape[0]
    first = 9 - taps
    seq, heads, cores = sizes
    peers = seq * heads * cores
    me = lax.axis_index("seq")
    back = seq - 1 - me
    hd = lax.axis_index("head")
    co = lax.axis_index("dp")
    rank = (me * heads + hd) * cores + co

    def copy(src, dst, send, recv, device):
        return pltpu.make_async_remote_copy(
            src_ref=src, dst_ref=dst, send_sem=send, recv_sem=recv, device_id=device,
            device_id_type=MESH,
        )

    def peer(o):
        at = lax.rem(rank + o, peers)
        high = at // cores
        return at, {"seq": high // heads, "head": lax.rem(high, heads), "dp": lax.rem(at, cores)}

    def lanes(c):
        return pl.ds(pl.multiple_of(c * columns, columns), columns)

    def x_load(c):
        return pltpu.make_async_copy(x_hbm.at[:, lanes(c)], xv.at[c], load_x.at[c])

    def g_load(c):
        return pltpu.make_async_copy(g_hbm.at[:, lanes(c)], gv.at[c], load_g.at[c])

    def halo_x():
        return copy(
            x_hbm.at[tokens - 16 : tokens], halo, halo_send.at[0], halo_recv.at[0], {"seq": me + 1}
        )

    def halo_bc():
        return copy(
            bc_hbm.at[tokens - 16 : tokens], halo_b, halo_send.at[1], halo_recv.at[1],
            {"seq": me + 1},
        )

    def forward(c):
        return copy(s_all.at[c], p_all.at[c], send_f.at[c], recv_f.at[c], {"seq": me + 1})

    def backward(c):
        return copy(u_all.at[c], q_all.at[c], send_b.at[c], recv_b.at[c], {"seq": me - 1})

    def edge_copy(c):
        two = pl.ds(2 * c, 2)
        return copy(edges.at[two], next_x.at[two], edge_send.at[c], edge_recv.at[c], {"seq": me - 1})

    def ride_copy(c):
        return copy(parts.at[c], ride_in.at[c], ride_send.at[c], ride_recv.at[c], {"seq": me - 1})

    def core_copy(c):
        return copy(
            parts.at[c], core_in.at[c], core_send.at[c], core_recv.at[c],
            {"dp": lax.rem(co + 1, cores)},
        )

    def tot_copy(c, z):
        return copy(tot.at[c], tot.at[c], tot_send.at[c, z], tot_recv.at[c], {"seq": z})

    def head_copy(half, o):
        return copy(
            dbc_out.at[half], head_in.at[half, hd], head_send.at[half, o],
            head_recv.at[half, hd], {"head": lax.rem(hd + o, heads)},
        )

    def nbc_copy(half, o):
        return copy(
            dbc_out.at[half, 0:16], next_bc.at[half, hd], nbc_send.at[half, o],
            nbc_recv.at[half, hd], {"head": lax.rem(hd + o, heads), "seq": me - 1},
        )

    def bct_copy(o):
        return copy(bct, bct_in.at[rank], bct_send.at[o], bct_recv.at[rank], peer(o)[1])

    def arrived(dst, sem, source):
        copy(source, dst, sem, sem, peer(1)[1]).wait_recv()

    small = [
        pltpu.make_async_copy(src, dst, load_small.at[i])
        for i, (src, dst) in enumerate(
            ((d_hbm, dv), (bc_hbm, bcv), (cbc_hbm, cbcv), (cw_hbm, cwv), (skip_hbm, skip_ref))
        )
    ]
    for load in small:
        load.start()

    @pl.loop(0, groups)
    def _(c):
        g_load(c).start()
        x_load(c).start()

    barrier = pltpu.get_barrier_semaphore()

    @pl.loop(1, peers)
    def _(o):
        pl.semaphore_signal(barrier, inc=1, device_id=peer(o)[1], device_id_type=MESH)

    pl.semaphore_wait(barrier, peers - 1)

    @pl.when(me < seq - 1)
    def _():
        halo_bc().start()
        halo_x().start()

    @pl.when(me == 0)
    def _():
        halo_b[...] = jnp.zeros(halo_b.shape, bf16)
        halo[...] = jnp.zeros(halo.shape, bf16)

    small[0].wait()
    d = dv[...]
    rest = jnp.log(d)
    upto = ones_where(iota((tokens, tokens), 0) <= iota((tokens, tokens), 1))
    rows = jnp.zeros(d.shape, f32)
    for _ in range(3):
        piece = rest.astype(bf16)
        rest = rest - piece.astype(f32)
        rows = rows + dot(piece, upto, 1, 0)
    squared = (1.0 - d) * (1.0 + d)
    cum_all[...] = rows - 0.5 * jnp.log(squared)
    last = rows[:, tokens - 1 :]
    factors = jnp.concatenate([jnp.exp(rows), jnp.sqrt(squared) * jnp.exp(last - rows)], axis=1)
    high = factors.astype(bf16).astype(f32)
    both = jnp.concatenate([high, factors - high], axis=0).astype(bf16)
    same = ones_where(iota((2 * count, 2 * count), 0) == iota((2 * count, 2 * count), 1))
    fac[...] = dot(both, same, 0, 0).astype(bf16)

    for load in small[1:]:
        load.wait()

    @pl.when(me > 0)
    def _():
        halo_bc().wait_recv()

    bp[0:8, :] = halo_b[...].astype(f32)[8:]
    bp[8:, :] = bcv[...].astype(f32)
    value, slope = silu_parts(conv_taps(bp, cbcv[...], first, tokens))
    mapped[...] = value.astype(bf16)
    dsbc[...] = slope
    unit = ones_where(iota((tokens, tokens), 0) == iota((tokens, tokens), 1))
    mapped_t[...] = dot(mapped[...], unit, 0, 0).astype(bf16)

    @pl.when(me > 0)
    def _():
        halo_x().wait_recv()

    def spread(c):
        pick = iota((2 * count, columns), 0) % count == c * width + iota(
            (2 * count, columns), 1
        ) // head_dim
        return dot(fac[...], ones_where(pick), 1, 0)

    def skip_row(c):
        lane = iota((1, columns), 1) // head_dim
        skip = jnp.zeros((1, columns), f32)
        for j in range(width):
            skip = jnp.where(lane == j, skip_ref[c * width + j], skip)
        return skip

    tiles = [slice(j * 128, (j + 1) * 128) for j in range(columns // 128)]
    strips = [slice(r, r + STRIP) for r in range(0, tokens, STRIP)]
    part = columns // 2

    def phase_a(c):
        factor = spread(c)
        g_load(c).wait()
        x_load(c).wait()
        lead_all[c] = factor[:tokens].astype(bf16)
        gt_all[c] = factor[tokens:].astype(bf16)
        old = halo[:, lanes(c)].astype(f32)[8:]
        weight = cwv[:, lanes(c)]
        for j, tile in enumerate(tiles):
            xp[j, 0:8] = old[:, tile]
            xp[j, 8:] = xv[c, :, tile].astype(f32)
        for e in range(2):
            et[2 * c + e] = factor[tokens - 1 : tokens, e * part : (e + 1) * part]
        for j, tile in enumerate(tiles):
            for rows in strips:
                lg_all[c, rows, tile] = gv[c, rows, tile] * lead_all[c, rows, tile]
                pre = weight[0:1, tile] * xp[j, pl.ds(first + rows.start, STRIP)]
                for k in range(1, taps):
                    pre = pre + weight[k : k + 1, tile] * xp[j, pl.ds(first + k + rows.start, STRIP)]
                value, slope = silu_parts(pre)
                inner = value.astype(bf16)
                in_all[c, rows, tile] = inner
                ds_all[c, rows, tile] = slope.astype(bf16)
                tw_all[c, rows, tile] = inner * gt_all[c, rows, tile]
        grown = dot(mapped_t[n:, :], lg_all[c], 1, 0).astype(bf16)
        state = dot(mapped_t[:n, :], tw_all[c], 1, 0).astype(bf16)
        for e in range(2):
            u_all[2 * c + e] = grown[:, e * part : (e + 1) * part]
            s_all[2 * c + e] = state[:, e * part : (e + 1) * part]

    def advance(c, hops, make, own, incoming):
        @pl.when(hops == 0)
        def _():
            incoming[c] = jnp.zeros(incoming.shape[1:], bf16)

        @pl.when(hops > 0)
        def _():
            make(c).wait_recv()

            @pl.when(hops < seq - 1)
            def _():
                own[c] = (incoming[c].astype(f32) * et[c] + own[c].astype(f32)).astype(bf16)

        @pl.when(hops < seq - 1)
        def _():
            make(c).start()

    def setup_b():
        turned = jnp.zeros((tokens, count), f32)
        rest = jnp.log(dv[...])
        upto = ones_where(iota((tokens, tokens), 0) <= iota((tokens, tokens), 1))
        for _ in range(3):
            piece = rest.astype(bf16)
            rest = rest - piece.astype(f32)
            turned = turned + dot(upto, piece, 0, 1)
        for c in range(groups):
            cum_t[c] = turned[:, c * width : (c + 1) * width]
            cum_r[c] = cum_all[c * width : (c + 1) * width, :]
        sim[...] = dot(mapped[:, n:], mapped[:, :n], 1, 1)
        dsim[...] = jnp.zeros_like(dsim)
        dbc[...] = jnp.zeros_like(dbc)

    def phase_b(c):
        mid = tokens // 2
        lower = iota((mid, mid), 0) >= iota((mid, mid), 1)
        empty = jnp.zeros((mid, mid), bf16)
        pair = 2 * head_dim
        side = iota((1, pair), 1) < head_dim
        g_t = gv[c].T
        corners = None
        turned = []
        for j in range(width // 2):
            cols = slice(j * pair, (j + 1) * pair)
            in_pair = in_all[c, :, cols]
            g_pair = gv[c, :, cols]
            found = []
            for e in range(2):
                h = 2 * j + e
                mine = side if e == 0 else jnp.logical_not(side)
                near = dot(jnp.where(mine, g_pair, jnp.zeros_like(g_pair)), in_pair, 1, 1)
                at = cum_t[c, :, h : h + 1]
                to = cum_r[c, h : h + 1, :]
                top = jnp.exp(jnp.where(lower, at[:mid] - to[:, :mid], -1e30))
                left = jnp.exp(at[mid:] - to[:, :mid])
                low = jnp.exp(jnp.where(lower, at[mid:] - to[:, mid:], -1e30))
                mix = jnp.concatenate(
                    [
                        jnp.concatenate([(top * sim[:mid, :mid]).astype(bf16), empty], axis=1),
                        jnp.concatenate(
                            [
                                (left * sim[mid:, :mid]).astype(bf16),
                                (low * sim[mid:, mid:]).astype(bf16),
                            ],
                            axis=1,
                        ),
                    ],
                    axis=0,
                )
                terms = [top * near[:mid, :mid], left * near[mid:, :mid], low * near[mid:, mid:]]
                corners = terms if corners is None else [a + b for a, b in zip(corners, terms)]
                found.append(dot(mix, in_pair, 1, 0))
                turned.append(dot(g_t[h * head_dim : (h + 1) * head_dim], mix, 1, 0))
            ya[c, :, cols] = jnp.where(side, found[0], found[1])
        dsim[:mid, :mid] += corners[0]
        dsim[mid:, :mid] += corners[1]
        dsim[mid:, mid:] += corners[2]
        da[c] = jnp.concatenate(turned, axis=0).T

    def phase_p(c):
        skip = skip_row(c)
        for e in range(2):
            p = p_all[2 * c + e]
            cols = slice(e * part, (e + 1) * part)
            seen = dot(mapped[:, n:], p, 1, 0)
            lead = lead_all[c, :, cols].astype(f32)
            y = scale * (ya[c, :, cols] + lead * seen)
            y = (y + skip[:, cols] * in_all[c, :, cols].astype(f32)).astype(bf16)
            y_ref[:, pl.ds(pl.multiple_of(c * columns + e * part, part), part)] = y
            dbc[1] += dot(lg_all[c, :, cols], p, 1, 1)

    def phase_q(c):
        skip = skip_row(c)
        weight = cwv[:, lanes(c)]
        old = halo[:, lanes(c)].astype(f32)
        for e in range(2):
            q = q_all[2 * c + e]
            cols = slice(e * part, (e + 1) * part)
            seen = dot(mapped[:, :n], q, 1, 0)
            dbc[0] += dot(tw_all[c, :, cols], q, 1, 1)
            for j in range(e * part // 128, (e + 1) * part // 128):
                tile = tiles[j]
                own = slice(j * 128 - e * part, (j + 1) * 128 - e * part)
                skipped = jnp.zeros((8, 128), f32)
                for rows in strips:
                    g = gv[c, rows, tile].astype(f32)
                    d_w = scale * (da[c, rows, tile] + gt_all[c, rows, tile].astype(f32) * seen[rows, own])
                    d_pre = (d_w + skip[:, tile] * g) * ds_all[c, rows, tile].astype(f32)
                    xp[j, rows] = d_pre
                    skipped = skipped + fold(g * in_all[c, rows, tile].astype(f32))
                xp[j, tokens:] = jnp.zeros((8, 128), f32)
                edge = xp[j, 0:8]
                base = (j % 2) * (taps - 1)
                edges[2 * c + j * 128 // part, base : base + taps - 1, :] = edge[0 : taps - 1]
                sums = [jnp.zeros((8, 128), f32) for _ in range(taps)]
                for rows in strips:
                    x = xv[c, rows, tile].astype(f32)
                    total = jnp.zeros((STRIP, 128), f32)
                    for k in range(taps):
                        moved = xp[j, pl.ds(taps - 1 - k + rows.start, STRIP)]
                        total = total + weight[k : k + 1, tile] * moved
                        sums[k] = sums[k] + fold(x * moved)
                    at = pl.ds(pl.multiple_of(c * columns + j * 128, 128), 128)
                    gx_ref[rows, at] = total.astype(bf16)
                    if rows.stop == tokens:
                        tails[c, :, tile] = total[STRIP - 16 :]
                for k in range(taps):
                    found = jnp.sum(sums[k], axis=0, keepdims=True)
                    for t in range(taps - 1 - k):
                        at = 16 - (taps - 1 - k) + t
                        found = found + old[at : at + 1, tile] * edge[t : t + 1]
                    parts[c, k : k + 1, tile] = found
                parts[c, taps : taps + 1, tile] = jnp.sum(skipped, axis=0, keepdims=True)
                parts[c, taps + 1 :, tile] = jnp.zeros((8 - taps - 1, 128), f32)

        @pl.when(me > 0)
        def _():
            edge_copy(c).start()

    def ride(c):
        @pl.when(me < seq - 1)
        def _():
            ride_copy(c).wait_recv()
            parts[c] = parts[c] + ride_in[c]

        @pl.when(me > 0)
        def _():
            ride_copy(c).start()

        @pl.when(me == 0)
        def _():
            core_copy(c).start()

    def send_total(c):
        core_copy(c).wait_recv()
        tot[c] = parts[c] + core_in[c]
        for z in range(1, seq):
            tot_copy(c, z).start()

    def finish(half):
        other = mapped[:, n:] if half == 0 else mapped[:, :n]
        side = 0 if half == 0 else 1
        cols = slice(half * n, (half + 1) * n)
        whole = dbc[half] + dot(dsim[...].astype(bf16), other, side, 0)
        whole = scale * whole * dsbc[:, cols]
        dbc_out[half] = whole.astype(bf16)
        for o in range(1, heads):
            head_copy(half, o).start()

        @pl.when(me > 0)
        def _():
            for o in range(heads):
                nbc_copy(half, o).start()

        head_in[half, hd] = dbc_out[half]
        for k in range(taps):
            bct[half * taps + k : half * taps + k + 1, :] = jnp.sum(
                whole * bp[pl.ds(first + k, tokens), cols], axis=0, keepdims=True
            )

    halves = 2 * groups
    shift = groups - 3

    def due(s, base, hops):
        gap = shift + 2 + 2 * hops
        c = lax.min(s - base, (s - gap + 4096) // 2 - 2048)
        return c, (c >= 0) & (c < groups) & (lax.max(base + c, 2 * c + gap) == s)

    @pl.loop(0, halves + 2 * (seq - 1) + shift + 1)
    def _(s):
        @pl.when(s < groups)
        def _():
            phase_a(s)
            for e in range(2):
                @pl.when(me == 0)
                def _():
                    advance(2 * s + e, me, forward, s_all, p_all)

                @pl.when(back == 0)
                def _():
                    advance(2 * s + e, back, backward, u_all, q_all)

        @pl.when(s == groups - 1)
        def _():
            setup_b()

        @pl.when((s >= groups) & (s < halves))
        def _():
            phase_b(s - groups)

        cq, has_q = due(s, halves, back)
        cr, has_r = due(s, halves + back, back)
        cp, has_p = due(s, halves, me)

        @pl.when(has_q)
        def _():
            phase_q(cq)

            @pl.when(cq == groups - 1)
            def _():
                finish(0)

        hf = s - shift - 2 * me
        hb = s - shift - 2 * back

        @pl.when((me > 0) & (hf >= 0) & (hf < halves))
        def _():
            advance(hf, me, forward, s_all, p_all)

        @pl.when((back > 0) & (hb >= 0) & (hb < halves))
        def _():
            advance(hb, back, backward, u_all, q_all)

        @pl.when(has_p)
        def _():
            phase_p(cp)

            @pl.when(cp == groups - 1)
            def _():
                finish(1)

        @pl.when(has_r)
        def _():
            ride(cr)

            @pl.when((me == 0) & (cr > 0))
            def _():
                send_total(cr - 1)

    @pl.loop(1, peers)
    def _(o):
        bct_copy(o).start()

    @pl.when(me == 0)
    def _():
        send_total(groups - 1)

    bct_in[rank] = bct[...]

    @pl.when(me < seq - 1)
    def _():
        at = iota((16, 1), 0)
        for c in range(groups):
            edge_copy(c).wait_recv()
            for j, tile in enumerate(tiles):
                fixed = tails[c, :, tile]
                lo = c * columns + j * 128
                for r in range(taps - 1):
                    row = jnp.zeros((1, 128), f32)
                    for k in range(r + 1):
                        e = (j % 2) * (taps - 1) + r - k
                        row = row + cwv[k : k + 1, lo : lo + 128] * next_x[
                            2 * c + j * 128 // part, e : e + 1, :
                        ]
                    fixed = fixed + jnp.where(at == 16 - (taps - 1) + r, row, 0.0)
                gx_ref[tokens - 16 :, lo : lo + 128] = fixed.astype(bf16)

    for half in range(2):
        for o in range(1, heads):
            at = lax.rem(hd + o, heads)
            arrived(head_in.at[half, at], head_recv.at[half, at], dbc_out.at[half])
        cols = slice(half * n, (half + 1) * n)
        full = head_in[half, 0].astype(f32)
        for h in range(1, heads):
            full = full + head_in[half, h].astype(f32)
        dbp[0:tokens, cols] = full

        @pl.when(me == seq - 1)
        def _():
            dbp[tokens:, cols] = jnp.zeros((8, n), f32)

        @pl.when(me < seq - 1)
        def _():
            for h in range(heads):
                arrived(next_bc.at[half, h], nbc_recv.at[half, h], dbc_out.at[half, 0:16])
            rows = next_bc[half, 0].astype(f32)
            for h in range(1, heads):
                rows = rows + next_bc[half, h].astype(f32)
            dbp[tokens:, cols] = rows[0:8]

    grad = jnp.zeros((tokens, 2 * n), f32)
    for k in range(taps):
        grad = grad + cbcv[k : k + 1, :] * dbp[pl.ds(taps - 1 - k, tokens), :]
    gbc_ref[...] = grad.astype(bf16)

    @pl.loop(1, peers)
    def _(o):
        at = lax.rem(rank + o, peers)
        arrived(bct_in.at[at], bct_recv.at[at], bct)

    bsum = bct_in[0]
    for i in range(1, peers):
        bsum = bsum + bct_in[i]
    bsum_ref[...] = bsum

    @pl.when(me > 0)
    def _():
        @pl.loop(0, groups)
        def _(c):
            arrived(tot.at[c], tot_recv.at[c], tot.at[c])

    sums_ref[...] = tot[...]

    for half in range(2):
        for o in range(1, heads):
            head_copy(half, o).wait_send()

    @pl.loop(1, peers)
    def _(o):
        bct_copy(o).wait_send()

    @pl.when(me < seq - 1)
    def _():
        halo_bc().wait_send()
        halo_x().wait_send()

        @pl.loop(0, halves)
        def _(h):
            forward(h).wait_send()

    @pl.when(me > 0)
    def _():
        for half in range(2):
            for o in range(heads):
                nbc_copy(half, o).wait_send()

        @pl.loop(0, halves)
        def _(h):
            backward(h).wait_send()

        @pl.loop(0, groups)
        def _(c):
            edge_copy(c).wait_send()
            ride_copy(c).wait_send()

    @pl.when(me == 0)
    def _():
        @pl.loop(0, groups)
        def _(c):
            core_copy(c).wait_send()
            for z in range(1, seq):
                tot_copy(c, z).wait_send()


def final_kernel(
    head_dim, norm, pieces, y_in, gx_in, gbc_in, tot, bsum, y_out, gx_out, gbc_out, sums_out, bsum_out,
    skip_out, sem,
):
    tokens = y_in.shape[0]
    groups, _, columns = tot.shape
    taps = sums_out.shape[0]
    count = skip_out.shape[1]
    width = columns // head_dim
    block = tokens // pieces
    moves = []
    for i in range(pieces):
        at = pl.ds(i * block, block)
        moves.append(pltpu.make_async_copy(y_in.at[at], y_out.at[at], sem.at[0, i]))
        moves.append(pltpu.make_async_copy(gx_in.at[at], gx_out.at[at], sem.at[1, i]))
    moves.append(pltpu.make_async_copy(gbc_in, gbc_out, sem.at[2, 0]))
    for move in moves:
        move.start()
    rows = []
    for c in range(groups):
        sums_out[:, c * columns : (c + 1) * columns] = tot[c, 0:taps] * norm
        rows.append(tot[c, taps : taps + 1])
    rest = jnp.concatenate(rows, axis=0)
    pick = ones_where(
        iota((columns, count), 0) // head_dim == iota((columns, count), 1) % width
    )
    heads = jnp.zeros((groups, count), f32)
    for _ in range(3):
        piece = rest.astype(bf16)
        rest = rest - piece.astype(f32)
        heads = heads + dot(piece, pick, 1, 0)
    own = iota((groups, count), 1) // width == iota((groups, count), 0)
    skip_out[...] = jnp.sum(jnp.where(own, heads, 0.0), axis=0, keepdims=True) * (
        norm * float(head_dim) ** (-0.5)
    )
    half = bsum.shape[1]
    bsum_out[:, :half] = bsum[0:taps] * norm
    bsum_out[:, half:] = bsum[taps:] * norm
    for move in moves:
        move.wait()


def local(x_input, bc_input, decays, conv_x, conv_bc, skip_gain, grad_out):
    x = x_input[0]
    bc = bc_input[0]
    d = decays[0]
    g = grad_out[0]
    tokens, channels = x.shape
    taps = conv_x.shape[0]
    count = d.shape[0]
    head_dim = channels // count
    n = bc.shape[1] // 2
    scale = float(n) ** (-0.5)
    seq = lax.axis_size("seq")
    heads = lax.axis_size("head")
    cores = lax.axis_size("dp")
    peers = seq * heads * cores
    width = next(k for k in (8, 4) if count % k == 0)
    groups = count // width
    columns = width * head_dim
    norm = float(tokens * seq * cores) ** (-0.5)
    sizes = (seq, heads, cores)

    held = pltpu.with_memory_space_constraint

    def out(shape, dtype):
        return jax.ShapeDtypeStruct(shape, dtype)

    dma = pltpu.SemaphoreType.DMA
    vmem = pltpu.VMEM
    anywhere = pl.BlockSpec(memory_space=pl.ANY)
    inside = pl.BlockSpec(memory_space=vmem)
    wide = (groups, tokens, columns)
    state = (2 * groups, n, columns // 2)
    part = (groups, 8, columns)
    y, gx, gbc, sums, bsum = pl.pallas_call(
        functools.partial(main_kernel, head_dim, scale, sizes),
        in_specs=[anywhere] * 7,
        out_specs=[inside] * 5,
        out_shape=[
            vmem((tokens, channels), bf16), vmem((tokens, channels), bf16),
            vmem((tokens, 2 * n), bf16), vmem(part, f32), vmem((8, n), f32),
        ],
        scratch_shapes=[
            vmem(wide, bf16), vmem(wide, bf16), vmem((tokens, 2 * n), bf16),
            vmem((count, tokens), f32), vmem((taps, channels), f32), vmem((taps, 2 * n), f32), pltpu.SMEM((count,), f32),
            vmem(wide, bf16), vmem(wide, bf16), vmem(wide, bf16), vmem(wide, bf16),
            vmem(wide, bf16), vmem(wide, bf16), vmem(wide, f32), vmem(wide, f32),
            vmem(state, bf16), vmem(state, bf16), vmem(state, bf16), vmem(state, bf16),
            vmem((2 * groups, 1, columns // 2), f32), vmem((2 * tokens, 2 * count), bf16),
            vmem((count, tokens), f32),
            vmem((groups, width, tokens), f32), vmem((groups, tokens, width), f32),
            vmem((16, channels), bf16), vmem((16, 2 * n), bf16),
            vmem((tokens, 2 * n), bf16), vmem((2 * n, tokens), bf16),
            vmem((tokens, 2 * n), f32), vmem((tokens + 8, 2 * n), f32),
            vmem((columns // 128, tokens + 8, 128), f32),
            vmem((tokens, tokens), f32), vmem((tokens, tokens), f32),
            vmem((2, tokens, n), f32),
            vmem((groups, 16, columns), f32), vmem((2 * groups, 8, 128), f32),
            vmem((2 * groups, 8, 128), f32), vmem(part, f32), vmem(part, f32), vmem(part, f32),
            vmem(part, f32), vmem((2, tokens, n), bf16), vmem((2, heads, tokens, n), bf16),
            vmem((2, heads, 16, n), bf16), vmem((tokens + 8, 2 * n), f32),
            vmem((8, n), f32), vmem((peers, 8, n), f32),
            dma((groups,)), dma((groups,)), dma((5,)), dma((2,)), dma((2,)),
            dma((2 * groups,)), dma((2 * groups,)), dma((2 * groups,)), dma((2 * groups,)),
            dma((groups,)), dma((groups,)), dma((groups,)), dma((groups,)),
            dma((groups,)), dma((groups,)), dma((groups, seq)), dma((groups,)),
            dma((2, heads)), dma((2, heads)), dma((2, heads)), dma((2, heads)),
            dma((peers,)), dma((peers,)),
        ],
        compiler_params=pltpu.CompilerParams(
            vmem_limit_bytes=44 * 1024 * 1024, collective_id=0, has_side_effects=True,
        ),
        name="main",
    )(*(held(a, pltpu.HBM) for a in (x, bc, d, conv_x, conv_bc, skip_gain, g)))

    pieces = 8
    y, gx, gbc, taps_x, taps_bc, skips = pl.pallas_call(
        functools.partial(final_kernel, head_dim, norm, pieces),
        in_specs=[inside] * 5,
        out_specs=[anywhere] * 3 + [inside] * 3,
        out_shape=[
            out((tokens, channels), bf16), out((tokens, channels), bf16),
            out((tokens, 2 * n), bf16), out((taps, channels), f32), out((taps, 2 * n), f32),
            out((1, count), f32),
        ],
        scratch_shapes=[dma((3, pieces))],
        compiler_params=pltpu.CompilerParams(vmem_limit_bytes=16 * 1024 * 1024),
        name="final",
    )(y, gx, gbc, sums, bsum)
    return y[None], gx[None], gbc[None], taps_x, taps_bc, skips.reshape(count)


def solution(mesh):
    return jax.shard_map(
        local,
        mesh=mesh,
        in_specs=(
            P(("groups", "dp"), "seq", "head"),
            P(("groups", "dp"), "seq", None),
            P(("groups", "dp"), "head", "seq"),
            P(None, "head"),
            P(),
            P("head"),
            P(("groups", "dp"), "seq", "head"),
        ),
        out_specs=(
            P(("groups", "dp"), "seq", "head"),
            P(("groups", "dp"), "seq", "head"),
            P(("groups", "dp"), "seq", None),
            P("groups", "head"),
            P("groups", None),
            P(("groups", "head")),
        ),
        check_vma=False,
    )
```

```python
import functools

import jax
import jax.numpy as jnp
from jax import lax
from jax.experimental import pallas as pl
from jax.experimental.pallas import tpu as pltpu
from jax.sharding import PartitionSpec as P

MESH = pl.DeviceIdType.MESH
f32 = jnp.float32
bf16 = jnp.bfloat16
STRIP = 64
LAG = 3
HOLD = 0


def dot(a, b, ca, cb):
    return lax.dot_general(a, b, (((ca,), (cb,)), ((), ())), preferred_element_type=f32)


def ones_where(mask):
    return mask.astype(f32).astype(bf16)


def iota(shape, axis):
    return lax.broadcasted_iota(jnp.int32, shape, axis)


def conv_taps(pad_ref, weight, first, tokens):
    total = weight[0:1, :] * pad_ref[pl.ds(first, tokens), :]
    for k in range(1, weight.shape[0]):
        total = total + weight[k : k + 1, :] * pad_ref[pl.ds(first + k, tokens), :]
    return total


def fold(a):
    return jnp.sum(a.reshape(a.shape[0] // 8, 8, a.shape[1]), axis=0)


def silu_parts(pre):
    sigma = 0.5 * jnp.tanh(0.5 * pre) + 0.5
    return pre * sigma, sigma * (1.0 + pre * (1.0 - sigma))


def main_kernel(
    head_dim, scale, sizes,
    x_hbm, bc_hbm, d_hbm, cw_hbm, cbc_hbm, skip_hbm, g_hbm,
    y_ref, gx_ref, gbc_ref, sums_ref, bsum_ref,
    xv, gv, bcv, dv, cwv, cbcv, skip_ref,
    in_all, ds_all, lead_all, gt_all, lg_all, tw_all, ya, da, s_all, u_all, p_all, q_all, et, fac, cum_all,
    cum_r, cum_t, halo, halo_b, mapped, mapped_t, dsbc, bp, xp, sim, dsim, dbc,
    tails, edges, next_x, parts, ride_in, core_in, tot, dbc_out, head_in, next_bc, dbp, bct, bct_in,
    load_x, load_g, load_small, halo_send, halo_recv, send_f, recv_f, send_b, recv_b,
    edge_send, edge_recv, ride_send, ride_recv, core_send, core_recv, tot_send, tot_recv,
    head_send, head_recv, nbc_send, nbc_recv, bct_send, bct_recv,
):
    groups, tokens, columns = xv.shape
    width = columns // head_dim
    count = groups * width
    n = mapped.shape[1] // 2
    taps = cwv.shape[0]
    first = 9 - taps
    seq, heads, cores = sizes
    peers = seq * heads * cores
    me = lax.axis_index("seq")
    back = seq - 1 - me
    hd = lax.axis_index("head")
    co = lax.axis_index("dp")
    rank = (me * heads + hd) * cores + co

    def copy(src, dst, send, recv, device):
        return pltpu.make_async_remote_copy(
            src_ref=src, dst_ref=dst, send_sem=send, recv_sem=recv, device_id=device,
            device_id_type=MESH,
        )

    def peer(o):
        at = lax.rem(rank + o, peers)
        high = at // cores
        return at, {"seq": high // heads, "head": lax.rem(high, heads), "dp": lax.rem(at, cores)}

    def lanes(c):
        return pl.ds(pl.multiple_of(c * columns, columns), columns)

    def x_load(c):
        return pltpu.make_async_copy(x_hbm.at[:, lanes(c)], xv.at[c], load_x.at[c])

    def g_load(c):
        return pltpu.make_async_copy(g_hbm.at[:, lanes(c)], gv.at[c], load_g.at[c])

    def halo_x(c):
        return copy(
            x_hbm.at[tokens - 16 : tokens, lanes(c)], halo.at[:, lanes(c)], halo_send.at[c],
            halo_recv.at[c], {"seq": me + 1},
        )

    def halo_bc():
        return copy(
            bc_hbm.at[tokens - 16 : tokens], halo_b, halo_send.at[groups], halo_recv.at[groups],
            {"seq": me + 1},
        )

    def forward(c):
        return copy(s_all.at[c], p_all.at[c], send_f.at[c], recv_f.at[c], {"seq": me + 1})

    def backward(c):
        return copy(u_all.at[c], q_all.at[c], send_b.at[c], recv_b.at[c], {"seq": me - 1})

    def edge_copy(c):
        two = pl.ds(2 * c, 2)
        return copy(edges.at[two], next_x.at[two], edge_send.at[c], edge_recv.at[c], {"seq": me - 1})

    def ride_copy(c):
        return copy(parts.at[c], ride_in.at[c], ride_send.at[c], ride_recv.at[c], {"seq": me - 1})

    def core_copy(c):
        return copy(
            parts.at[c], core_in.at[c], core_send.at[c], core_recv.at[c],
            {"dp": lax.rem(co + 1, cores)},
        )

    def tot_copy(c, z):
        return copy(tot.at[c], tot.at[c], tot_send.at[c, z], tot_recv.at[c], {"seq": z})

    def head_copy(half, o):
        return copy(
            dbc_out.at[half], head_in.at[half, hd], head_send.at[half, o],
            head_recv.at[half, hd], {"head": lax.rem(hd + o, heads)},
        )

    def nbc_copy(half, o):
        return copy(
            dbc_out.at[half, 0:16], next_bc.at[half, hd], nbc_send.at[half, o],
            nbc_recv.at[half, hd], {"head": lax.rem(hd + o, heads), "seq": me - 1},
        )

    def bct_copy(o):
        return copy(bct, bct_in.at[rank], bct_send.at[o], bct_recv.at[rank], peer(o)[1])

    def arrived(dst, sem, source):
        copy(source, dst, sem, sem, peer(1)[1]).wait_recv()

    small = [
        pltpu.make_async_copy(src, dst, load_small.at[i])
        for i, (src, dst) in enumerate(
            ((d_hbm, dv), (bc_hbm, bcv), (cbc_hbm, cbcv), (cw_hbm, cwv), (skip_hbm, skip_ref))
        )
    ]
    for load in small:
        load.start()

    @pl.loop(0, groups)
    def _(c):
        g_load(c).start()
        x_load(c).start()

    barrier = pltpu.get_barrier_semaphore()

    @pl.loop(1, peers)
    def _(o):
        pl.semaphore_signal(barrier, inc=1, device_id=peer(o)[1], device_id_type=MESH)

    pl.semaphore_wait(barrier, peers - 1)

    @pl.when(me < seq - 1)
    def _():
        halo_bc().start()
        for c in range(groups):
            halo_x(c).start()

    @pl.when(me == 0)
    def _():
        halo_b[...] = jnp.zeros(halo_b.shape, bf16)
        halo[...] = jnp.zeros(halo.shape, bf16)

    small[0].wait()
    d = dv[...]
    rest = jnp.log(d)
    upto = ones_where(iota((tokens, tokens), 0) <= iota((tokens, tokens), 1))
    rows = jnp.zeros(d.shape, f32)
    for _ in range(3):
        piece = rest.astype(bf16)
        rest = rest - piece.astype(f32)
        rows = rows + dot(piece, upto, 1, 0)
    squared = (1.0 - d) * (1.0 + d)
    cum_all[...] = rows - 0.5 * jnp.log(squared)
    last = rows[:, tokens - 1 :]
    factors = jnp.concatenate([jnp.exp(rows), jnp.sqrt(squared) * jnp.exp(last - rows)], axis=1)
    high = factors.astype(bf16).astype(f32)
    both = jnp.concatenate([high, factors - high], axis=0).astype(bf16)
    same = ones_where(iota((2 * count, 2 * count), 0) == iota((2 * count, 2 * count), 1))
    fac[...] = dot(both, same, 0, 0).astype(bf16)

    for load in small[1:]:
        load.wait()

    @pl.when(me > 0)
    def _():
        halo_bc().wait_recv()

    bp[0:8, :] = halo_b[...].astype(f32)[8:]
    bp[8:, :] = bcv[...].astype(f32)
    value, slope = silu_parts(conv_taps(bp, cbcv[...], first, tokens))
    mapped[...] = value.astype(bf16)
    dsbc[...] = slope
    unit = ones_where(iota((tokens, tokens), 0) == iota((tokens, tokens), 1))
    mapped_t[...] = dot(mapped[...], unit, 0, 0).astype(bf16)

    def spread(c):
        pick = iota((2 * count, columns), 0) % count == c * width + iota(
            (2 * count, columns), 1
        ) // head_dim
        return dot(fac[...], ones_where(pick), 1, 0)

    def skip_row(c):
        lane = iota((1, columns), 1) // head_dim
        skip = jnp.zeros((1, columns), f32)
        for j in range(width):
            skip = jnp.where(lane == j, skip_ref[c * width + j], skip)
        return skip

    tiles = [slice(j * 128, (j + 1) * 128) for j in range(columns // 128)]
    strips = [slice(r, r + STRIP) for r in range(0, tokens, STRIP)]
    part = columns // 2

    def phase_a(c):
        factor = spread(c)

        @pl.when(me > 0)
        def _():
            halo_x(c).wait_recv()

        g_load(c).wait()
        x_load(c).wait()
        lead_all[c] = factor[:tokens].astype(bf16)
        gt_all[c] = factor[tokens:].astype(bf16)
        old = halo[:, lanes(c)].astype(f32)[8:]
        weight = cwv[:, lanes(c)]
        for j, tile in enumerate(tiles):
            xp[j, 0:8] = old[:, tile]
            xp[j, 8:] = xv[c, :, tile].astype(f32)
        for e in range(2):
            et[2 * c + e] = factor[tokens - 1 : tokens, e * part : (e + 1) * part]
        for j, tile in enumerate(tiles):
            for rows in strips:
                lg_all[c, rows, tile] = gv[c, rows, tile] * lead_all[c, rows, tile]
                pre = weight[0:1, tile] * xp[j, pl.ds(first + rows.start, STRIP)]
                for k in range(1, taps):
                    pre = pre + weight[k : k + 1, tile] * xp[j, pl.ds(first + k + rows.start, STRIP)]
                value, slope = silu_parts(pre)
                inner = value.astype(bf16)
                in_all[c, rows, tile] = inner
                ds_all[c, rows, tile] = slope.astype(bf16)
                tw_all[c, rows, tile] = inner * gt_all[c, rows, tile]
        grown = dot(mapped_t[n:, :], lg_all[c], 1, 0).astype(bf16)
        state = dot(mapped_t[:n, :], tw_all[c], 1, 0).astype(bf16)
        for e in range(2):
            u_all[2 * c + e] = grown[:, e * part : (e + 1) * part]
            s_all[2 * c + e] = state[:, e * part : (e + 1) * part]

    def advance(c, hops, make, own, incoming):
        @pl.when(hops == 0)
        def _():
            incoming[c] = jnp.zeros(incoming.shape[1:], bf16)

        @pl.when(hops > 0)
        def _():
            make(c).wait_recv()

            @pl.when(hops < seq - 1)
            def _():
                own[c] = (incoming[c].astype(f32) * et[c] + own[c].astype(f32)).astype(bf16)

        @pl.when(hops < seq - 1)
        def _():
            make(c).start()

    def setup_b():
        turned = jnp.zeros((tokens, count), f32)
        rest = jnp.log(dv[...])
        upto = ones_where(iota((tokens, tokens), 0) <= iota((tokens, tokens), 1))
        for _ in range(3):
            piece = rest.astype(bf16)
            rest = rest - piece.astype(f32)
            turned = turned + dot(upto, piece, 0, 1)
        for c in range(groups):
            cum_t[c] = turned[:, c * width : (c + 1) * width]
            cum_r[c] = cum_all[c * width : (c + 1) * width, :]
        sim[...] = dot(mapped[:, n:], mapped[:, :n], 1, 1)
        dsim[...] = jnp.zeros_like(dsim)
        dbc[...] = jnp.zeros_like(dbc)

    def phase_b(c):
        mid = tokens // 2
        lower = iota((mid, mid), 0) >= iota((mid, mid), 1)
        empty = jnp.zeros((mid, mid), bf16)
        pair = 2 * head_dim
        side = iota((1, pair), 1) < head_dim
        g_t = gv[c].T
        corners = None
        turned = []
        for j in range(width // 2):
            cols = slice(j * pair, (j + 1) * pair)
            in_pair = in_all[c, :, cols]
            g_pair = gv[c, :, cols]
            found = []
            for e in range(2):
                h = 2 * j + e
                mine = side if e == 0 else jnp.logical_not(side)
                near = dot(jnp.where(mine, g_pair, jnp.zeros_like(g_pair)), in_pair, 1, 1)
                at = cum_t[c, :, h : h + 1]
                to = cum_r[c, h : h + 1, :]
                top = jnp.exp(jnp.where(lower, at[:mid] - to[:, :mid], -1e30))
                left = jnp.exp(at[mid:] - to[:, :mid])
                low = jnp.exp(jnp.where(lower, at[mid:] - to[:, mid:], -1e30))
                mix = jnp.concatenate(
                    [
                        jnp.concatenate([(top * sim[:mid, :mid]).astype(bf16), empty], axis=1),
                        jnp.concatenate(
                            [
                                (left * sim[mid:, :mid]).astype(bf16),
                                (low * sim[mid:, mid:]).astype(bf16),
                            ],
                            axis=1,
                        ),
                    ],
                    axis=0,
                )
                terms = [top * near[:mid, :mid], left * near[mid:, :mid], low * near[mid:, mid:]]
                corners = terms if corners is None else [a + b for a, b in zip(corners, terms)]
                found.append(dot(mix, in_pair, 1, 0))
                turned.append(dot(g_t[h * head_dim : (h + 1) * head_dim], mix, 1, 0))
            ya[c, :, cols] = jnp.where(side, found[0], found[1])
        dsim[:mid, :mid] += corners[0]
        dsim[mid:, :mid] += corners[1]
        dsim[mid:, mid:] += corners[2]
        da[c] = jnp.concatenate(turned, axis=0).T

    def phase_p(c):
        skip = skip_row(c)
        for e in range(2):
            p = p_all[2 * c + e]
            cols = slice(e * part, (e + 1) * part)
            seen = dot(mapped[:, n:], p, 1, 0)
            lead = lead_all[c, :, cols].astype(f32)
            y = scale * (ya[c, :, cols] + lead * seen)
            y = (y + skip[:, cols] * in_all[c, :, cols].astype(f32)).astype(bf16)
            y_ref[:, pl.ds(pl.multiple_of(c * columns + e * part, part), part)] = y
            dbc[1] += dot(lg_all[c, :, cols], p, 1, 1)

    def phase_q(c):
        skip = skip_row(c)
        weight = cwv[:, lanes(c)]
        old = halo[:, lanes(c)].astype(f32)
        for e in range(2):
            q = q_all[2 * c + e]
            cols = slice(e * part, (e + 1) * part)
            seen = dot(mapped[:, :n], q, 1, 0)
            dbc[0] += dot(tw_all[c, :, cols], q, 1, 1)
            for j in range(e * part // 128, (e + 1) * part // 128):
                tile = tiles[j]
                own = slice(j * 128 - e * part, (j + 1) * 128 - e * part)
                skipped = jnp.zeros((8, 128), f32)
                for rows in strips:
                    g = gv[c, rows, tile].astype(f32)
                    d_w = scale * (da[c, rows, tile] + gt_all[c, rows, tile].astype(f32) * seen[rows, own])
                    d_pre = (d_w + skip[:, tile] * g) * ds_all[c, rows, tile].astype(f32)
                    xp[j, rows] = d_pre
                    skipped = skipped + fold(g * in_all[c, rows, tile].astype(f32))
                xp[j, tokens:] = jnp.zeros((8, 128), f32)
                edge = xp[j, 0:8]
                base = (j % 2) * (taps - 1)
                edges[2 * c + j * 128 // part, base : base + taps - 1, :] = edge[0 : taps - 1]
                sums = [jnp.zeros((8, 128), f32) for _ in range(taps)]
                for rows in strips:
                    x = xv[c, rows, tile].astype(f32)
                    total = jnp.zeros((STRIP, 128), f32)
                    for k in range(taps):
                        moved = xp[j, pl.ds(taps - 1 - k + rows.start, STRIP)]
                        total = total + weight[k : k + 1, tile] * moved
                        sums[k] = sums[k] + fold(x * moved)
                    at = pl.ds(pl.multiple_of(c * columns + j * 128, 128), 128)
                    gx_ref[rows, at] = total.astype(bf16)
                    if rows.stop == tokens:
                        tails[c, :, tile] = total[STRIP - 16 :]
                for k in range(taps):
                    found = jnp.sum(sums[k], axis=0, keepdims=True)
                    for t in range(taps - 1 - k):
                        at = 16 - (taps - 1 - k) + t
                        found = found + old[at : at + 1, tile] * edge[t : t + 1]
                    parts[c, k : k + 1, tile] = found
                parts[c, taps : taps + 1, tile] = jnp.sum(skipped, axis=0, keepdims=True)
                parts[c, taps + 1 :, tile] = jnp.zeros((8 - taps - 1, 128), f32)

        @pl.when(me > 0)
        def _():
            edge_copy(c).start()

    def ride(c):
        @pl.when(me < seq - 1)
        def _():
            ride_copy(c).wait_recv()
            parts[c] = parts[c] + ride_in[c]

        @pl.when(me > 0)
        def _():
            ride_copy(c).start()

        @pl.when(me == 0)
        def _():
            core_copy(c).start()

    def send_total(c):
        core_copy(c).wait_recv()
        tot[c] = parts[c] + core_in[c]
        for z in range(1, seq):
            tot_copy(c, z).start()

    def finish(half):
        other = mapped[:, n:] if half == 0 else mapped[:, :n]
        side = 0 if half == 0 else 1
        cols = slice(half * n, (half + 1) * n)
        whole = dbc[half] + dot(dsim[...].astype(bf16), other, side, 0)
        whole = scale * whole * dsbc[:, cols]
        dbc_out[half] = whole.astype(bf16)
        for o in range(1, heads):
            head_copy(half, o).start()

        @pl.when(me > 0)
        def _():
            for o in range(heads):
                nbc_copy(half, o).start()

        head_in[half, hd] = dbc_out[half]
        for k in range(taps):
            bct[half * taps + k : half * taps + k + 1, :] = jnp.sum(
                whole * bp[pl.ds(first + k, tokens), cols], axis=0, keepdims=True
            )

    halves = 2 * groups
    hold = HOLD * co
    shift = groups - 1 - LAG + hold

    def due(s, base, hops):
        gap = lax.min(hops, 1) * (shift + 2 + LAG * hops)
        c = lax.min(s - base, (s - gap + 4096) // 2 - 2048)
        return c, (c >= 0) & (c < groups) & (lax.max(base + c, 2 * c + gap) == s)

    @pl.loop(0, halves + LAG * (seq - 2) + groups + HOLD * (cores - 1))
    def _(s):
        @pl.when(s < groups)
        def _():
            phase_a(s)

        ready = s - hold

        @pl.when((ready >= 0) & (ready < groups))
        def _():
            for e in range(2):
                @pl.when(me == 0)
                def _():
                    advance(2 * ready + e, me, forward, s_all, p_all)

                @pl.when(back == 0)
                def _():
                    advance(2 * ready + e, back, backward, u_all, q_all)

        @pl.when(s == groups - 1)
        def _():
            setup_b()

        @pl.when((s >= groups) & (s < halves))
        def _():
            phase_b(s - groups)

        cq, has_q = due(s, groups + groups * lax.min(back, 1), back)
        cr, has_r = due(s, groups + lax.min(back, 1) * (groups - 2 + 2 * back), back)
        cp, has_p = due(s, halves, me)

        @pl.when(has_q)
        def _():
            phase_q(cq)

        hf = s - shift - LAG * me
        hb = s - shift - LAG * back

        @pl.when((me > 0) & (hf >= 0) & (hf < halves))
        def _():
            advance(hf, me, forward, s_all, p_all)

        @pl.when((back > 0) & (hb >= 0) & (hb < halves))
        def _():
            advance(hb, back, backward, u_all, q_all)

        @pl.when(has_r)
        def _():
            ride(cr)

            @pl.when((me == 0) & (cr > 0))
            def _():
                send_total(cr - 1)

        @pl.when(has_q & (cq == groups - 1))
        def _():
            finish(0)

        @pl.when(has_p)
        def _():
            phase_p(cp)

            @pl.when(cp == groups - 1)
            def _():
                finish(1)

    @pl.when(me == 0)
    def _():
        send_total(groups - 1)

    @pl.loop(1, peers)
    def _(o):
        bct_copy(o).start()

    bct_in[rank] = bct[...]

    @pl.when(me < seq - 1)
    def _():
        at = iota((16, 1), 0)
        for c in range(groups):
            edge_copy(c).wait_recv()
            for j, tile in enumerate(tiles):
                fixed = tails[c, :, tile]
                lo = c * columns + j * 128
                for r in range(taps - 1):
                    row = jnp.zeros((1, 128), f32)
                    for k in range(r + 1):
                        e = (j % 2) * (taps - 1) + r - k
                        row = row + cwv[k : k + 1, lo : lo + 128] * next_x[
                            2 * c + j * 128 // part, e : e + 1, :
                        ]
                    fixed = fixed + jnp.where(at == 16 - (taps - 1) + r, row, 0.0)
                gx_ref[tokens - 16 :, lo : lo + 128] = fixed.astype(bf16)

    for half in range(2):
        for o in range(1, heads):
            at = lax.rem(hd + o, heads)
            arrived(head_in.at[half, at], head_recv.at[half, at], dbc_out.at[half])
        cols = slice(half * n, (half + 1) * n)
        full = head_in[half, 0].astype(f32)
        for h in range(1, heads):
            full = full + head_in[half, h].astype(f32)
        dbp[0:tokens, cols] = full

        @pl.when(me == seq - 1)
        def _():
            dbp[tokens:, cols] = jnp.zeros((8, n), f32)

        @pl.when(me < seq - 1)
        def _():
            for h in range(heads):
                arrived(next_bc.at[half, h], nbc_recv.at[half, h], dbc_out.at[half, 0:16])
            rows = next_bc[half, 0].astype(f32)
            for h in range(1, heads):
                rows = rows + next_bc[half, h].astype(f32)
            dbp[tokens:, cols] = rows[0:8]

    grad = jnp.zeros((tokens, 2 * n), f32)
    for k in range(taps):
        grad = grad + cbcv[k : k + 1, :] * dbp[pl.ds(taps - 1 - k, tokens), :]
    gbc_ref[...] = grad.astype(bf16)

    @pl.loop(1, peers)
    def _(o):
        at = lax.rem(rank + o, peers)
        arrived(bct_in.at[at], bct_recv.at[at], bct)

    bsum = bct_in[0]
    for i in range(1, peers):
        bsum = bsum + bct_in[i]
    bsum_ref[...] = bsum

    @pl.when(me > 0)
    def _():
        @pl.loop(0, groups)
        def _(c):
            arrived(tot.at[c], tot_recv.at[c], tot.at[c])

    sums_ref[...] = tot[...]

    for half in range(2):
        for o in range(1, heads):
            head_copy(half, o).wait_send()

    @pl.loop(1, peers)
    def _(o):
        bct_copy(o).wait_send()

    @pl.when(me < seq - 1)
    def _():
        halo_bc().wait_send()
        for c in range(groups):
            halo_x(c).wait_send()

        @pl.loop(0, halves)
        def _(h):
            forward(h).wait_send()

    @pl.when(me > 0)
    def _():
        for half in range(2):
            for o in range(heads):
                nbc_copy(half, o).wait_send()

        @pl.loop(0, halves)
        def _(h):
            backward(h).wait_send()

        @pl.loop(0, groups)
        def _(c):
            edge_copy(c).wait_send()
            ride_copy(c).wait_send()

    @pl.when(me == 0)
    def _():
        @pl.loop(0, groups)
        def _(c):
            core_copy(c).wait_send()
            for z in range(1, seq):
                tot_copy(c, z).wait_send()


def final_kernel(
    head_dim, norm, pieces, y_in, gx_in, gbc_in, tot, bsum, y_out, gx_out, gbc_out, sums_out, bsum_out,
    skip_out, sums, sums_bc, skips, sem,
):
    tokens = y_in.shape[0]
    groups, _, columns = tot.shape
    taps = sums.shape[0]
    count = skips.shape[1]
    width = columns // head_dim
    block = tokens // pieces
    moves = []
    for i in range(pieces):
        at = pl.ds(i * block, block)
        moves.append(pltpu.make_async_copy(y_in.at[at], y_out.at[at], sem.at[0, i]))
        moves.append(pltpu.make_async_copy(gx_in.at[at], gx_out.at[at], sem.at[1, i]))
    moves.append(pltpu.make_async_copy(gbc_in, gbc_out, sem.at[2, 0]))
    for move in moves:
        move.start()
    rows = []
    for c in range(groups):
        sums[:, c * columns : (c + 1) * columns] = tot[c, 0:taps] * norm
        rows.append(tot[c, taps : taps + 1])
    rest = jnp.concatenate(rows, axis=0)
    pick = ones_where(
        iota((columns, count), 0) // head_dim == iota((columns, count), 1) % width
    )
    heads = jnp.zeros((groups, count), f32)
    for _ in range(3):
        piece = rest.astype(bf16)
        rest = rest - piece.astype(f32)
        heads = heads + dot(piece, pick, 1, 0)
    own = iota((groups, count), 1) // width == iota((groups, count), 0)
    skips[...] = jnp.sum(jnp.where(own, heads, 0.0), axis=0, keepdims=True) * (
        norm * float(head_dim) ** (-0.5)
    )
    half = bsum.shape[1]
    sums_bc[:, :half] = bsum[0:taps] * norm
    sums_bc[:, half:] = bsum[taps:] * norm
    late = [
        pltpu.make_async_copy(src, dst, sem.at[2, i + 1])
        for i, (src, dst) in enumerate(((sums, sums_out), (sums_bc, bsum_out), (skips, skip_out)))
    ]
    for move in late:
        move.start()
    for move in moves + late:
        move.wait()


def local(x_input, bc_input, decays, conv_x, conv_bc, skip_gain, grad_out):
    x = x_input[0]
    bc = bc_input[0]
    d = decays[0]
    g = grad_out[0]
    tokens, channels = x.shape
    taps = conv_x.shape[0]
    count = d.shape[0]
    head_dim = channels // count
    n = bc.shape[1] // 2
    scale = float(n) ** (-0.5)
    seq = lax.axis_size("seq")
    heads = lax.axis_size("head")
    cores = lax.axis_size("dp")
    peers = seq * heads * cores
    width = next(k for k in (8, 4) if count % k == 0)
    groups = count // width
    columns = width * head_dim
    norm = float(tokens * seq * cores) ** (-0.5)
    sizes = (seq, heads, cores)

    held = pltpu.with_memory_space_constraint

    def out(shape, dtype):
        return jax.ShapeDtypeStruct(shape, dtype)

    dma = pltpu.SemaphoreType.DMA
    vmem = pltpu.VMEM
    anywhere = pl.BlockSpec(memory_space=pl.ANY)
    inside = pl.BlockSpec(memory_space=vmem)
    wide = (groups, tokens, columns)
    state = (2 * groups, n, columns // 2)
    part = (groups, 8, columns)
    y, gx, gbc, sums, bsum = pl.pallas_call(
        functools.partial(main_kernel, head_dim, scale, sizes),
        in_specs=[anywhere] * 7,
        out_specs=[inside] * 5,
        out_shape=[
            vmem((tokens, channels), bf16), vmem((tokens, channels), bf16),
            vmem((tokens, 2 * n), bf16), vmem(part, f32), vmem((8, n), f32),
        ],
        scratch_shapes=[
            vmem(wide, bf16), vmem(wide, bf16), vmem((tokens, 2 * n), bf16),
            vmem((count, tokens), f32), vmem((taps, channels), f32), vmem((taps, 2 * n), f32), pltpu.SMEM((count,), f32),
            vmem(wide, bf16), vmem(wide, bf16), vmem(wide, bf16), vmem(wide, bf16),
            vmem(wide, bf16), vmem(wide, bf16), vmem(wide, f32), vmem(wide, f32),
            vmem(state, bf16), vmem(state, bf16), vmem(state, bf16), vmem(state, bf16),
            vmem((2 * groups, 1, columns // 2), f32), vmem((2 * tokens, 2 * count), bf16),
            vmem((count, tokens), f32),
            vmem((groups, width, tokens), f32), vmem((groups, tokens, width), f32),
            vmem((16, channels), bf16), vmem((16, 2 * n), bf16),
            vmem((tokens, 2 * n), bf16), vmem((2 * n, tokens), bf16),
            vmem((tokens, 2 * n), f32), vmem((tokens + 8, 2 * n), f32),
            vmem((columns // 128, tokens + 8, 128), f32),
            vmem((tokens, tokens), f32), vmem((tokens, tokens), f32),
            vmem((2, tokens, n), f32),
            vmem((groups, 16, columns), f32), vmem((2 * groups, 8, 128), f32),
            vmem((2 * groups, 8, 128), f32), vmem(part, f32), vmem(part, f32), vmem(part, f32),
            vmem(part, f32), vmem((2, tokens, n), bf16), vmem((2, heads, tokens, n), bf16),
            vmem((2, heads, 16, n), bf16), vmem((tokens + 8, 2 * n), f32),
            vmem((8, n), f32), vmem((peers, 8, n), f32),
            dma((groups,)), dma((groups,)), dma((5,)), dma((groups + 1,)), dma((groups + 1,)),
            dma((2 * groups,)), dma((2 * groups,)), dma((2 * groups,)), dma((2 * groups,)),
            dma((groups,)), dma((groups,)), dma((groups,)), dma((groups,)),
            dma((groups,)), dma((groups,)), dma((groups, seq)), dma((groups,)),
            dma((2, heads)), dma((2, heads)), dma((2, heads)), dma((2, heads)),
            dma((peers,)), dma((peers,)),
        ],
        compiler_params=pltpu.CompilerParams(
            vmem_limit_bytes=44 * 1024 * 1024, collective_id=0, has_side_effects=True,
        ),
        name="main",
    )(*(held(a, pltpu.HBM) for a in (x, bc, d, conv_x, conv_bc, skip_gain, g)))

    pieces = 4
    y, gx, gbc, taps_x, taps_bc, skips = pl.pallas_call(
        functools.partial(final_kernel, head_dim, norm, pieces),
        in_specs=[inside] * 5,
        out_specs=[anywhere] * 6,
        out_shape=[
            out((tokens, channels), bf16), out((tokens, channels), bf16),
            out((tokens, 2 * n), bf16), out((taps, channels), f32), out((taps, 2 * n), f32),
            out((1, count), f32),
        ],
        scratch_shapes=[
            vmem((taps, channels), f32), vmem((taps, 2 * n), f32), vmem((1, count), f32),
            dma((3, 4)),
        ],
        compiler_params=pltpu.CompilerParams(vmem_limit_bytes=16 * 1024 * 1024),
        name="final",
    )(y, gx, gbc, sums, bsum)
    return y[None], gx[None], gbc[None], taps_x, taps_bc, skips.reshape(count)


def solution(mesh):
    return jax.shard_map(
        local,
        mesh=mesh,
        in_specs=(
            P(("groups", "dp"), "seq", "head"),
            P(("groups", "dp"), "seq", None),
            P(("groups", "dp"), "head", "seq"),
            P(None, "head"),
            P(),
            P("head"),
            P(("groups", "dp"), "seq", "head"),
        ),
        out_specs=(
            P(("groups", "dp"), "seq", "head"),
            P(("groups", "dp"), "seq", "head"),
            P(("groups", "dp"), "seq", None),
            P("groups", "head"),
            P("groups", None),
            P(("groups", "head")),
        ),
        check_vma=False,
    )
```

```python
import functools

import jax
import jax.numpy as jnp
from jax import lax
from jax.experimental import pallas as pl
from jax.experimental.pallas import tpu as pltpu
from jax.sharding import PartitionSpec as P

MESH = pl.DeviceIdType.MESH
f32 = jnp.float32
bf16 = jnp.bfloat16
STRIP = 64
LAG = 3
HOLD = 0
RIDE = 4


def dot(a, b, ca, cb):
    return lax.dot_general(a, b, (((ca,), (cb,)), ((), ())), preferred_element_type=f32)


def ones_where(mask):
    return mask.astype(f32).astype(bf16)


def iota(shape, axis):
    return lax.broadcasted_iota(jnp.int32, shape, axis)


def conv_taps(pad_ref, weight, first, tokens):
    total = weight[0:1, :] * pad_ref[pl.ds(first, tokens), :]
    for k in range(1, weight.shape[0]):
        total = total + weight[k : k + 1, :] * pad_ref[pl.ds(first + k, tokens), :]
    return total


def fold(a):
    return jnp.sum(a.reshape(a.shape[0] // 8, 8, a.shape[1]), axis=0)


def silu_parts(pre):
    sigma = 0.5 * jnp.tanh(0.5 * pre) + 0.5
    return pre * sigma, sigma * (1.0 + pre * (1.0 - sigma))


def main_kernel(
    head_dim, scale, sizes,
    x_hbm, bc_hbm, d_hbm, cw_hbm, cbc_hbm, skip_hbm, g_hbm,
    y_ref, gx_ref, gbc_ref, sums_ref, bsum_ref,
    xv, gv, bcv, dv, cwv, cbcv, skip_ref,
    in_all, ds_all, lead_all, gt_all, lg_all, tw_all, ya, da, s_all, u_all, p_all, q_all, et, fac, cum_all,
    cum_r, cum_t, halo, halo_b, mapped, mapped_t, dsbc, bp, xp, sim, dsim, dbc,
    skip_sums, tails, edges, next_x, parts, ride_in, core_in, tot, dbc_out, head_in, next_bc, dbp, bct, bct_in,
    load_x, load_g, load_small, halo_send, halo_recv, send_f, recv_f, send_b, recv_b,
    edge_send, edge_recv, ride_send, ride_recv, core_send, core_recv, tot_send, tot_recv,
    head_send, head_recv, nbc_send, nbc_recv, bct_send, bct_recv,
):
    groups, tokens, columns = xv.shape
    width = columns // head_dim
    count = groups * width
    n = mapped.shape[1] // 2
    taps = cwv.shape[0]
    first = 9 - taps
    seq, heads, cores = sizes
    peers = seq * heads * cores
    me = lax.axis_index("seq")
    back = seq - 1 - me
    hd = lax.axis_index("head")
    co = lax.axis_index("dp")
    rank = (me * heads + hd) * cores + co

    def copy(src, dst, send, recv, device):
        return pltpu.make_async_remote_copy(
            src_ref=src, dst_ref=dst, send_sem=send, recv_sem=recv, device_id=device,
            device_id_type=MESH,
        )

    def peer(o):
        at = lax.rem(rank + o, peers)
        high = at // cores
        return at, {"seq": high // heads, "head": lax.rem(high, heads), "dp": lax.rem(at, cores)}

    def lanes(c):
        return pl.ds(pl.multiple_of(c * columns, columns), columns)

    def x_load(c):
        return pltpu.make_async_copy(x_hbm.at[:, lanes(c)], xv.at[c], load_x.at[c])

    def g_load(c):
        return pltpu.make_async_copy(g_hbm.at[:, lanes(c)], gv.at[c], load_g.at[c])

    def halo_x(c):
        return copy(
            x_hbm.at[tokens - 16 : tokens, lanes(c)], halo.at[:, lanes(c)], halo_send.at[c],
            halo_recv.at[c], {"seq": me + 1},
        )

    def halo_bc():
        return copy(
            bc_hbm.at[tokens - 16 : tokens], halo_b, halo_send.at[groups], halo_recv.at[groups],
            {"seq": me + 1},
        )

    def forward(c):
        return copy(s_all.at[c], p_all.at[c], send_f.at[c], recv_f.at[c], {"seq": me + 1})

    def backward(c):
        return copy(u_all.at[c], q_all.at[c], send_b.at[c], recv_b.at[c], {"seq": me - 1})

    def edge_copy(c):
        return copy(edges.at[c], next_x.at[c], edge_send.at[c], edge_recv.at[c], {"seq": me - 1})

    def ride_copy(c):
        return copy(parts.at[c], ride_in.at[c], ride_send.at[c], ride_recv.at[c], {"seq": me - 1})

    def core_copy(c):
        return copy(
            parts.at[c], core_in.at[c], core_send.at[c], core_recv.at[c],
            {"dp": lax.rem(co + 1, cores)},
        )

    def tot_copies(c):
        return [
            copy(
                tot.at[c], tot.at[c], tot_send.at[c, z * cores + q], tot_recv.at[c],
                {"seq": z, "dp": lax.rem(co + q, cores)},
            )
            for z in range(seq)
            for q in range(cores)
            if z + q > 0
        ]

    def owner(c):
        return co == lax.rem(groups - c, cores)

    def head_copy(half, o):
        return copy(
            dbc_out.at[half], head_in.at[half, hd], head_send.at[half, o],
            head_recv.at[half, hd], {"head": lax.rem(hd + o, heads)},
        )

    def nbc_copy(half, o):
        return copy(
            dbc_out.at[half, 0:16], next_bc.at[half, hd], nbc_send.at[half, o],
            nbc_recv.at[half, hd], {"head": lax.rem(hd + o, heads), "seq": me - 1},
        )

    def bct_copy(o):
        return copy(bct, bct_in.at[rank], bct_send.at[o], bct_recv.at[rank], peer(o)[1])

    def arrived(dst, sem, source):
        copy(source, dst, sem, sem, peer(1)[1]).wait_recv()

    small = [
        pltpu.make_async_copy(src, dst, load_small.at[i])
        for i, (src, dst) in enumerate(
            ((d_hbm, dv), (bc_hbm, bcv), (cbc_hbm, cbcv), (cw_hbm, cwv), (skip_hbm, skip_ref))
        )
    ]
    for load in small:
        load.start()

    @pl.loop(0, groups)
    def _(c):
        g_load(c).start()
        x_load(c).start()

    barrier = pltpu.get_barrier_semaphore()

    @pl.loop(1, peers)
    def _(o):
        pl.semaphore_signal(barrier, inc=1, device_id=peer(o)[1], device_id_type=MESH)

    pl.semaphore_wait(barrier, peers - 1)

    @pl.when(me < seq - 1)
    def _():
        halo_bc().start()
        for c in range(groups):
            halo_x(c).start()

    @pl.when(me == 0)
    def _():
        halo_b[...] = jnp.zeros(halo_b.shape, bf16)
        halo[...] = jnp.zeros(halo.shape, bf16)

    small[0].wait()
    d = dv[...]
    rest = jnp.log(d)
    upto = ones_where(iota((tokens, tokens), 0) <= iota((tokens, tokens), 1))
    rows = jnp.zeros(d.shape, f32)
    for _ in range(3):
        piece = rest.astype(bf16)
        rest = rest - piece.astype(f32)
        rows = rows + dot(piece, upto, 1, 0)
    squared = (1.0 - d) * (1.0 + d)
    cum_all[...] = rows - 0.5 * jnp.log(squared)
    last = rows[:, tokens - 1 :]
    factors = jnp.concatenate([jnp.exp(rows), jnp.sqrt(squared) * jnp.exp(last - rows)], axis=1)
    high = factors.astype(bf16).astype(f32)
    both = jnp.concatenate([high, factors - high], axis=0).astype(bf16)
    same = ones_where(iota((2 * count, 2 * count), 0) == iota((2 * count, 2 * count), 1))
    fac[...] = dot(both, same, 0, 0).astype(bf16)

    for load in small[1:]:
        load.wait()

    @pl.when(me > 0)
    def _():
        halo_bc().wait_recv()

    bp[0:8, :] = halo_b[...].astype(f32)[8:]
    bp[8:, :] = bcv[...].astype(f32)
    value, slope = silu_parts(conv_taps(bp, cbcv[...], first, tokens))
    mapped[...] = value.astype(bf16)
    dsbc[...] = slope
    unit = ones_where(iota((tokens, tokens), 0) == iota((tokens, tokens), 1))
    mapped_t[...] = dot(mapped[...], unit, 0, 0).astype(bf16)

    def spread(c):
        pick = iota((2 * count, columns), 0) % count == c * width + iota(
            (2 * count, columns), 1
        ) // head_dim
        return dot(fac[...], ones_where(pick), 1, 0)

    def skip_row(c):
        lane = iota((1, columns), 1) // head_dim
        skip = jnp.zeros((1, columns), f32)
        for j in range(width):
            skip = jnp.where(lane == j, skip_ref[c * width + j], skip)
        return skip

    tiles = [slice(j * 128, (j + 1) * 128) for j in range(columns // 128)]
    strips = [slice(r, r + STRIP) for r in range(0, tokens, STRIP)]
    part = columns // 2

    def phase_a(c):
        factor = spread(c)

        @pl.when(me > 0)
        def _():
            halo_x(c).wait_recv()

        g_load(c).wait()
        x_load(c).wait()
        lead_all[c] = factor[:tokens].astype(bf16)
        gt_all[c] = factor[tokens:].astype(bf16)
        old = halo[:, lanes(c)].astype(f32)[8:]
        weight = cwv[:, lanes(c)]
        for j, tile in enumerate(tiles):
            xp[j, 0:8] = old[:, tile]
            xp[j, 8:] = xv[c, :, tile].astype(f32)
        for e in range(2):
            et[2 * c + e] = factor[tokens - 1 : tokens, e * part : (e + 1) * part]
        for j, tile in enumerate(tiles):
            skipped = jnp.zeros((8, 128), f32)
            for rows in strips:
                lg_all[c, rows, tile] = gv[c, rows, tile] * lead_all[c, rows, tile]
                pre = weight[0:1, tile] * xp[j, pl.ds(first + rows.start, STRIP)]
                for k in range(1, taps):
                    pre = pre + weight[k : k + 1, tile] * xp[j, pl.ds(first + k + rows.start, STRIP)]
                value, slope = silu_parts(pre)
                inner = value.astype(bf16)
                in_all[c, rows, tile] = inner
                ds_all[c, rows, tile] = slope.astype(bf16)
                tw_all[c, rows, tile] = inner * gt_all[c, rows, tile]
                skipped = skipped + fold(gv[c, rows, tile].astype(f32) * inner.astype(f32))
            skip_sums[c, j] = skipped
        grown = dot(mapped_t[n:, :], lg_all[c], 1, 0).astype(bf16)
        state = dot(mapped_t[:n, :], tw_all[c], 1, 0).astype(bf16)
        for e in range(2):
            u_all[2 * c + e] = grown[:, e * part : (e + 1) * part]
            s_all[2 * c + e] = state[:, e * part : (e + 1) * part]

    def advance(c, hops, make, own, incoming):
        @pl.when(hops == 0)
        def _():
            incoming[c] = jnp.zeros(incoming.shape[1:], bf16)

        @pl.when(hops > 0)
        def _():
            make(c).wait_recv()

            @pl.when(hops < seq - 1)
            def _():
                own[c] = (incoming[c].astype(f32) * et[c] + own[c].astype(f32)).astype(bf16)

        @pl.when(hops < seq - 1)
        def _():
            make(c).start()

    def setup_b():
        turned = jnp.zeros((tokens, count), f32)
        rest = jnp.log(dv[...])
        upto = ones_where(iota((tokens, tokens), 0) <= iota((tokens, tokens), 1))
        for _ in range(3):
            piece = rest.astype(bf16)
            rest = rest - piece.astype(f32)
            turned = turned + dot(upto, piece, 0, 1)
        for c in range(groups):
            cum_t[c] = turned[:, c * width : (c + 1) * width]
            cum_r[c] = cum_all[c * width : (c + 1) * width, :]
        sim[...] = dot(mapped[:, n:], mapped[:, :n], 1, 1)
        dsim[...] = jnp.zeros_like(dsim)
        dbc[...] = jnp.zeros_like(dbc)
        count_tiles = groups * len(tiles)
        rest = jnp.sum(skip_sums[...].reshape(count_tiles, 8, 128), axis=1)
        pick = ones_where(iota((8, 128), 1) // head_dim == iota((8, 128), 0))
        found = jnp.zeros((8, count_tiles), f32)
        for _ in range(3):
            piece = rest.astype(bf16)
            rest = rest - piece.astype(f32)
            found = found + dot(pick, piece, 1, 1)
        parts[groups] = jnp.zeros(parts.shape[1:], f32)
        parts[groups, :, 0:count_tiles] = found
        share(groups)

    def phase_b(c):
        mid = tokens // 2
        lower = iota((mid, mid), 0) >= iota((mid, mid), 1)
        empty = jnp.zeros((mid, mid), bf16)
        pair = 2 * head_dim
        side = iota((1, pair), 1) < head_dim
        g_t = gv[c].T
        corners = None
        turned = []
        for j in range(width // 2):
            cols = slice(j * pair, (j + 1) * pair)
            in_pair = in_all[c, :, cols]
            g_pair = gv[c, :, cols]
            found = []
            for e in range(2):
                h = 2 * j + e
                mine = side if e == 0 else jnp.logical_not(side)
                near = dot(jnp.where(mine, g_pair, jnp.zeros_like(g_pair)), in_pair, 1, 1)
                at = cum_t[c, :, h : h + 1]
                to = cum_r[c, h : h + 1, :]
                top = jnp.exp(jnp.where(lower, at[:mid] - to[:, :mid], -1e30))
                left = jnp.exp(at[mid:] - to[:, :mid])
                low = jnp.exp(jnp.where(lower, at[mid:] - to[:, mid:], -1e30))
                mix = jnp.concatenate(
                    [
                        jnp.concatenate([(top * sim[:mid, :mid]).astype(bf16), empty], axis=1),
                        jnp.concatenate(
                            [
                                (left * sim[mid:, :mid]).astype(bf16),
                                (low * sim[mid:, mid:]).astype(bf16),
                            ],
                            axis=1,
                        ),
                    ],
                    axis=0,
                )
                terms = [top * near[:mid, :mid], left * near[mid:, :mid], low * near[mid:, mid:]]
                corners = terms if corners is None else [a + b for a, b in zip(corners, terms)]
                found.append(dot(mix, in_pair, 1, 0))
                turned.append(dot(g_t[h * head_dim : (h + 1) * head_dim], mix, 1, 0))
            ya[c, :, cols] = jnp.where(side, found[0], found[1])
        dsim[:mid, :mid] += corners[0]
        dsim[mid:, :mid] += corners[1]
        dsim[mid:, mid:] += corners[2]
        da[c] = jnp.concatenate(turned, axis=0).T

    def phase_p(c):
        skip = skip_row(c)
        for e in range(2):
            p = p_all[2 * c + e]
            cols = slice(e * part, (e + 1) * part)
            seen = dot(mapped[:, n:], p, 1, 0)
            lead = lead_all[c, :, cols].astype(f32)
            y = scale * (ya[c, :, cols] + lead * seen)
            y = (y + skip[:, cols] * in_all[c, :, cols].astype(f32)).astype(bf16)
            y_ref[:, pl.ds(pl.multiple_of(c * columns + e * part, part), part)] = y
            dbc[1] += dot(lg_all[c, :, cols], p, 1, 1)

    def phase_q(c):
        skip = skip_row(c)
        weight = cwv[:, lanes(c)]
        old = halo[:, lanes(c)].astype(f32)
        heads_of = []
        for e in range(2):
            q = q_all[2 * c + e]
            cols = slice(e * part, (e + 1) * part)
            seen = dot(mapped[:, :n], q, 1, 0)
            dbc[0] += dot(tw_all[c, :, cols], q, 1, 1)
            for j in range(e * part // 128, (e + 1) * part // 128):
                tile = tiles[j]
                own = slice(j * 128 - e * part, (j + 1) * 128 - e * part)
                for rows in strips:
                    g = gv[c, rows, tile].astype(f32)
                    d_w = scale * (da[c, rows, tile] + gt_all[c, rows, tile].astype(f32) * seen[rows, own])
                    d_pre = (d_w + skip[:, tile] * g) * ds_all[c, rows, tile].astype(f32)
                    xp[j, rows] = d_pre
                xp[j, tokens:] = jnp.zeros((8, 128), f32)
                edge = xp[j, 0:8]
                heads_of.append(edge[0 : taps - 1])
                sums = [jnp.zeros((8, 128), f32) for _ in range(taps)]
                for rows in strips:
                    x = xv[c, rows, tile].astype(f32)
                    total = jnp.zeros((STRIP, 128), f32)
                    for k in range(taps):
                        moved = xp[j, pl.ds(taps - 1 - k + rows.start, STRIP)]
                        total = total + weight[k : k + 1, tile] * moved
                        sums[k] = sums[k] + fold(x * moved)
                    at = pl.ds(pl.multiple_of(c * columns + j * 128, 128), 128)
                    gx_ref[rows, at] = total.astype(bf16)
                    if rows.stop == tokens:
                        tails[c, :, tile] = total[STRIP - 16 :]
                for k in range(taps):
                    found = jnp.sum(sums[k], axis=0, keepdims=True)
                    for t in range(taps - 1 - k):
                        at = 16 - (taps - 1 - k) + t
                        found = found + old[at : at + 1, tile] * edge[t : t + 1]
                    row = (j % 2) * taps + k
                    parts[c, row : row + 1, j // 2 * 128 : (j // 2 + 1) * 128] = found

        heads_of.append(jnp.zeros((16 - len(tiles) * (taps - 1), 128), f32))
        edges[c] = jnp.concatenate(heads_of, axis=0).astype(bf16)

        @pl.when(me > 0)
        def _():
            edge_copy(c).start()

        share(c)

    def share(c):
        @pl.when(jnp.logical_not(owner(c)))
        def _():
            core_copy(c).start()

    def ride(c):
        @pl.when(owner(c))
        def _():
            arrived(core_in.at[c], core_recv.at[c], parts.at[c])
            parts[c] = parts[c] + core_in[c]

            @pl.when(me < seq - 1)
            def _():
                ride_copy(c).wait_recv()
                parts[c] = parts[c] + ride_in[c]

            @pl.when(me > 0)
            def _():
                ride_copy(c).start()

            @pl.when(me == 0)
            def _():
                tot[c] = parts[c]
                for move in tot_copies(c):
                    move.start()

    def finish(half):
        other = mapped[:, n:] if half == 0 else mapped[:, :n]
        side = 0 if half == 0 else 1
        cols = slice(half * n, (half + 1) * n)
        whole = dbc[half] + dot(dsim[...].astype(bf16), other, side, 0)
        whole = scale * whole * dsbc[:, cols]
        dbc_out[half] = whole.astype(bf16)
        for o in range(1, heads):
            head_copy(half, o).start()

        @pl.when(me > 0)
        def _():
            for o in range(heads):
                nbc_copy(half, o).start()

        head_in[half, hd] = dbc_out[half]
        for k in range(taps):
            bct[half * taps + k : half * taps + k + 1, :] = jnp.sum(
                whole * bp[pl.ds(first + k, tokens), cols], axis=0, keepdims=True
            )

    halves = 2 * groups
    hold = HOLD * co
    shift = groups - 1 - LAG + hold

    def due(s, base, hops):
        gap = lax.min(hops, 1) * (shift + 2 + LAG * hops)
        c = lax.min(s - base, (s - gap + 4096) // 2 - 2048)
        return c, (c >= 0) & (c < groups) & (lax.max(base + c, 2 * c + gap) == s)

    slots = halves + groups + max(LAG * (seq - 2), RIDE * (seq - 1) - 2)

    @pl.loop(0, slots + HOLD * (cores - 1))
    def _(s):
        @pl.when(s < groups)
        def _():
            phase_a(s)

        ready = s - hold

        @pl.when((ready >= 0) & (ready < groups))
        def _():
            for e in range(2):
                @pl.when(me == 0)
                def _():
                    advance(2 * ready + e, me, forward, s_all, p_all)

                @pl.when(back == 0)
                def _():
                    advance(2 * ready + e, back, backward, u_all, q_all)

        @pl.when(s == groups - 1)
        def _():
            setup_b()

        @pl.when((s >= groups) & (s < halves))
        def _():
            phase_b(s - groups)

        cq, has_q = due(s, groups + groups * lax.min(back, 1), back)
        cr, has_r = due(s, groups + 1 + lax.min(back, 1) * (groups - 3 + RIDE * back), back)
        cp, has_p = due(s, halves, me)

        @pl.when(has_q)
        def _():
            phase_q(cq)

        hf = s - shift - LAG * me
        hb = s - shift - LAG * back

        @pl.when((me > 0) & (hf >= 0) & (hf < halves))
        def _():
            advance(hf, me, forward, s_all, p_all)

        @pl.when((back > 0) & (hb >= 0) & (hb < halves))
        def _():
            advance(hb, back, backward, u_all, q_all)

        @pl.when(has_q & (cq == groups - 1))
        def _():
            finish(0)

        @pl.when(has_p)
        def _():
            phase_p(cp)

            @pl.when(cp == groups - 1)
            def _():
                finish(1)

        @pl.when(s == groups + 1 + RIDE * back)
        def _():
            ride(groups)

        @pl.when(has_r)
        def _():
            ride(cr)

    @pl.loop(1, peers)
    def _(o):
        bct_copy(o).start()

    bct_in[rank] = bct[...]

    @pl.when(me < seq - 1)
    def _():
        at = iota((16, 1), 0)
        for c in range(groups):
            edge_copy(c).wait_recv()
            after = next_x[c].astype(f32)
            for j, tile in enumerate(tiles):
                fixed = tails[c, :, tile]
                lo = c * columns + j * 128
                for r in range(taps - 1):
                    row = jnp.zeros((1, 128), f32)
                    for k in range(r + 1):
                        e = j * (taps - 1) + r - k
                        row = row + cwv[k : k + 1, lo : lo + 128] * after[e : e + 1]
                    fixed = fixed + jnp.where(at == 16 - (taps - 1) + r, row, 0.0)
                gx_ref[tokens - 16 :, lo : lo + 128] = fixed.astype(bf16)

    for half in range(2):
        for o in range(1, heads):
            at = lax.rem(hd + o, heads)
            arrived(head_in.at[half, at], head_recv.at[half, at], dbc_out.at[half])
        cols = slice(half * n, (half + 1) * n)
        full = head_in[half, 0].astype(f32)
        for h in range(1, heads):
            full = full + head_in[half, h].astype(f32)
        dbp[0:tokens, cols] = full

        @pl.when(me == seq - 1)
        def _():
            dbp[tokens:, cols] = jnp.zeros((8, n), f32)

        @pl.when(me < seq - 1)
        def _():
            for h in range(heads):
                arrived(next_bc.at[half, h], nbc_recv.at[half, h], dbc_out.at[half, 0:16])
            rows = next_bc[half, 0].astype(f32)
            for h in range(1, heads):
                rows = rows + next_bc[half, h].astype(f32)
            dbp[tokens:, cols] = rows[0:8]

    grad = jnp.zeros((tokens, 2 * n), f32)
    for k in range(taps):
        grad = grad + cbcv[k : k + 1, :] * dbp[pl.ds(taps - 1 - k, tokens), :]
    gbc_ref[...] = grad.astype(bf16)

    @pl.loop(1, peers)
    def _(o):
        at = lax.rem(rank + o, peers)
        arrived(bct_in.at[at], bct_recv.at[at], bct)

    bsum = bct_in[0]
    for i in range(1, peers):
        bsum = bsum + bct_in[i]
    bsum_ref[...] = bsum

    @pl.loop(0, groups + 1)
    def _(c):
        @pl.when(jnp.logical_not(owner(c) & (me == 0)))
        def _():
            arrived(tot.at[c], tot_recv.at[c], tot.at[c])

    sums_ref[...] = tot[...]

    for half in range(2):
        for o in range(1, heads):
            head_copy(half, o).wait_send()

    @pl.loop(1, peers)
    def _(o):
        bct_copy(o).wait_send()

    @pl.when(me < seq - 1)
    def _():
        halo_bc().wait_send()
        for c in range(groups):
            halo_x(c).wait_send()

        @pl.loop(0, halves)
        def _(h):
            forward(h).wait_send()

    @pl.when(me > 0)
    def _():
        for half in range(2):
            for o in range(heads):
                nbc_copy(half, o).wait_send()

        @pl.loop(0, halves)
        def _(h):
            backward(h).wait_send()

        @pl.loop(0, groups)
        def _(c):
            edge_copy(c).wait_send()

    @pl.loop(0, groups + 1)
    def _(c):
        @pl.when(jnp.logical_not(owner(c)))
        def _():
            core_copy(c).wait_send()

        @pl.when(owner(c) & (me > 0))
        def _():
            ride_copy(c).wait_send()

        @pl.when(owner(c) & (me == 0))
        def _():
            for move in tot_copies(c):
                move.wait_send()


def final_kernel(
    head_dim, norm, pieces, y_in, gx_in, gbc_in, tot, bsum, y_out, gx_out, gbc_out, sums_out, bsum_out,
    skip_out, sums, sums_bc, skips, sem,
):
    tokens = y_in.shape[0]
    groups = tot.shape[0] - 1
    columns = 2 * tot.shape[2]
    taps = sums.shape[0]
    count = skips.shape[1]
    block = tokens // pieces
    moves = []
    for i in range(pieces):
        at = pl.ds(i * block, block)
        moves.append(pltpu.make_async_copy(y_in.at[at], y_out.at[at], sem.at[0, i]))
        moves.append(pltpu.make_async_copy(gx_in.at[at], gx_out.at[at], sem.at[1, i]))
    moves.append(pltpu.make_async_copy(gbc_in, gbc_out, sem.at[2, 0]))
    for move in moves:
        move.start()
    tiles = columns // 128
    for c in range(groups):
        for j in range(tiles):
            lo = c * columns + j * 128
            row = (j % 2) * taps
            sums[:, lo : lo + 128] = norm * tot[
                c, row : row + taps, j // 2 * 128 : (j // 2 + 1) * 128
            ]
    rest = tot[groups, :, 0 : groups * tiles]
    near = 128 // head_dim
    pick = ones_where(
        iota((groups * tiles, count), 0) == iota((groups * tiles, count), 1) // near
    )
    found = jnp.zeros((8, count), f32)
    for _ in range(3):
        piece = rest.astype(bf16)
        rest = rest - piece.astype(f32)
        found = found + dot(piece, pick, 1, 0)
    own = iota((8, count), 1) % near == iota((8, count), 0)
    skips[...] = jnp.sum(jnp.where(own, found, 0.0), axis=0, keepdims=True) * (
        norm * float(head_dim) ** (-0.5)
    )
    half = bsum.shape[1]
    sums_bc[:, :half] = bsum[0:taps] * norm
    sums_bc[:, half:] = bsum[taps:] * norm
    late = [
        pltpu.make_async_copy(src, dst, sem.at[2, i + 1])
        for i, (src, dst) in enumerate(((sums, sums_out), (sums_bc, bsum_out), (skips, skip_out)))
    ]
    for move in late:
        move.start()
    for move in moves + late:
        move.wait()


def local(x_input, bc_input, decays, conv_x, conv_bc, skip_gain, grad_out):
    x = x_input[0]
    bc = bc_input[0]
    d = decays[0]
    g = grad_out[0]
    tokens, channels = x.shape
    taps = conv_x.shape[0]
    count = d.shape[0]
    head_dim = channels // count
    n = bc.shape[1] // 2
    scale = float(n) ** (-0.5)
    seq = lax.axis_size("seq")
    heads = lax.axis_size("head")
    cores = lax.axis_size("dp")
    peers = seq * heads * cores
    width = next(k for k in (8, 4) if count % k == 0)
    groups = count // width
    columns = width * head_dim
    norm = float(tokens * seq * cores) ** (-0.5)
    sizes = (seq, heads, cores)

    held = pltpu.with_memory_space_constraint

    def out(shape, dtype):
        return jax.ShapeDtypeStruct(shape, dtype)

    dma = pltpu.SemaphoreType.DMA
    vmem = pltpu.VMEM
    anywhere = pl.BlockSpec(memory_space=pl.ANY)
    inside = pl.BlockSpec(memory_space=vmem)
    wide = (groups, tokens, columns)
    state = (2 * groups, n, columns // 2)
    part = (groups + 1, 8, columns // 2)
    y, gx, gbc, sums, bsum = pl.pallas_call(
        functools.partial(main_kernel, head_dim, scale, sizes),
        in_specs=[anywhere] * 7,
        out_specs=[inside] * 5,
        out_shape=[
            vmem((tokens, channels), bf16), vmem((tokens, channels), bf16),
            vmem((tokens, 2 * n), bf16), vmem(part, f32), vmem((8, n), f32),
        ],
        scratch_shapes=[
            vmem(wide, bf16), vmem(wide, bf16), vmem((tokens, 2 * n), bf16),
            vmem((count, tokens), f32), vmem((taps, channels), f32), vmem((taps, 2 * n), f32), pltpu.SMEM((count,), f32),
            vmem(wide, bf16), vmem(wide, bf16), vmem(wide, bf16), vmem(wide, bf16),
            vmem(wide, bf16), vmem(wide, bf16), vmem(wide, f32), vmem(wide, f32),
            vmem(state, bf16), vmem(state, bf16), vmem(state, bf16), vmem(state, bf16),
            vmem((2 * groups, 1, columns // 2), f32), vmem((2 * tokens, 2 * count), bf16),
            vmem((count, tokens), f32),
            vmem((groups, width, tokens), f32), vmem((groups, tokens, width), f32),
            vmem((16, channels), bf16), vmem((16, 2 * n), bf16),
            vmem((tokens, 2 * n), bf16), vmem((2 * n, tokens), bf16),
            vmem((tokens, 2 * n), f32), vmem((tokens + 8, 2 * n), f32),
            vmem((columns // 128, tokens + 8, 128), f32),
            vmem((tokens, tokens), f32), vmem((tokens, tokens), f32),
            vmem((2, tokens, n), f32),
            vmem((groups, columns // 128, 8, 128), f32),
            vmem((groups, 16, columns), f32), vmem((groups, 16, 128), bf16),
            vmem((groups, 16, 128), bf16), vmem(part, f32), vmem(part, f32), vmem(part, f32),
            vmem(part, f32), vmem((2, tokens, n), bf16), vmem((2, heads, tokens, n), bf16),
            vmem((2, heads, 16, n), bf16), vmem((tokens + 8, 2 * n), f32),
            vmem((8, n), f32), vmem((peers, 8, n), f32),
            dma((groups,)), dma((groups,)), dma((5,)), dma((groups + 1,)), dma((groups + 1,)),
            dma((2 * groups,)), dma((2 * groups,)), dma((2 * groups,)), dma((2 * groups,)),
            dma((groups,)), dma((groups,)), dma((groups + 1,)), dma((groups + 1,)),
            dma((groups + 1,)), dma((groups + 1,)), dma((groups + 1, seq * cores)),
            dma((groups + 1,)),
            dma((2, heads)), dma((2, heads)), dma((2, heads)), dma((2, heads)),
            dma((peers,)), dma((peers,)),
        ],
        compiler_params=pltpu.CompilerParams(
            vmem_limit_bytes=44 * 1024 * 1024, collective_id=0, has_side_effects=True,
        ),
        name="main",
    )(*(held(a, pltpu.HBM) for a in (x, bc, d, conv_x, conv_bc, skip_gain, g)))

    pieces = 4
    y, gx, gbc, taps_x, taps_bc, skips = pl.pallas_call(
        functools.partial(final_kernel, head_dim, norm, pieces),
        in_specs=[inside] * 5,
        out_specs=[anywhere] * 6,
        out_shape=[
            out((tokens, channels), bf16), out((tokens, channels), bf16),
            out((tokens, 2 * n), bf16), out((taps, channels), f32), out((taps, 2 * n), f32),
            out((1, count), f32),
        ],
        scratch_shapes=[
            vmem((taps, channels), f32), vmem((taps, 2 * n), f32), vmem((1, count), f32),
            dma((3, 4)),
        ],
        compiler_params=pltpu.CompilerParams(vmem_limit_bytes=16 * 1024 * 1024),
        name="final",
    )(y, gx, gbc, sums, bsum)
    return y[None], gx[None], gbc[None], taps_x, taps_bc, skips.reshape(count)


def solution(mesh):
    return jax.shard_map(
        local,
        mesh=mesh,
        in_specs=(
            P(("groups", "dp"), "seq", "head"),
            P(("groups", "dp"), "seq", None),
            P(("groups", "dp"), "head", "seq"),
            P(None, "head"),
            P(),
            P("head"),
            P(("groups", "dp"), "seq", "head"),
        ),
        out_specs=(
            P(("groups", "dp"), "seq", "head"),
            P(("groups", "dp"), "seq", "head"),
            P(("groups", "dp"), "seq", None),
            P("groups", "head"),
            P("groups", None),
            P(("groups", "head")),
        ),
        check_vma=False,
    )
```

```python
import functools

import jax
import jax.numpy as jnp
from jax import lax
from jax.experimental import pallas as pl
from jax.experimental.pallas import tpu as pltpu
from jax.sharding import PartitionSpec as P

MESH = pl.DeviceIdType.MESH
f32 = jnp.float32
bf16 = jnp.bfloat16
STRIP = 64
LAG = 3
RIDE = 4
EARLY = 2


def dot(a, b, ca, cb):
    return lax.dot_general(a, b, (((ca,), (cb,)), ((), ())), preferred_element_type=f32)


def ones_where(mask):
    return mask.astype(f32).astype(bf16)


def iota(shape, axis):
    return lax.broadcasted_iota(jnp.int32, shape, axis)


def conv_taps(pad_ref, weight, first, tokens):
    total = weight[0:1, :] * pad_ref[pl.ds(first, tokens), :]
    for k in range(1, weight.shape[0]):
        total = total + weight[k : k + 1, :] * pad_ref[pl.ds(first + k, tokens), :]
    return total


def fold(a):
    return jnp.sum(a.reshape(a.shape[0] // 8, 8, a.shape[1]), axis=0)


def silu_parts(pre):
    sigma = 0.5 * jnp.tanh(0.5 * pre) + 0.5
    return pre * sigma, sigma * (1.0 + pre * (1.0 - sigma))


def main_kernel(
    head_dim, scale, sizes,
    x_hbm, bc_hbm, d_hbm, cw_hbm, cbc_hbm, skip_hbm, g_hbm,
    y_ref, gx_ref, gbc_ref, sums_ref, bsum_ref,
    xv, gv, bcv, dv, cwv, cbcv, skip_ref,
    in_all, ds_all, lead_all, gt_all, lg_all, tw_all, ya, da, s_all, u_all, p_all, q_all, et, fac, cum_all,
    cum_r, cum_t, halo, halo_b, mapped, mapped_t, dsbc, bp, xp, sim, dsim, dbc,
    skip_sums, tails, edges, next_x, parts, ride_in, core_in, tot, dbc_out, head_in, next_bc, dbp, bct, bct_in,
    load_x, load_g, load_small, halo_send, halo_recv, send_f, recv_f, send_b, recv_b,
    edge_send, edge_recv, ride_send, ride_recv, core_send, core_recv, tot_send, tot_recv,
    head_send, head_recv, nbc_send, nbc_recv, bct_send, bct_recv,
):
    groups, tokens, columns = xv.shape
    width = columns // head_dim
    count = groups * width
    n = mapped.shape[1] // 2
    taps = cwv.shape[0]
    first = 9 - taps
    seq, heads, cores = sizes
    peers = seq * heads * cores
    me = lax.axis_index("seq")
    back = seq - 1 - me
    hd = lax.axis_index("head")
    co = lax.axis_index("dp")
    rank = (me * heads + hd) * cores + co

    def copy(src, dst, send, recv, device):
        return pltpu.make_async_remote_copy(
            src_ref=src, dst_ref=dst, send_sem=send, recv_sem=recv, device_id=device,
            device_id_type=MESH,
        )

    def peer(o):
        at = lax.rem(rank + o, peers)
        high = at // cores
        return at, {"seq": high // heads, "head": lax.rem(high, heads), "dp": lax.rem(at, cores)}

    def lanes(c):
        return pl.ds(pl.multiple_of(c * columns, columns), columns)

    def x_load(c):
        return pltpu.make_async_copy(x_hbm.at[:, lanes(c)], xv.at[c], load_x.at[c])

    def g_load(c):
        return pltpu.make_async_copy(g_hbm.at[:, lanes(c)], gv.at[c], load_g.at[c])

    def halo_x(c):
        return copy(
            x_hbm.at[tokens - 16 : tokens, lanes(c)], halo.at[:, lanes(c)], halo_send.at[c],
            halo_recv.at[c], {"seq": me + 1},
        )

    def halo_bc():
        return copy(
            bc_hbm.at[tokens - 16 : tokens], halo_b, halo_send.at[groups], halo_recv.at[groups],
            {"seq": me + 1},
        )

    def forward(c):
        return copy(s_all.at[c], p_all.at[c], send_f.at[c], recv_f.at[c], {"seq": me + 1})

    def backward(c):
        return copy(u_all.at[c], q_all.at[c], send_b.at[c], recv_b.at[c], {"seq": me - 1})

    def edge_copy(c):
        return copy(edges.at[c], next_x.at[c], edge_send.at[c], edge_recv.at[c], {"seq": me - 1})

    def ride_copy(c):
        return copy(parts.at[c], ride_in.at[c], ride_send.at[c], ride_recv.at[c], {"seq": me - 1})

    def core_copy(c):
        return copy(
            parts.at[c], core_in.at[c], core_send.at[c], core_recv.at[c],
            {"dp": lax.rem(co + 1, cores)},
        )

    def tot_copies(c):
        return [
            copy(
                tot.at[c], tot.at[c], tot_send.at[c, z * cores + q], tot_recv.at[c],
                {"seq": z, "dp": lax.rem(co + q, cores)},
            )
            for z in range(seq)
            for q in range(cores)
            if z + q > 0
        ]

    def owner(c):
        return co == lax.rem(groups - c, cores)

    def head_copy(half, o):
        return copy(
            dbc_out.at[half], head_in.at[half, hd], head_send.at[half, o],
            head_recv.at[half, hd], {"head": lax.rem(hd + o, heads)},
        )

    def nbc_copy(half, o):
        return copy(
            dbc_out.at[half, 0:16], next_bc.at[half, hd], nbc_send.at[half, o],
            nbc_recv.at[half, hd], {"head": lax.rem(hd + o, heads), "seq": me - 1},
        )

    def bct_copy(o):
        return copy(bct, bct_in.at[rank], bct_send.at[o], bct_recv.at[rank], peer(o)[1])

    def arrived(dst, sem, source):
        copy(source, dst, sem, sem, peer(1)[1]).wait_recv()

    small = [
        pltpu.make_async_copy(src, dst, load_small.at[i])
        for i, (src, dst) in enumerate(
            ((d_hbm, dv), (bc_hbm, bcv), (cbc_hbm, cbcv), (cw_hbm, cwv), (skip_hbm, skip_ref))
        )
    ]
    for load in small:
        load.start()

    @pl.loop(0, groups)
    def _(c):
        g_load(c).start()
        x_load(c).start()

    barrier = pltpu.get_barrier_semaphore()

    @pl.loop(1, peers)
    def _(o):
        pl.semaphore_signal(barrier, inc=1, device_id=peer(o)[1], device_id_type=MESH)

    pl.semaphore_wait(barrier, peers - 1)

    @pl.when(me < seq - 1)
    def _():
        halo_bc().start()
        for c in range(groups):
            halo_x(c).start()

    @pl.when(me == 0)
    def _():
        halo_b[...] = jnp.zeros(halo_b.shape, bf16)
        halo[...] = jnp.zeros(halo.shape, bf16)

    small[0].wait()
    d = dv[...]
    rest = jnp.log(d)
    upto = ones_where(iota((tokens, tokens), 0) <= iota((tokens, tokens), 1))
    rows = jnp.zeros(d.shape, f32)
    for _ in range(3):
        piece = rest.astype(bf16)
        rest = rest - piece.astype(f32)
        rows = rows + dot(piece, upto, 1, 0)
    squared = (1.0 - d) * (1.0 + d)
    cum_all[...] = rows - 0.5 * jnp.log(squared)
    last = rows[:, tokens - 1 :]
    factors = jnp.concatenate([jnp.exp(rows), jnp.sqrt(squared) * jnp.exp(last - rows)], axis=1)
    high = factors.astype(bf16).astype(f32)
    both = jnp.concatenate([high, factors - high], axis=0).astype(bf16)
    same = ones_where(iota((2 * count, 2 * count), 0) == iota((2 * count, 2 * count), 1))
    fac[...] = dot(both, same, 0, 0).astype(bf16)

    def spread(c):
        pick = iota((2 * count, columns), 0) % count == c * width + iota(
            (2 * count, columns), 1
        ) // head_dim
        return dot(fac[...], ones_where(pick), 1, 0)

    def skip_row(c):
        lane = iota((1, columns), 1) // head_dim
        skip = jnp.zeros((1, columns), f32)
        for j in range(width):
            skip = jnp.where(lane == j, skip_ref[c * width + j], skip)
        return skip

    tiles = [slice(j * 128, (j + 1) * 128) for j in range(columns // 128)]
    strips = [slice(r, r + STRIP) for r in range(0, tokens, STRIP)]
    part = columns // 2

    def phase_u(c):
        factor = spread(c)
        lead_all[c] = factor[:tokens].astype(bf16)
        gt_all[c] = factor[tokens:].astype(bf16)
        for e in range(2):
            et[2 * c + e] = factor[tokens - 1 : tokens, e * part : (e + 1) * part]
        for tile in tiles:
            for rows in strips:
                lg_all[c, rows, tile] = gv[c, rows, tile] * lead_all[c, rows, tile]

    def send_u(c, to):
        grown = dot(mapped_t[n:, :], lg_all[c], 1, 0).astype(bf16)
        for e in range(2):
            u_all[2 * to + e] = grown[:, e * part : (e + 1) * part]

    def phase_a(c):
        x_load(c).wait()

        @pl.when(me > 0)
        def _():
            halo_x(c).wait_recv()

        @pl.when(c < groups - 1)
        def _():
            g_load(c + 1).wait()

        after = lax.min(c + 1, groups - 1)
        phase_u(after)
        old = halo[:, lanes(c)].astype(f32)[8:]
        weight = cwv[:, lanes(c)]
        for j, tile in enumerate(tiles):
            xp[j, 0:8] = old[:, tile]
            xp[j, 8:] = xv[c, :, tile].astype(f32)
        for j, tile in enumerate(tiles):
            skipped = jnp.zeros((8, 128), f32)
            for rows in strips:
                pre = weight[0:1, tile] * xp[j, pl.ds(first + rows.start, STRIP)]
                for k in range(1, taps):
                    pre = pre + weight[k : k + 1, tile] * xp[j, pl.ds(first + k + rows.start, STRIP)]
                value, slope = silu_parts(pre)
                inner = value.astype(bf16)
                in_all[c, rows, tile] = inner
                ds_all[c, rows, tile] = slope.astype(bf16)
                tw_all[c, rows, tile] = inner * gt_all[c, rows, tile]
                skipped = skipped + fold(gv[c, rows, tile].astype(f32) * inner.astype(f32))
            skip_sums[c, j] = skipped
        state = dot(mapped_t[:n, :], tw_all[c], 1, 0).astype(bf16)
        send_u(after, c + 1)
        for e in range(2):
            s_all[2 * c + e] = state[:, e * part : (e + 1) * part]

    def advance(c, hops, make, own, incoming):
        @pl.when(hops == 0)
        def _():
            incoming[c] = jnp.zeros(incoming.shape[1:], bf16)

        @pl.when(hops > 0)
        def _():
            make(c).wait_recv()

            @pl.when(hops < seq - 1)
            def _():
                own[c] = (incoming[c].astype(f32) * et[c] + own[c].astype(f32)).astype(bf16)

        @pl.when(hops < seq - 1)
        def _():
            make(c).start()

    def setup_b():
        turned = jnp.zeros((tokens, count), f32)
        rest = jnp.log(dv[...])
        upto = ones_where(iota((tokens, tokens), 0) <= iota((tokens, tokens), 1))
        for _ in range(3):
            piece = rest.astype(bf16)
            rest = rest - piece.astype(f32)
            turned = turned + dot(upto, piece, 0, 1)
        for c in range(groups):
            cum_t[c] = turned[:, c * width : (c + 1) * width]
            cum_r[c] = cum_all[c * width : (c + 1) * width, :]
        sim[...] = dot(mapped[:, n:], mapped[:, :n], 1, 1)
        dsim[...] = jnp.zeros_like(dsim)
        dbc[...] = jnp.zeros_like(dbc)
        count_tiles = groups * len(tiles)
        rest = jnp.sum(skip_sums[...].reshape(count_tiles, 8, 128), axis=1)
        pick = ones_where(iota((8, 128), 1) // head_dim == iota((8, 128), 0))
        found = jnp.zeros((8, count_tiles), f32)
        for _ in range(3):
            piece = rest.astype(bf16)
            rest = rest - piece.astype(f32)
            found = found + dot(pick, piece, 1, 1)
        parts[groups] = jnp.zeros(parts.shape[1:], f32)
        parts[groups, :, 0:count_tiles] = found
        share(groups)

    def phase_b(c):
        mid = tokens // 2
        lower = iota((mid, mid), 0) >= iota((mid, mid), 1)
        empty = jnp.zeros((mid, mid), bf16)
        pair = 2 * head_dim
        side = iota((1, pair), 1) < head_dim
        g_t = gv[c].T
        corners = None
        turned = []
        for j in range(width // 2):
            cols = slice(j * pair, (j + 1) * pair)
            in_pair = in_all[c, :, cols]
            g_pair = gv[c, :, cols]
            found = []
            for e in range(2):
                h = 2 * j + e
                mine = side if e == 0 else jnp.logical_not(side)
                near = dot(jnp.where(mine, g_pair, jnp.zeros_like(g_pair)), in_pair, 1, 1)
                at = cum_t[c, :, h : h + 1]
                to = cum_r[c, h : h + 1, :]
                top = jnp.exp(jnp.where(lower, at[:mid] - to[:, :mid], -1e30))
                left = jnp.exp(at[mid:] - to[:, :mid])
                low = jnp.exp(jnp.where(lower, at[mid:] - to[:, mid:], -1e30))
                mix = jnp.concatenate(
                    [
                        jnp.concatenate([(top * sim[:mid, :mid]).astype(bf16), empty], axis=1),
                        jnp.concatenate(
                            [
                                (left * sim[mid:, :mid]).astype(bf16),
                                (low * sim[mid:, mid:]).astype(bf16),
                            ],
                            axis=1,
                        ),
                    ],
                    axis=0,
                )
                terms = [top * near[:mid, :mid], left * near[mid:, :mid], low * near[mid:, mid:]]
                corners = terms if corners is None else [a + b for a, b in zip(corners, terms)]
                found.append(dot(mix, in_pair, 1, 0))
                turned.append(dot(g_t[h * head_dim : (h + 1) * head_dim], mix, 1, 0))
            ya[c, :, cols] = jnp.where(side, found[0], found[1])
        dsim[:mid, :mid] += corners[0]
        dsim[mid:, :mid] += corners[1]
        dsim[mid:, mid:] += corners[2]
        da[c] = jnp.concatenate(turned, axis=0).T

    def phase_p(c):
        skip = skip_row(c)
        for e in range(2):
            p = p_all[2 * c + e]
            cols = slice(e * part, (e + 1) * part)
            seen = dot(mapped[:, n:], p, 1, 0)
            lead = lead_all[c, :, cols].astype(f32)
            y = scale * (ya[c, :, cols] + lead * seen)
            y = (y + skip[:, cols] * in_all[c, :, cols].astype(f32)).astype(bf16)
            y_ref[:, pl.ds(pl.multiple_of(c * columns + e * part, part), part)] = y
            dbc[1] += dot(lg_all[c, :, cols], p, 1, 1)

    def phase_q(c):
        skip = skip_row(c)
        weight = cwv[:, lanes(c)]
        old = halo[:, lanes(c)].astype(f32)
        heads_of = []
        for e in range(2):
            q = q_all[2 * c + e]
            cols = slice(e * part, (e + 1) * part)
            seen = dot(mapped[:, :n], q, 1, 0)
            dbc[0] += dot(tw_all[c, :, cols], q, 1, 1)
            for j in range(e * part // 128, (e + 1) * part // 128):
                tile = tiles[j]
                own = slice(j * 128 - e * part, (j + 1) * 128 - e * part)
                for rows in strips:
                    g = gv[c, rows, tile].astype(f32)
                    d_w = scale * (da[c, rows, tile] + gt_all[c, rows, tile].astype(f32) * seen[rows, own])
                    d_pre = (d_w + skip[:, tile] * g) * ds_all[c, rows, tile].astype(f32)
                    xp[j, rows] = d_pre
                xp[j, tokens:] = jnp.zeros((8, 128), f32)
                edge = xp[j, 0:8]
                heads_of.append(edge[0 : taps - 1])
                sums = [jnp.zeros((8, 128), f32) for _ in range(taps)]
                for rows in strips:
                    x = xv[c, rows, tile].astype(f32)
                    total = jnp.zeros((STRIP, 128), f32)
                    for k in range(taps):
                        moved = xp[j, pl.ds(taps - 1 - k + rows.start, STRIP)]
                        total = total + weight[k : k + 1, tile] * moved
                        sums[k] = sums[k] + fold(x * moved)
                    at = pl.ds(pl.multiple_of(c * columns + j * 128, 128), 128)
                    gx_ref[rows, at] = total.astype(bf16)
                    if rows.stop == tokens:
                        tails[c, :, tile] = total[STRIP - 16 :]
                for k in range(taps):
                    found = jnp.sum(sums[k], axis=0, keepdims=True)
                    for t in range(taps - 1 - k):
                        at = 16 - (taps - 1 - k) + t
                        found = found + old[at : at + 1, tile] * edge[t : t + 1]
                    row = (j % 2) * taps + k
                    parts[c, row : row + 1, j // 2 * 128 : (j // 2 + 1) * 128] = found

        heads_of.append(jnp.zeros((16 - len(tiles) * (taps - 1), 128), f32))
        edges[c] = jnp.concatenate(heads_of, axis=0).astype(bf16)

        @pl.when(me > 0)
        def _():
            edge_copy(c).start()

        share(c)

    def share(c):
        @pl.when(jnp.logical_not(owner(c)))
        def _():
            core_copy(c).start()

    def ride(c):
        @pl.when(owner(c))
        def _():
            arrived(core_in.at[c], core_recv.at[c], parts.at[c])
            parts[c] = parts[c] + core_in[c]

            @pl.when(me < seq - 1)
            def _():
                ride_copy(c).wait_recv()
                parts[c] = parts[c] + ride_in[c]

            @pl.when(me > 0)
            def _():
                ride_copy(c).start()

            @pl.when(me == 0)
            def _():
                tot[c] = parts[c]
                for move in tot_copies(c):
                    move.start()

    def finish(half):
        other = mapped[:, n:] if half == 0 else mapped[:, :n]
        side = 0 if half == 0 else 1
        cols = slice(half * n, (half + 1) * n)
        whole = dbc[half] + dot(dsim[...].astype(bf16), other, side, 0)
        whole = scale * whole * dsbc[:, cols]
        dbc_out[half] = whole.astype(bf16)
        for o in range(1, heads):
            head_copy(half, o).start()

        @pl.when(me > 0)
        def _():
            for o in range(heads):
                nbc_copy(half, o).start()

        head_in[half, hd] = dbc_out[half]
        for k in range(taps):
            bct[half * taps + k : half * taps + k + 1, :] = jnp.sum(
                whole * bp[pl.ds(first + k, tokens), cols], axis=0, keepdims=True
            )

    g_load(0).wait()
    phase_u(0)

    for load in small[1:]:
        load.wait()

    @pl.when(me > 0)
    def _():
        halo_bc().wait_recv()

    bp[0:8, :] = halo_b[...].astype(f32)[8:]
    bp[8:, :] = bcv[...].astype(f32)
    value, slope = silu_parts(conv_taps(bp, cbcv[...], first, tokens))
    mapped[...] = value.astype(bf16)
    dsbc[...] = slope
    unit = ones_where(iota((tokens, tokens), 0) == iota((tokens, tokens), 1))
    mapped_t[...] = dot(mapped[...], unit, 0, 0).astype(bf16)
    send_u(0, 0)

    @pl.when(back == 0)
    def _():
        for e in range(2):
            advance(e, back, backward, u_all, q_all)

    halves = 2 * groups
    shift = groups - 1 - LAG

    def due(s, base, hops):
        gap = lax.min(hops, 1) * (shift + 2 + LAG * hops)
        c = lax.min(s - base, (s - gap + 4096) // 2 - 2048)
        return c, (c >= 0) & (c < groups) & (lax.max(base + c, 2 * c + gap) == s)

    slots = halves + groups + max(LAG * (seq - 2), RIDE * (seq - 1) - 2)

    both = lax.max(halves + groups - 1, halves + shift + LAG * lax.max(me, back))

    @pl.loop(0, slots)
    def _(s):
        @pl.when(s < groups)
        def _():
            phase_a(s)

        @pl.when((s < groups) & (me == 0))
        def _():
            for e in range(2):
                advance(2 * s + e, me, forward, s_all, p_all)

        @pl.when((s < groups - 1) & (back == 0))
        def _():
            for e in range(2):
                advance(2 * s + 2 + e, back, backward, u_all, q_all)

        @pl.when(s == groups - 1)
        def _():
            setup_b()

        @pl.when((s >= groups) & (s < halves))
        def _():
            phase_b(s - groups)

        cq, has_q = due(s, groups + groups * lax.min(back, 1), back)
        cr, has_r = due(s, groups + 1 + lax.min(back, 1) * (groups - 3 + RIDE * back) - EARLY * lax.max(1 - me, 0), back)
        cp, has_p = due(s, halves, me)

        @pl.when(has_q)
        def _():
            phase_q(cq)

        hf = s - shift - LAG * me
        hb = s - shift - LAG * back

        @pl.when((me > 0) & (hf >= 0) & (hf < halves))
        def _():
            advance(hf, me, forward, s_all, p_all)

        @pl.when((back > 0) & (hb >= 0) & (hb < halves))
        def _():
            advance(hb, back, backward, u_all, q_all)

        @pl.when(has_q & (cq == groups - 1))
        def _():
            finish(0)

        @pl.when(has_p)
        def _():
            phase_p(cp)

            @pl.when(cp == groups - 1)
            def _():
                finish(1)

        @pl.when(s == both)
        def _():
            bct_in[rank] = bct[...]

            @pl.loop(1, peers)
            def _(o):
                bct_copy(o).start()

        @pl.when(s == groups + 1 + RIDE * back)
        def _():
            ride(groups)

        @pl.when(has_r)
        def _():
            ride(cr)


    @pl.when(me < seq - 1)
    def _():
        at = iota((16, 1), 0)
        for c in range(groups):
            edge_copy(c).wait_recv()
            after = next_x[c].astype(f32)
            for j, tile in enumerate(tiles):
                fixed = tails[c, :, tile]
                lo = c * columns + j * 128
                for r in range(taps - 1):
                    row = jnp.zeros((1, 128), f32)
                    for k in range(r + 1):
                        e = j * (taps - 1) + r - k
                        row = row + cwv[k : k + 1, lo : lo + 128] * after[e : e + 1]
                    fixed = fixed + jnp.where(at == 16 - (taps - 1) + r, row, 0.0)
                gx_ref[tokens - 16 :, lo : lo + 128] = fixed.astype(bf16)

    for half in range(2):
        for o in range(1, heads):
            at = lax.rem(hd + o, heads)
            arrived(head_in.at[half, at], head_recv.at[half, at], dbc_out.at[half])
        cols = slice(half * n, (half + 1) * n)
        full = head_in[half, 0].astype(f32)
        for h in range(1, heads):
            full = full + head_in[half, h].astype(f32)
        dbp[0:tokens, cols] = full

        @pl.when(me == seq - 1)
        def _():
            dbp[tokens:, cols] = jnp.zeros((8, n), f32)

        @pl.when(me < seq - 1)
        def _():
            for h in range(heads):
                arrived(next_bc.at[half, h], nbc_recv.at[half, h], dbc_out.at[half, 0:16])
            rows = next_bc[half, 0].astype(f32)
            for h in range(1, heads):
                rows = rows + next_bc[half, h].astype(f32)
            dbp[tokens:, cols] = rows[0:8]

    grad = jnp.zeros((tokens, 2 * n), f32)
    for k in range(taps):
        grad = grad + cbcv[k : k + 1, :] * dbp[pl.ds(taps - 1 - k, tokens), :]
    gbc_ref[...] = grad.astype(bf16)

    @pl.loop(1, peers)
    def _(o):
        at = lax.rem(rank + o, peers)
        arrived(bct_in.at[at], bct_recv.at[at], bct)

    bsum = bct_in[0]
    for i in range(1, peers):
        bsum = bsum + bct_in[i]
    bsum_ref[...] = bsum

    @pl.loop(0, groups + 1)
    def _(c):
        @pl.when(jnp.logical_not(owner(c) & (me == 0)))
        def _():
            arrived(tot.at[c], tot_recv.at[c], tot.at[c])

    sums_ref[...] = tot[...]

    for half in range(2):
        for o in range(1, heads):
            head_copy(half, o).wait_send()

    @pl.loop(1, peers)
    def _(o):
        bct_copy(o).wait_send()

    @pl.when(me < seq - 1)
    def _():
        halo_bc().wait_send()
        for c in range(groups):
            halo_x(c).wait_send()

        @pl.loop(0, halves)
        def _(h):
            forward(h).wait_send()

    @pl.when(me > 0)
    def _():
        for half in range(2):
            for o in range(heads):
                nbc_copy(half, o).wait_send()

        @pl.loop(0, halves)
        def _(h):
            backward(h).wait_send()

        @pl.loop(0, groups)
        def _(c):
            edge_copy(c).wait_send()

    @pl.loop(0, groups + 1)
    def _(c):
        @pl.when(jnp.logical_not(owner(c)))
        def _():
            core_copy(c).wait_send()

        @pl.when(owner(c) & (me > 0))
        def _():
            ride_copy(c).wait_send()

        @pl.when(owner(c) & (me == 0))
        def _():
            for move in tot_copies(c):
                move.wait_send()


def final_kernel(
    head_dim, norm, pieces, y_in, gx_in, gbc_in, tot, bsum, y_out, gx_out, gbc_out, sums_out, bsum_out,
    skip_out, sums, sums_bc, skips, sem,
):
    tokens = y_in.shape[0]
    groups = tot.shape[0] - 1
    columns = 2 * tot.shape[2]
    taps = sums.shape[0]
    count = skips.shape[1]
    block = tokens // pieces
    moves = []
    for i in range(pieces):
        at = pl.ds(i * block, block)
        moves.append(pltpu.make_async_copy(y_in.at[at], y_out.at[at], sem.at[0, i]))
        moves.append(pltpu.make_async_copy(gx_in.at[at], gx_out.at[at], sem.at[1, i]))
    moves.append(pltpu.make_async_copy(gbc_in, gbc_out, sem.at[2, 0]))
    for move in moves:
        move.start()
    tiles = columns // 128
    for c in range(groups):
        for j in range(tiles):
            lo = c * columns + j * 128
            row = (j % 2) * taps
            sums[:, lo : lo + 128] = norm * tot[
                c, row : row + taps, j // 2 * 128 : (j // 2 + 1) * 128
            ]
    rest = tot[groups, :, 0 : groups * tiles]
    near = 128 // head_dim
    pick = ones_where(
        iota((groups * tiles, count), 0) == iota((groups * tiles, count), 1) // near
    )
    found = jnp.zeros((8, count), f32)
    for _ in range(3):
        piece = rest.astype(bf16)
        rest = rest - piece.astype(f32)
        found = found + dot(piece, pick, 1, 0)
    own = iota((8, count), 1) % near == iota((8, count), 0)
    skips[...] = jnp.sum(jnp.where(own, found, 0.0), axis=0, keepdims=True) * (
        norm * float(head_dim) ** (-0.5)
    )
    half = bsum.shape[1]
    sums_bc[:, :half] = bsum[0:taps] * norm
    sums_bc[:, half:] = bsum[taps:] * norm
    late = [
        pltpu.make_async_copy(src, dst, sem.at[2, i + 1])
        for i, (src, dst) in enumerate(((sums, sums_out), (sums_bc, bsum_out), (skips, skip_out)))
    ]
    for move in late:
        move.start()
    for move in moves + late:
        move.wait()


def local(x_input, bc_input, decays, conv_x, conv_bc, skip_gain, grad_out):
    x = x_input[0]
    bc = bc_input[0]
    d = decays[0]
    g = grad_out[0]
    tokens, channels = x.shape
    taps = conv_x.shape[0]
    count = d.shape[0]
    head_dim = channels // count
    n = bc.shape[1] // 2
    scale = float(n) ** (-0.5)
    seq = lax.axis_size("seq")
    heads = lax.axis_size("head")
    cores = lax.axis_size("dp")
    peers = seq * heads * cores
    width = next(k for k in (8, 4) if count % k == 0)
    groups = count // width
    columns = width * head_dim
    norm = float(tokens * seq * cores) ** (-0.5)
    sizes = (seq, heads, cores)

    held = pltpu.with_memory_space_constraint

    def out(shape, dtype):
        return jax.ShapeDtypeStruct(shape, dtype)

    dma = pltpu.SemaphoreType.DMA
    vmem = pltpu.VMEM
    anywhere = pl.BlockSpec(memory_space=pl.ANY)
    inside = pl.BlockSpec(memory_space=vmem)
    wide = (groups, tokens, columns)
    state = (2 * groups, n, columns // 2)
    part = (groups + 1, 8, columns // 2)
    y, gx, gbc, sums, bsum = pl.pallas_call(
        functools.partial(main_kernel, head_dim, scale, sizes),
        in_specs=[anywhere] * 7,
        out_specs=[inside] * 5,
        out_shape=[
            vmem((tokens, channels), bf16), vmem((tokens, channels), bf16),
            vmem((tokens, 2 * n), bf16), vmem(part, f32), vmem((8, n), f32),
        ],
        scratch_shapes=[
            vmem(wide, bf16), vmem(wide, bf16), vmem((tokens, 2 * n), bf16),
            vmem((count, tokens), f32), vmem((taps, channels), f32), vmem((taps, 2 * n), f32), pltpu.SMEM((count,), f32),
            vmem(wide, bf16), vmem(wide, bf16), vmem(wide, bf16), vmem(wide, bf16),
            vmem(wide, bf16), vmem(wide, bf16), vmem(wide, f32), vmem(wide, f32),
            vmem(state, bf16), vmem((2 * groups + 2, n, columns // 2), bf16), vmem(state, bf16),
            vmem(state, bf16),
            vmem((2 * groups, 1, columns // 2), f32), vmem((2 * tokens, 2 * count), bf16),
            vmem((count, tokens), f32),
            vmem((groups, width, tokens), f32), vmem((groups, tokens, width), f32),
            vmem((16, channels), bf16), vmem((16, 2 * n), bf16),
            vmem((tokens, 2 * n), bf16), vmem((2 * n, tokens), bf16),
            vmem((tokens, 2 * n), f32), vmem((tokens + 8, 2 * n), f32),
            vmem((columns // 128, tokens + 8, 128), f32),
            vmem((tokens, tokens), f32), vmem((tokens, tokens), f32),
            vmem((2, tokens, n), f32),
            vmem((groups, columns // 128, 8, 128), f32),
            vmem((groups, 16, columns), f32), vmem((groups, 16, 128), bf16),
            vmem((groups, 16, 128), bf16), vmem(part, f32), vmem(part, f32), vmem(part, f32),
            vmem(part, f32), vmem((2, tokens, n), bf16), vmem((2, heads, tokens, n), bf16),
            vmem((2, heads, 16, n), bf16), vmem((tokens + 8, 2 * n), f32),
            vmem((8, n), f32), vmem((peers, 8, n), f32),
            dma((groups,)), dma((groups,)), dma((5,)), dma((groups + 1,)), dma((groups + 1,)),
            dma((2 * groups,)), dma((2 * groups,)), dma((2 * groups,)), dma((2 * groups,)),
            dma((groups,)), dma((groups,)), dma((groups + 1,)), dma((groups + 1,)),
            dma((groups + 1,)), dma((groups + 1,)), dma((groups + 1, seq * cores)),
            dma((groups + 1,)),
            dma((2, heads)), dma((2, heads)), dma((2, heads)), dma((2, heads)),
            dma((peers,)), dma((peers,)),
        ],
        compiler_params=pltpu.CompilerParams(
            vmem_limit_bytes=44 * 1024 * 1024, collective_id=0, has_side_effects=True,
        ),
        name="main",
    )(*(held(a, pltpu.HBM) for a in (x, bc, d, conv_x, conv_bc, skip_gain, g)))

    pieces = 4
    y, gx, gbc, taps_x, taps_bc, skips = pl.pallas_call(
        functools.partial(final_kernel, head_dim, norm, pieces),
        in_specs=[inside] * 5,
        out_specs=[anywhere] * 6,
        out_shape=[
            out((tokens, channels), bf16), out((tokens, channels), bf16),
            out((tokens, 2 * n), bf16), out((taps, channels), f32), out((taps, 2 * n), f32),
            out((1, count), f32),
        ],
        scratch_shapes=[
            vmem((taps, channels), f32), vmem((taps, 2 * n), f32), vmem((1, count), f32),
            dma((3, 4)),
        ],
        compiler_params=pltpu.CompilerParams(vmem_limit_bytes=16 * 1024 * 1024),
        name="final",
    )(y, gx, gbc, sums, bsum)
    return y[None], gx[None], gbc[None], taps_x, taps_bc, skips.reshape(count)


def solution(mesh):
    return jax.shard_map(
        local,
        mesh=mesh,
        in_specs=(
            P(("groups", "dp"), "seq", "head"),
            P(("groups", "dp"), "seq", None),
            P(("groups", "dp"), "head", "seq"),
            P(None, "head"),
            P(),
            P("head"),
            P(("groups", "dp"), "seq", "head"),
        ),
        out_specs=(
            P(("groups", "dp"), "seq", "head"),
            P(("groups", "dp"), "seq", "head"),
            P(("groups", "dp"), "seq", None),
            P("groups", "head"),
            P("groups", None),
            P(("groups", "head")),
        ),
        check_vma=False,
    )
```

```python
import functools

import jax
import jax.numpy as jnp
from jax import lax
from jax.experimental import pallas as pl
from jax.experimental.pallas import tpu as pltpu
from jax.sharding import PartitionSpec as P

MESH = pl.DeviceIdType.MESH
f32 = jnp.float32
bf16 = jnp.bfloat16
STRIP = 64
LAG = 3
RIDE = 4
EARLY = 2


def dot(a, b, ca, cb):
    return lax.dot_general(a, b, (((ca,), (cb,)), ((), ())), preferred_element_type=f32)


def ones_where(mask):
    return mask.astype(f32).astype(bf16)


def iota(shape, axis):
    return lax.broadcasted_iota(jnp.int32, shape, axis)


def conv_taps(pad_ref, weight, first, tokens):
    total = weight[0:1, :] * pad_ref[pl.ds(first, tokens), :]
    for k in range(1, weight.shape[0]):
        total = total + weight[k : k + 1, :] * pad_ref[pl.ds(first + k, tokens), :]
    return total


def fold(a):
    return jnp.sum(a.reshape(a.shape[0] // 8, 8, a.shape[1]), axis=0)


def silu_parts(pre):
    sigma = 0.5 * jnp.tanh(0.5 * pre) + 0.5
    return pre * sigma, sigma * (1.0 + pre * (1.0 - sigma))


def main_kernel(
    head_dim, scale, sizes,
    x_hbm, bc_hbm, d_hbm, cw_hbm, cbc_hbm, skip_hbm, g_hbm,
    y_ref, gx_ref, gbc_ref, sums_ref, bsum_ref,
    xv, gv, bcv, dv, cwv, cbcv, skip_ref,
    in_all, ds_all, lead_all, gt_all, lg_all, tw_all, ya, da, s_all, u_all, p_all, q_all, et, fac, cum_all,
    cum_r, cum_t, halo, halo_b, mapped, mapped_t, dsbc, bp, xp, sim, dsim, dbc,
    skip_sums, tails, edges, next_x, parts, ride_in, core_in, tot, dbc_out, head_in, next_bc, dbp, bct, bct_in,
    load_x, load_g, load_small, halo_send, halo_recv, send_f, recv_f, send_b, recv_b,
    edge_send, edge_recv, ride_send, ride_recv, core_send, core_recv, tot_send, tot_recv,
    head_send, head_recv, nbc_send, nbc_recv, bct_send, bct_recv,
):
    groups, tokens, columns = xv.shape
    width = columns // head_dim
    count = groups * width
    n = mapped.shape[1] // 2
    taps = cwv.shape[0]
    first = 9 - taps
    seq, heads, cores = sizes
    peers = seq * heads * cores
    me = lax.axis_index("seq")
    back = seq - 1 - me
    hd = lax.axis_index("head")
    co = lax.axis_index("dp")
    rank = (me * heads + hd) * cores + co

    def copy(src, dst, send, recv, device):
        return pltpu.make_async_remote_copy(
            src_ref=src, dst_ref=dst, send_sem=send, recv_sem=recv, device_id=device,
            device_id_type=MESH,
        )

    def peer(o):
        at = lax.rem(rank + o, peers)
        high = at // cores
        return at, {"seq": high // heads, "head": lax.rem(high, heads), "dp": lax.rem(at, cores)}

    def lanes(c):
        return pl.ds(pl.multiple_of(c * columns, columns), columns)

    def x_load(c):
        return pltpu.make_async_copy(x_hbm.at[:, lanes(c)], xv.at[c], load_x.at[c])

    def g_load(c):
        return pltpu.make_async_copy(g_hbm.at[:, lanes(c)], gv.at[c], load_g.at[c])

    def halo_x(c):
        return copy(
            x_hbm.at[tokens - 16 : tokens, lanes(c)], halo.at[:, lanes(c)], halo_send.at[c],
            halo_recv.at[c], {"seq": me + 1},
        )

    def halo_bc():
        return copy(
            bc_hbm.at[tokens - 16 : tokens], halo_b, halo_send.at[groups], halo_recv.at[groups],
            {"seq": me + 1},
        )

    def forward(c):
        return copy(s_all.at[c], p_all.at[c], send_f.at[c], recv_f.at[c], {"seq": me + 1})

    def backward(c):
        return copy(u_all.at[c], q_all.at[c], send_b.at[c], recv_b.at[c], {"seq": me - 1})

    def edge_copy(c):
        return copy(edges.at[c], next_x.at[c], edge_send.at[c], edge_recv.at[c], {"seq": me - 1})

    def ride_copy(c):
        return copy(parts.at[c], ride_in.at[c], ride_send.at[c], ride_recv.at[c], {"seq": me - 1})

    def core_copy(c):
        return copy(
            parts.at[c], core_in.at[c], core_send.at[c], core_recv.at[c],
            {"dp": lax.rem(co + 1, cores)},
        )

    def tot_copies(c):
        return [
            copy(
                tot.at[c], tot.at[c], tot_send.at[c, z * cores + q], tot_recv.at[c],
                {"seq": z, "dp": lax.rem(co + q, cores)},
            )
            for z in range(seq)
            for q in range(cores)
            if z + q > 0
        ]

    def owner(c):
        return co == lax.rem(groups - c, cores)

    def head_copy(half, o):
        return copy(
            dbc_out.at[half], head_in.at[half, hd], head_send.at[half, o],
            head_recv.at[half, hd], {"head": lax.rem(hd + o, heads)},
        )

    def nbc_copy(half, o):
        return copy(
            dbc_out.at[half, 0:16], next_bc.at[half, hd], nbc_send.at[half, o],
            nbc_recv.at[half, hd], {"head": lax.rem(hd + o, heads), "seq": me - 1},
        )

    def bct_copy(o):
        return copy(bct, bct_in.at[rank], bct_send.at[o], bct_recv.at[rank], peer(o)[1])

    def arrived(dst, sem, source):
        copy(source, dst, sem, sem, peer(1)[1]).wait_recv()

    small = [
        pltpu.make_async_copy(src, dst, load_small.at[i])
        for i, (src, dst) in enumerate(
            ((d_hbm, dv), (bc_hbm, bcv), (cbc_hbm, cbcv), (cw_hbm, cwv), (skip_hbm, skip_ref))
        )
    ]
    for load in small:
        load.start()

    @pl.loop(0, groups)
    def _(c):
        g_load(c).start()
        x_load(c).start()

    barrier = pltpu.get_barrier_semaphore()

    @pl.loop(1, peers)
    def _(o):
        pl.semaphore_signal(barrier, inc=1, device_id=peer(o)[1], device_id_type=MESH)

    pl.semaphore_wait(barrier, peers - 1)

    @pl.when(me < seq - 1)
    def _():
        halo_bc().start()
        for c in range(groups):
            halo_x(c).start()

    @pl.when(me == 0)
    def _():
        halo_b[...] = jnp.zeros(halo_b.shape, bf16)
        halo[...] = jnp.zeros(halo.shape, bf16)

    small[0].wait()
    d = dv[...]
    rest = jnp.log(d)
    upto = ones_where(iota((tokens, tokens), 0) <= iota((tokens, tokens), 1))
    rows = jnp.zeros(d.shape, f32)
    for _ in range(3):
        piece = rest.astype(bf16)
        rest = rest - piece.astype(f32)
        rows = rows + dot(piece, upto, 1, 0)
    squared = (1.0 - d) * (1.0 + d)
    cum_all[...] = rows - 0.5 * jnp.log(squared)
    last = rows[:, tokens - 1 :]
    factors = jnp.concatenate([jnp.exp(rows), jnp.sqrt(squared) * jnp.exp(last - rows)], axis=1)
    high = factors.astype(bf16).astype(f32)
    both = jnp.concatenate([high, factors - high], axis=0).astype(bf16)
    same = ones_where(iota((2 * count, 2 * count), 0) == iota((2 * count, 2 * count), 1))
    fac[...] = dot(both, same, 0, 0).astype(bf16)

    def spread(c):
        pick = iota((2 * count, columns), 0) % count == c * width + iota(
            (2 * count, columns), 1
        ) // head_dim
        return dot(fac[...], ones_where(pick), 1, 0)

    def skip_row(c):
        lane = iota((1, columns), 1) // head_dim
        skip = jnp.zeros((1, columns), f32)
        for j in range(width):
            skip = jnp.where(lane == j, skip_ref[c * width + j], skip)
        return skip

    tiles = [slice(j * 128, (j + 1) * 128) for j in range(columns // 128)]
    strips = [slice(r, r + STRIP) for r in range(0, tokens, STRIP)]
    part = columns // 2

    def phase_u(c):
        factor = spread(c)
        lead_all[c] = factor[:tokens].astype(bf16)
        gt_all[c] = factor[tokens:].astype(bf16)
        for e in range(2):
            et[2 * c + e] = factor[tokens - 1 : tokens, e * part : (e + 1) * part]
        for tile in tiles:
            for rows in strips:
                lg_all[c, rows, tile] = gv[c, rows, tile] * lead_all[c, rows, tile]

    def send_u(c, to):
        grown = dot(mapped_t[n:, :], lg_all[c], 1, 0).astype(bf16)
        for e in range(2):
            u_all[2 * to + e] = grown[:, e * part : (e + 1) * part]

    def phase_a(c):
        x_load(c).wait()

        @pl.when(me > 0)
        def _():
            halo_x(c).wait_recv()

        @pl.when(c < groups - 1)
        def _():
            g_load(c + 1).wait()

        after = lax.min(c + 1, groups - 1)
        phase_u(after)
        old = halo[:, lanes(c)].astype(f32)[8:]
        weight = cwv[:, lanes(c)]
        for j, tile in enumerate(tiles):
            xp[j, 0:8] = old[:, tile]
            xp[j, 8:] = xv[c, :, tile].astype(f32)
        for j, tile in enumerate(tiles):
            skipped = jnp.zeros((8, 128), f32)
            for rows in strips:
                pre = weight[0:1, tile] * xp[j, pl.ds(first + rows.start, STRIP)]
                for k in range(1, taps):
                    pre = pre + weight[k : k + 1, tile] * xp[j, pl.ds(first + k + rows.start, STRIP)]
                value, slope = silu_parts(pre)
                inner = value.astype(bf16)
                in_all[c, rows, tile] = inner
                ds_all[c, rows, tile] = slope.astype(bf16)
                tw_all[c, rows, tile] = inner * gt_all[c, rows, tile]
                skipped = skipped + fold(gv[c, rows, tile].astype(f32) * inner.astype(f32))
            skip_sums[c, j] = skipped
        state = dot(mapped_t[:n, :], tw_all[c], 1, 0).astype(bf16)
        send_u(after, c + 1)
        for e in range(2):
            s_all[2 * c + e] = state[:, e * part : (e + 1) * part]

    def advance(c, hops, make, own, incoming):
        @pl.when(hops == 0)
        def _():
            incoming[c] = jnp.zeros(incoming.shape[1:], bf16)

        @pl.when(hops > 0)
        def _():
            make(c).wait_recv()

            @pl.when(hops < seq - 1)
            def _():
                own[c] = (incoming[c].astype(f32) * et[c] + own[c].astype(f32)).astype(bf16)

        @pl.when(hops < seq - 1)
        def _():
            make(c).start()

    def setup_b():
        turned = jnp.zeros((tokens, count), f32)
        rest = jnp.log(dv[...])
        upto = ones_where(iota((tokens, tokens), 0) <= iota((tokens, tokens), 1))
        for _ in range(3):
            piece = rest.astype(bf16)
            rest = rest - piece.astype(f32)
            turned = turned + dot(upto, piece, 0, 1)
        for c in range(groups):
            cum_t[c] = turned[:, c * width : (c + 1) * width]
            cum_r[c] = cum_all[c * width : (c + 1) * width, :]
        sim[...] = dot(mapped[:, n:], mapped[:, :n], 1, 1)
        dsim[...] = jnp.zeros_like(dsim)
        dbc[...] = jnp.zeros_like(dbc)
        count_tiles = groups * len(tiles)
        rest = jnp.sum(skip_sums[...].reshape(count_tiles, 8, 128), axis=1)
        pick = ones_where(iota((8, 128), 1) // head_dim == iota((8, 128), 0))
        found = jnp.zeros((8, count_tiles), f32)
        for _ in range(3):
            piece = rest.astype(bf16)
            rest = rest - piece.astype(f32)
            found = found + dot(pick, piece, 1, 1)
        parts[groups] = jnp.zeros(parts.shape[1:], f32)
        parts[groups, :, 0:count_tiles] = found
        share(groups)

    def phase_b(c):
        mid = tokens // 2
        lower = iota((mid, mid), 0) >= iota((mid, mid), 1)
        empty = jnp.zeros((mid, mid), bf16)
        pair = 2 * head_dim
        side = iota((1, pair), 1) < head_dim
        g_t = gv[c].T
        corners = None
        turned = []
        for j in range(width // 2):
            cols = slice(j * pair, (j + 1) * pair)
            in_pair = in_all[c, :, cols]
            g_pair = gv[c, :, cols]
            found = []
            for e in range(2):
                h = 2 * j + e
                mine = side if e == 0 else jnp.logical_not(side)
                near = dot(jnp.where(mine, g_pair, jnp.zeros_like(g_pair)), in_pair, 1, 1)
                at = cum_t[c, :, h : h + 1]
                to = cum_r[c, h : h + 1, :]
                top = jnp.exp(jnp.where(lower, at[:mid] - to[:, :mid], -1e30))
                left = jnp.exp(at[mid:] - to[:, :mid])
                low = jnp.exp(jnp.where(lower, at[mid:] - to[:, mid:], -1e30))
                mix = jnp.concatenate(
                    [
                        jnp.concatenate([(top * sim[:mid, :mid]).astype(bf16), empty], axis=1),
                        jnp.concatenate(
                            [
                                (left * sim[mid:, :mid]).astype(bf16),
                                (low * sim[mid:, mid:]).astype(bf16),
                            ],
                            axis=1,
                        ),
                    ],
                    axis=0,
                )
                terms = [top * near[:mid, :mid], left * near[mid:, :mid], low * near[mid:, mid:]]
                corners = terms if corners is None else [a + b for a, b in zip(corners, terms)]
                found.append(dot(mix, in_pair, 1, 0))
                turned.append(dot(g_t[h * head_dim : (h + 1) * head_dim], mix, 1, 0))
            ya[c, :, cols] = jnp.where(side, found[0], found[1])
        dsim[:mid, :mid] += corners[0]
        dsim[mid:, :mid] += corners[1]
        dsim[mid:, mid:] += corners[2]
        da[c] = jnp.concatenate(turned, axis=0).T

    def phase_p(c):
        skip = skip_row(c)
        for e in range(2):
            p = p_all[2 * c + e]
            cols = slice(e * part, (e + 1) * part)
            seen = dot(mapped[:, n:], p, 1, 0)
            lead = lead_all[c, :, cols].astype(f32)
            y = scale * (ya[c, :, cols] + lead * seen)
            y = (y + skip[:, cols] * in_all[c, :, cols].astype(f32)).astype(bf16)
            y_ref[:, pl.ds(pl.multiple_of(c * columns + e * part, part), part)] = y
            dbc[1] += dot(lg_all[c, :, cols], p, 1, 1)

    def phase_q(c):
        skip = skip_row(c)
        weight = cwv[:, lanes(c)]
        old = halo[:, lanes(c)].astype(f32)
        heads_of = []
        for e in range(2):
            q = q_all[2 * c + e]
            cols = slice(e * part, (e + 1) * part)
            seen = dot(mapped[:, :n], q, 1, 0)
            dbc[0] += dot(tw_all[c, :, cols], q, 1, 1)
            for j in range(e * part // 128, (e + 1) * part // 128):
                tile = tiles[j]
                own = slice(j * 128 - e * part, (j + 1) * 128 - e * part)
                for rows in strips:
                    g = gv[c, rows, tile].astype(f32)
                    d_w = scale * (da[c, rows, tile] + gt_all[c, rows, tile].astype(f32) * seen[rows, own])
                    d_pre = (d_w + skip[:, tile] * g) * ds_all[c, rows, tile].astype(f32)
                    xp[j, rows] = d_pre
                xp[j, tokens:] = jnp.zeros((8, 128), f32)
                edge = xp[j, 0:8]
                heads_of.append(edge[0 : taps - 1])
                sums = [jnp.zeros((8, 128), f32) for _ in range(taps)]
                for rows in strips:
                    x = xv[c, rows, tile].astype(f32)
                    total = jnp.zeros((STRIP, 128), f32)
                    for k in range(taps):
                        moved = xp[j, pl.ds(taps - 1 - k + rows.start, STRIP)]
                        total = total + weight[k : k + 1, tile] * moved
                        sums[k] = sums[k] + fold(x * moved)
                    at = pl.ds(pl.multiple_of(c * columns + j * 128, 128), 128)
                    gx_ref[rows, at] = total.astype(bf16)
                    if rows.stop == tokens:
                        tails[c, :, tile] = total[STRIP - 16 :]
                for k in range(taps):
                    found = jnp.sum(sums[k], axis=0, keepdims=True)
                    for t in range(taps - 1 - k):
                        at = 16 - (taps - 1 - k) + t
                        found = found + old[at : at + 1, tile] * edge[t : t + 1]
                    row = (j % 2) * taps + k
                    parts[c, row : row + 1, j // 2 * 128 : (j // 2 + 1) * 128] = found

        heads_of.append(jnp.zeros((16 - len(tiles) * (taps - 1), 128), f32))
        edges[c] = jnp.concatenate(heads_of, axis=0).astype(bf16)

        @pl.when(me > 0)
        def _():
            edge_copy(c).start()

        share(c)

    def share(c):
        @pl.when(jnp.logical_not(owner(c)))
        def _():
            core_copy(c).start()

    def ride(c):
        @pl.when(owner(c))
        def _():
            arrived(core_in.at[c], core_recv.at[c], parts.at[c])
            parts[c] = parts[c] + core_in[c]

            @pl.when(me < seq - 1)
            def _():
                ride_copy(c).wait_recv()
                parts[c] = parts[c] + ride_in[c]

            @pl.when(me > 0)
            def _():
                ride_copy(c).start()

            @pl.when(me == 0)
            def _():
                tot[c] = parts[c]
                for move in tot_copies(c):
                    move.start()

    def finish(half):
        other = mapped[:, n:] if half == 0 else mapped[:, :n]
        side = 0 if half == 0 else 1
        cols = slice(half * n, (half + 1) * n)
        whole = dbc[half] + dot(dsim[...].astype(bf16), other, side, 0)
        whole = scale * whole * dsbc[:, cols]
        dbc_out[half] = whole.astype(bf16)
        for o in range(1, heads):
            head_copy(half, o).start()

        @pl.when(me > 0)
        def _():
            for o in range(heads):
                nbc_copy(half, o).start()

        head_in[half, hd] = dbc_out[half]
        for k in range(taps):
            bct[half * taps + k : half * taps + k + 1, :] = jnp.sum(
                whole * bp[pl.ds(first + k, tokens), cols], axis=0, keepdims=True
            )

    g_load(0).wait()
    phase_u(0)

    for load in small[1:]:
        load.wait()

    @pl.when(me > 0)
    def _():
        halo_bc().wait_recv()

    bp[0:8, :] = halo_b[...].astype(f32)[8:]
    bp[8:, :] = bcv[...].astype(f32)
    value, slope = silu_parts(conv_taps(bp, cbcv[...], first, tokens))
    mapped[...] = value.astype(bf16)
    dsbc[...] = slope
    unit = ones_where(iota((tokens, tokens), 0) == iota((tokens, tokens), 1))
    mapped_t[...] = dot(mapped[...], unit, 0, 0).astype(bf16)
    send_u(0, 0)

    @pl.when(back == 0)
    def _():
        for e in range(2):
            advance(e, back, backward, u_all, q_all)

    halves = 2 * groups
    shift = groups - 3 - LAG

    def due(s, base, hops):
        gap = lax.min(hops, 1) * (shift + 2 + LAG * hops)
        c = lax.min(s - base, (s - gap + 4096) // 2 - 2048)
        return c, (c >= 0) & (c < groups) & (lax.max(base + c, 2 * c + gap) == s)

    slots = halves + groups + max(LAG * (seq - 2), RIDE * (seq - 1) - 2)

    both = lax.max(halves + groups - 1, halves + shift + LAG * lax.max(me, back))

    @pl.loop(0, slots)
    def _(s):
        @pl.when(s < groups)
        def _():
            phase_a(s)

        @pl.when((s < groups) & (me == 0))
        def _():
            for e in range(2):
                advance(2 * s + e, me, forward, s_all, p_all)

        @pl.when((s < groups - 1) & (back == 0))
        def _():
            for e in range(2):
                advance(2 * s + 2 + e, back, backward, u_all, q_all)

        @pl.when(s == groups - 1)
        def _():
            setup_b()

        @pl.when((s >= groups) & (s < halves))
        def _():
            phase_b(s - groups)

        cq, has_q = due(s, groups + groups * lax.min(back, 1), back)
        cr, has_r = due(s, groups + 1 + lax.min(back, 1) * (groups - 3 + RIDE * back) - EARLY * lax.max(1 - me, 0), back)
        cp, has_p = due(s, halves, me)

        @pl.when(has_q)
        def _():
            phase_q(cq)

        hf = s - shift - LAG * me
        hb = s - shift + 1 - LAG * back

        @pl.when((me > 0) & (hf >= 0) & (hf < halves))
        def _():
            advance(hf, me, forward, s_all, p_all)

        @pl.when((back > 0) & (hb >= 0) & (hb < halves))
        def _():
            advance(hb, back, backward, u_all, q_all)

        @pl.when(has_q & (cq == groups - 1))
        def _():
            finish(0)

        @pl.when(has_p)
        def _():
            phase_p(cp)

            @pl.when(cp == groups - 1)
            def _():
                finish(1)

        @pl.when(s == both)
        def _():
            bct_in[rank] = bct[...]

            @pl.loop(1, peers)
            def _(o):
                bct_copy(o).start()

        @pl.when(s == groups + 1 + RIDE * back)
        def _():
            ride(groups)

        @pl.when(has_r)
        def _():
            ride(cr)


    @pl.when(me < seq - 1)
    def _():
        at = iota((16, 1), 0)
        for c in range(groups):
            edge_copy(c).wait_recv()
            after = next_x[c].astype(f32)
            for j, tile in enumerate(tiles):
                fixed = tails[c, :, tile]
                lo = c * columns + j * 128
                for r in range(taps - 1):
                    row = jnp.zeros((1, 128), f32)
                    for k in range(r + 1):
                        e = j * (taps - 1) + r - k
                        row = row + cwv[k : k + 1, lo : lo + 128] * after[e : e + 1]
                    fixed = fixed + jnp.where(at == 16 - (taps - 1) + r, row, 0.0)
                gx_ref[tokens - 16 :, lo : lo + 128] = fixed.astype(bf16)

    for half in range(2):
        for o in range(1, heads):
            at = lax.rem(hd + o, heads)
            arrived(head_in.at[half, at], head_recv.at[half, at], dbc_out.at[half])
        cols = slice(half * n, (half + 1) * n)
        full = head_in[half, 0].astype(f32)
        for h in range(1, heads):
            full = full + head_in[half, h].astype(f32)
        dbp[0:tokens, cols] = full

        @pl.when(me == seq - 1)
        def _():
            dbp[tokens:, cols] = jnp.zeros((8, n), f32)

        @pl.when(me < seq - 1)
        def _():
            for h in range(heads):
                arrived(next_bc.at[half, h], nbc_recv.at[half, h], dbc_out.at[half, 0:16])
            rows = next_bc[half, 0].astype(f32)
            for h in range(1, heads):
                rows = rows + next_bc[half, h].astype(f32)
            dbp[tokens:, cols] = rows[0:8]

    grad = jnp.zeros((tokens, 2 * n), f32)
    for k in range(taps):
        grad = grad + cbcv[k : k + 1, :] * dbp[pl.ds(taps - 1 - k, tokens), :]
    gbc_ref[...] = grad.astype(bf16)

    @pl.loop(1, peers)
    def _(o):
        at = lax.rem(rank + o, peers)
        arrived(bct_in.at[at], bct_recv.at[at], bct)

    bsum = bct_in[0]
    for i in range(1, peers):
        bsum = bsum + bct_in[i]
    bsum_ref[...] = bsum

    @pl.loop(0, groups + 1)
    def _(c):
        @pl.when(jnp.logical_not(owner(c) & (me == 0)))
        def _():
            arrived(tot.at[c], tot_recv.at[c], tot.at[c])

    sums_ref[...] = tot[...]

    for half in range(2):
        for o in range(1, heads):
            head_copy(half, o).wait_send()

    @pl.loop(1, peers)
    def _(o):
        bct_copy(o).wait_send()

    @pl.when(me < seq - 1)
    def _():
        halo_bc().wait_send()
        for c in range(groups):
            halo_x(c).wait_send()

        @pl.loop(0, halves)
        def _(h):
            forward(h).wait_send()

    @pl.when(me > 0)
    def _():
        for half in range(2):
            for o in range(heads):
                nbc_copy(half, o).wait_send()

        @pl.loop(0, halves)
        def _(h):
            backward(h).wait_send()

        @pl.loop(0, groups)
        def _(c):
            edge_copy(c).wait_send()

    @pl.loop(0, groups + 1)
    def _(c):
        @pl.when(jnp.logical_not(owner(c)))
        def _():
            core_copy(c).wait_send()

        @pl.when(owner(c) & (me > 0))
        def _():
            ride_copy(c).wait_send()

        @pl.when(owner(c) & (me == 0))
        def _():
            for move in tot_copies(c):
                move.wait_send()


def final_kernel(
    head_dim, norm, pieces, y_in, gx_in, gbc_in, tot, bsum, y_out, gx_out, gbc_out, sums_out, bsum_out,
    skip_out, sums, sums_bc, skips, sem,
):
    tokens = y_in.shape[0]
    groups = tot.shape[0] - 1
    columns = 2 * tot.shape[2]
    taps = sums.shape[0]
    count = skips.shape[1]
    block = tokens // pieces
    moves = []
    for i in range(pieces):
        at = pl.ds(i * block, block)
        moves.append(pltpu.make_async_copy(y_in.at[at], y_out.at[at], sem.at[0, i]))
        moves.append(pltpu.make_async_copy(gx_in.at[at], gx_out.at[at], sem.at[1, i]))
    moves.append(pltpu.make_async_copy(gbc_in, gbc_out, sem.at[2, 0]))
    for move in moves:
        move.start()
    tiles = columns // 128
    for c in range(groups):
        for j in range(tiles):
            lo = c * columns + j * 128
            row = (j % 2) * taps
            sums[:, lo : lo + 128] = norm * tot[
                c, row : row + taps, j // 2 * 128 : (j // 2 + 1) * 128
            ]
    rest = tot[groups, :, 0 : groups * tiles]
    near = 128 // head_dim
    pick = ones_where(
        iota((groups * tiles, count), 0) == iota((groups * tiles, count), 1) // near
    )
    found = jnp.zeros((8, count), f32)
    for _ in range(3):
        piece = rest.astype(bf16)
        rest = rest - piece.astype(f32)
        found = found + dot(piece, pick, 1, 0)
    own = iota((8, count), 1) % near == iota((8, count), 0)
    skips[...] = jnp.sum(jnp.where(own, found, 0.0), axis=0, keepdims=True) * (
        norm * float(head_dim) ** (-0.5)
    )
    half = bsum.shape[1]
    sums_bc[:, :half] = bsum[0:taps] * norm
    sums_bc[:, half:] = bsum[taps:] * norm
    late = [
        pltpu.make_async_copy(src, dst, sem.at[2, i + 1])
        for i, (src, dst) in enumerate(((sums, sums_out), (sums_bc, bsum_out), (skips, skip_out)))
    ]
    for move in late:
        move.start()
    for move in moves + late:
        move.wait()


def local(x_input, bc_input, decays, conv_x, conv_bc, skip_gain, grad_out):
    x = x_input[0]
    bc = bc_input[0]
    d = decays[0]
    g = grad_out[0]
    tokens, channels = x.shape
    taps = conv_x.shape[0]
    count = d.shape[0]
    head_dim = channels // count
    n = bc.shape[1] // 2
    scale = float(n) ** (-0.5)
    seq = lax.axis_size("seq")
    heads = lax.axis_size("head")
    cores = lax.axis_size("dp")
    peers = seq * heads * cores
    width = next(k for k in (8, 4) if count % k == 0)
    groups = count // width
    columns = width * head_dim
    norm = float(tokens * seq * cores) ** (-0.5)
    sizes = (seq, heads, cores)

    held = pltpu.with_memory_space_constraint

    def out(shape, dtype):
        return jax.ShapeDtypeStruct(shape, dtype)

    dma = pltpu.SemaphoreType.DMA
    vmem = pltpu.VMEM
    anywhere = pl.BlockSpec(memory_space=pl.ANY)
    inside = pl.BlockSpec(memory_space=vmem)
    wide = (groups, tokens, columns)
    state = (2 * groups, n, columns // 2)
    part = (groups + 1, 8, columns // 2)
    y, gx, gbc, sums, bsum = pl.pallas_call(
        functools.partial(main_kernel, head_dim, scale, sizes),
        in_specs=[anywhere] * 7,
        out_specs=[inside] * 5,
        out_shape=[
            vmem((tokens, channels), bf16), vmem((tokens, channels), bf16),
            vmem((tokens, 2 * n), bf16), vmem(part, f32), vmem((8, n), f32),
        ],
        scratch_shapes=[
            vmem(wide, bf16), vmem(wide, bf16), vmem((tokens, 2 * n), bf16),
            vmem((count, tokens), f32), vmem((taps, channels), f32), vmem((taps, 2 * n), f32), pltpu.SMEM((count,), f32),
            vmem(wide, bf16), vmem(wide, bf16), vmem(wide, bf16), vmem(wide, bf16),
            vmem(wide, bf16), vmem(wide, bf16), vmem(wide, f32), vmem(wide, f32),
            vmem(state, bf16), vmem((2 * groups + 2, n, columns // 2), bf16), vmem(state, bf16),
            vmem(state, bf16),
            vmem((2 * groups, 1, columns // 2), f32), vmem((2 * tokens, 2 * count), bf16),
            vmem((count, tokens), f32),
            vmem((groups, width, tokens), f32), vmem((groups, tokens, width), f32),
            vmem((16, channels), bf16), vmem((16, 2 * n), bf16),
            vmem((tokens, 2 * n), bf16), vmem((2 * n, tokens), bf16),
            vmem((tokens, 2 * n), f32), vmem((tokens + 8, 2 * n), f32),
            vmem((columns // 128, tokens + 8, 128), f32),
            vmem((tokens, tokens), f32), vmem((tokens, tokens), f32),
            vmem((2, tokens, n), f32),
            vmem((groups, columns // 128, 8, 128), f32),
            vmem((groups, 16, columns), f32), vmem((groups, 16, 128), bf16),
            vmem((groups, 16, 128), bf16), vmem(part, f32), vmem(part, f32), vmem(part, f32),
            vmem(part, f32), vmem((2, tokens, n), bf16), vmem((2, heads, tokens, n), bf16),
            vmem((2, heads, 16, n), bf16), vmem((tokens + 8, 2 * n), f32),
            vmem((8, n), f32), vmem((peers, 8, n), f32),
            dma((groups,)), dma((groups,)), dma((5,)), dma((groups + 1,)), dma((groups + 1,)),
            dma((2 * groups,)), dma((2 * groups,)), dma((2 * groups,)), dma((2 * groups,)),
            dma((groups,)), dma((groups,)), dma((groups + 1,)), dma((groups + 1,)),
            dma((groups + 1,)), dma((groups + 1,)), dma((groups + 1, seq * cores)),
            dma((groups + 1,)),
            dma((2, heads)), dma((2, heads)), dma((2, heads)), dma((2, heads)),
            dma((peers,)), dma((peers,)),
        ],
        compiler_params=pltpu.CompilerParams(
            vmem_limit_bytes=44 * 1024 * 1024, collective_id=0, has_side_effects=True,
        ),
        name="main",
    )(*(held(a, pltpu.HBM) for a in (x, bc, d, conv_x, conv_bc, skip_gain, g)))

    pieces = 4
    y, gx, gbc, taps_x, taps_bc, skips = pl.pallas_call(
        functools.partial(final_kernel, head_dim, norm, pieces),
        in_specs=[inside] * 5,
        out_specs=[anywhere] * 6,
        out_shape=[
            out((tokens, channels), bf16), out((tokens, channels), bf16),
            out((tokens, 2 * n), bf16), out((taps, channels), f32), out((taps, 2 * n), f32),
            out((1, count), f32),
        ],
        scratch_shapes=[
            vmem((taps, channels), f32), vmem((taps, 2 * n), f32), vmem((1, count), f32),
            dma((3, 4)),
        ],
        compiler_params=pltpu.CompilerParams(vmem_limit_bytes=16 * 1024 * 1024),
        name="final",
    )(y, gx, gbc, sums, bsum)
    return y[None], gx[None], gbc[None], taps_x, taps_bc, skips.reshape(count)


def solution(mesh):
    return jax.shard_map(
        local,
        mesh=mesh,
        in_specs=(
            P(("groups", "dp"), "seq", "head"),
            P(("groups", "dp"), "seq", None),
            P(("groups", "dp"), "head", "seq"),
            P(None, "head"),
            P(),
            P("head"),
            P(("groups", "dp"), "seq", "head"),
        ),
        out_specs=(
            P(("groups", "dp"), "seq", "head"),
            P(("groups", "dp"), "seq", "head"),
            P(("groups", "dp"), "seq", None),
            P("groups", "head"),
            P("groups", None),
            P(("groups", "head")),
        ),
        check_vma=False,
    )
```

```python
import functools

import jax
import jax.numpy as jnp
from jax import lax
from jax.experimental import pallas as pl
from jax.experimental.pallas import tpu as pltpu
from jax.sharding import PartitionSpec as P

MESH = pl.DeviceIdType.MESH
f32 = jnp.float32
bf16 = jnp.bfloat16
STRIP = 64
LAG = 3
RIDE = 5
EARLY = 3


def dot(a, b, ca, cb):
    return lax.dot_general(a, b, (((ca,), (cb,)), ((), ())), preferred_element_type=f32)


def ones_where(mask):
    return mask.astype(f32).astype(bf16)


def iota(shape, axis):
    return lax.broadcasted_iota(jnp.int32, shape, axis)


def conv_taps(pad_ref, weight, first, tokens):
    total = weight[0:1, :] * pad_ref[pl.ds(first, tokens), :]
    for k in range(1, weight.shape[0]):
        total = total + weight[k : k + 1, :] * pad_ref[pl.ds(first + k, tokens), :]
    return total


def fold(a):
    return jnp.sum(a.reshape(a.shape[0] // 8, 8, a.shape[1]), axis=0)


def silu_parts(pre):
    sigma = 0.5 * jnp.tanh(0.5 * pre) + 0.5
    return pre * sigma, sigma * (1.0 + pre * (1.0 - sigma))


def main_kernel(
    head_dim, scale, sizes,
    x_hbm, bc_hbm, d_hbm, cw_hbm, cbc_hbm, skip_hbm, g_hbm,
    y_ref, gx_ref, gbc_ref, sums_ref, bsum_ref,
    xv, gv, bcv, dv, cwv, cbcv, skip_ref,
    in_all, ds_all, lead_all, gt_all, lg_all, tw_all, ya, da, s_all, u_all, p_all, q_all, et, fac, cum_all,
    cum_r, cum_t, halo, halo_b, mapped, mapped_t, dsbc, bp, xp, sim, dsim, dbc,
    skip_sums, tails, edges, next_x, parts, ride_in, core_in, tot, dbc_out, head_in, next_bc, dbp, bct, bct_in,
    load_x, load_g, load_small, halo_send, halo_recv, send_f, recv_f, send_b, recv_b,
    edge_send, edge_recv, ride_send, ride_recv, core_send, core_recv, tot_send, tot_recv,
    head_send, head_recv, nbc_send, nbc_recv, bct_send, bct_recv,
):
    groups, tokens, columns = xv.shape
    width = columns // head_dim
    count = groups * width
    n = mapped.shape[1] // 2
    taps = cwv.shape[0]
    first = 9 - taps
    seq, heads, cores = sizes
    peers = seq * heads * cores
    me = lax.axis_index("seq")
    back = seq - 1 - me
    hd = lax.axis_index("head")
    co = lax.axis_index("dp")
    rank = (me * heads + hd) * cores + co

    def copy(src, dst, send, recv, device):
        return pltpu.make_async_remote_copy(
            src_ref=src, dst_ref=dst, send_sem=send, recv_sem=recv, device_id=device,
            device_id_type=MESH,
        )

    def peer(o):
        at = lax.rem(rank + o, peers)
        high = at // cores
        return at, {"seq": high // heads, "head": lax.rem(high, heads), "dp": lax.rem(at, cores)}

    def lanes(c):
        return pl.ds(pl.multiple_of(c * columns, columns), columns)

    def x_load(c):
        return pltpu.make_async_copy(x_hbm.at[:, lanes(c)], xv.at[c], load_x.at[c])

    def g_load(c):
        return pltpu.make_async_copy(g_hbm.at[:, lanes(c)], gv.at[c], load_g.at[c])

    def halo_x(c):
        return copy(
            x_hbm.at[tokens - 16 : tokens, lanes(c)], halo.at[:, lanes(c)], halo_send.at[c],
            halo_recv.at[c], {"seq": me + 1},
        )

    def halo_bc():
        return copy(
            bc_hbm.at[tokens - 16 : tokens], halo_b, halo_send.at[groups], halo_recv.at[groups],
            {"seq": me + 1},
        )

    def forward(c):
        return copy(s_all.at[c], p_all.at[c], send_f.at[c], recv_f.at[c], {"seq": me + 1})

    def backward(c):
        return copy(u_all.at[c], q_all.at[c], send_b.at[c], recv_b.at[c], {"seq": me - 1})

    def edge_copy(c):
        return copy(edges.at[c], next_x.at[c], edge_send.at[c], edge_recv.at[c], {"seq": me - 1})

    def ride_copy(c):
        return copy(parts.at[c], ride_in.at[c], ride_send.at[c], ride_recv.at[c], {"seq": me - 1})

    def core_copy(c):
        return copy(
            parts.at[c], core_in.at[c], core_send.at[c], core_recv.at[c],
            {"dp": lax.rem(co + 1, cores)},
        )

    def tot_copies(c):
        return [
            copy(
                tot.at[c], tot.at[c], tot_send.at[c, z * cores + q], tot_recv.at[c],
                {"seq": z, "dp": lax.rem(co + q, cores)},
            )
            for z in range(seq)
            for q in range(cores)
            if z + q > 0
        ]

    def owner(c):
        return co == lax.rem(groups - c, cores)

    def head_copy(half, o):
        return copy(
            dbc_out.at[half], head_in.at[half, hd], head_send.at[half, o],
            head_recv.at[half, hd], {"head": lax.rem(hd + o, heads)},
        )

    def nbc_copy(half, o):
        return copy(
            dbc_out.at[half, 0:16], next_bc.at[half, hd], nbc_send.at[half, o],
            nbc_recv.at[half, hd], {"head": lax.rem(hd + o, heads), "seq": me - 1},
        )

    def bct_copy(o):
        return copy(bct, bct_in.at[rank], bct_send.at[o], bct_recv.at[rank], peer(o)[1])

    def arrived(dst, sem, source):
        copy(source, dst, sem, sem, peer(1)[1]).wait_recv()

    small = [
        pltpu.make_async_copy(src, dst, load_small.at[i])
        for i, (src, dst) in enumerate(
            ((d_hbm, dv), (bc_hbm, bcv), (cbc_hbm, cbcv), (cw_hbm, cwv), (skip_hbm, skip_ref))
        )
    ]
    for load in small:
        load.start()

    @pl.loop(0, groups)
    def _(c):
        g_load(c).start()
        x_load(c).start()

    barrier = pltpu.get_barrier_semaphore()

    @pl.loop(1, peers)
    def _(o):
        pl.semaphore_signal(barrier, inc=1, device_id=peer(o)[1], device_id_type=MESH)

    pl.semaphore_wait(barrier, peers - 1)

    @pl.when(me < seq - 1)
    def _():
        halo_bc().start()
        for c in range(groups):
            halo_x(c).start()

    @pl.when(me == 0)
    def _():
        halo_b[...] = jnp.zeros(halo_b.shape, bf16)
        halo[...] = jnp.zeros(halo.shape, bf16)

    small[0].wait()
    d = dv[...]
    rest = jnp.log(d)
    upto = ones_where(iota((tokens, tokens), 0) <= iota((tokens, tokens), 1))
    rows = jnp.zeros(d.shape, f32)
    for _ in range(3):
        piece = rest.astype(bf16)
        rest = rest - piece.astype(f32)
        rows = rows + dot(piece, upto, 1, 0)
    squared = (1.0 - d) * (1.0 + d)
    cum_all[...] = rows - 0.5 * jnp.log(squared)
    last = rows[:, tokens - 1 :]
    factors = jnp.concatenate([jnp.exp(rows), jnp.sqrt(squared) * jnp.exp(last - rows)], axis=1)
    high = factors.astype(bf16).astype(f32)
    both = jnp.concatenate([high, factors - high], axis=0).astype(bf16)
    same = ones_where(iota((2 * count, 2 * count), 0) == iota((2 * count, 2 * count), 1))
    fac[...] = dot(both, same, 0, 0).astype(bf16)

    def spread(c):
        pick = iota((2 * count, columns), 0) % count == c * width + iota(
            (2 * count, columns), 1
        ) // head_dim
        return dot(fac[...], ones_where(pick), 1, 0)

    def skip_row(c):
        lane = iota((1, columns), 1) // head_dim
        skip = jnp.zeros((1, columns), f32)
        for j in range(width):
            skip = jnp.where(lane == j, skip_ref[c * width + j], skip)
        return skip

    tiles = [slice(j * 128, (j + 1) * 128) for j in range(columns // 128)]
    strips = [slice(r, r + STRIP) for r in range(0, tokens, STRIP)]
    part = columns // 2

    def phase_u(c):
        factor = spread(c)
        lead_all[c] = factor[:tokens].astype(bf16)
        gt_all[c] = factor[tokens:].astype(bf16)
        for e in range(2):
            et[2 * c + e] = factor[tokens - 1 : tokens, e * part : (e + 1) * part]
        for tile in tiles:
            for rows in strips:
                lg_all[c, rows, tile] = gv[c, rows, tile] * lead_all[c, rows, tile]

    def send_u(c, to):
        grown = dot(mapped_t[n:, :], lg_all[c], 1, 0).astype(bf16)
        for e in range(2):
            u_all[2 * to + e] = grown[:, e * part : (e + 1) * part]

    def phase_a(c):
        x_load(c).wait()

        @pl.when(me > 0)
        def _():
            halo_x(c).wait_recv()

        @pl.when(c < groups - 1)
        def _():
            g_load(c + 1).wait()

        after = lax.min(c + 1, groups - 1)
        phase_u(after)
        old = halo[:, lanes(c)].astype(f32)[8:]
        weight = cwv[:, lanes(c)]
        for j, tile in enumerate(tiles):
            xp[j, 0:8] = old[:, tile]
            xp[j, 8:] = xv[c, :, tile].astype(f32)
        for j, tile in enumerate(tiles):
            skipped = jnp.zeros((8, 128), f32)
            for rows in strips:
                pre = weight[0:1, tile] * xp[j, pl.ds(first + rows.start, STRIP)]
                for k in range(1, taps):
                    pre = pre + weight[k : k + 1, tile] * xp[j, pl.ds(first + k + rows.start, STRIP)]
                value, slope = silu_parts(pre)
                inner = value.astype(bf16)
                in_all[c, rows, tile] = inner
                ds_all[c, rows, tile] = slope.astype(bf16)
                tw_all[c, rows, tile] = inner * gt_all[c, rows, tile]
                skipped = skipped + fold(gv[c, rows, tile].astype(f32) * inner.astype(f32))
            skip_sums[c, j] = skipped
        state = dot(mapped_t[:n, :], tw_all[c], 1, 0).astype(bf16)
        send_u(after, c + 1)
        for e in range(2):
            s_all[2 * c + e] = state[:, e * part : (e + 1) * part]

    def advance(c, hops, make, own, incoming):
        @pl.when(hops == 0)
        def _():
            incoming[c] = jnp.zeros(incoming.shape[1:], bf16)

        @pl.when(hops > 0)
        def _():
            make(c).wait_recv()

            @pl.when(hops < seq - 1)
            def _():
                own[c] = (incoming[c].astype(f32) * et[c] + own[c].astype(f32)).astype(bf16)

        @pl.when(hops < seq - 1)
        def _():
            make(c).start()

    def setup_b():
        turned = jnp.zeros((tokens, count), f32)
        rest = jnp.log(dv[...])
        upto = ones_where(iota((tokens, tokens), 0) <= iota((tokens, tokens), 1))
        for _ in range(3):
            piece = rest.astype(bf16)
            rest = rest - piece.astype(f32)
            turned = turned + dot(upto, piece, 0, 1)
        for c in range(groups):
            cum_t[c] = turned[:, c * width : (c + 1) * width]
            cum_r[c] = cum_all[c * width : (c + 1) * width, :]
        sim[...] = dot(mapped[:, n:], mapped[:, :n], 1, 1)
        dsim[...] = jnp.zeros_like(dsim)
        dbc[...] = jnp.zeros_like(dbc)
        count_tiles = groups * len(tiles)
        rest = jnp.sum(skip_sums[...].reshape(count_tiles, 8, 128), axis=1)
        pick = ones_where(iota((8, 128), 1) // head_dim == iota((8, 128), 0))
        found = jnp.zeros((8, count_tiles), f32)
        for _ in range(3):
            piece = rest.astype(bf16)
            rest = rest - piece.astype(f32)
            found = found + dot(pick, piece, 1, 1)
        parts[groups] = jnp.zeros(parts.shape[1:], f32)
        parts[groups, :, 0:count_tiles] = found
        share(groups)

    def phase_b(c):
        mid = tokens // 2
        lower = iota((mid, mid), 0) >= iota((mid, mid), 1)
        empty = jnp.zeros((mid, mid), bf16)
        pair = 2 * head_dim
        side = iota((1, pair), 1) < head_dim
        g_t = gv[c].T
        corners = None
        turned = []
        for j in range(width // 2):
            cols = slice(j * pair, (j + 1) * pair)
            in_pair = in_all[c, :, cols]
            g_pair = gv[c, :, cols]
            found = []
            for e in range(2):
                h = 2 * j + e
                mine = side if e == 0 else jnp.logical_not(side)
                near = dot(jnp.where(mine, g_pair, jnp.zeros_like(g_pair)), in_pair, 1, 1)
                at = cum_t[c, :, h : h + 1]
                to = cum_r[c, h : h + 1, :]
                top = jnp.exp(jnp.where(lower, at[:mid] - to[:, :mid], -1e30))
                left = jnp.exp(at[mid:] - to[:, :mid])
                low = jnp.exp(jnp.where(lower, at[mid:] - to[:, mid:], -1e30))
                mix = jnp.concatenate(
                    [
                        jnp.concatenate([(top * sim[:mid, :mid]).astype(bf16), empty], axis=1),
                        jnp.concatenate(
                            [
                                (left * sim[mid:, :mid]).astype(bf16),
                                (low * sim[mid:, mid:]).astype(bf16),
                            ],
                            axis=1,
                        ),
                    ],
                    axis=0,
                )
                terms = [top * near[:mid, :mid], left * near[mid:, :mid], low * near[mid:, mid:]]
                corners = terms if corners is None else [a + b for a, b in zip(corners, terms)]
                found.append(dot(mix, in_pair, 1, 0))
                turned.append(dot(g_t[h * head_dim : (h + 1) * head_dim], mix, 1, 0))
            ya[c, :, cols] = jnp.where(side, found[0], found[1])
        dsim[:mid, :mid] += corners[0]
        dsim[mid:, :mid] += corners[1]
        dsim[mid:, mid:] += corners[2]
        da[c] = jnp.concatenate(turned, axis=0).T

    def phase_p(c):
        skip = skip_row(c)
        for e in range(2):
            p = p_all[2 * c + e]
            cols = slice(e * part, (e + 1) * part)
            seen = dot(mapped[:, n:], p, 1, 0)
            lead = lead_all[c, :, cols].astype(f32)
            y = scale * (ya[c, :, cols] + lead * seen)
            y = (y + skip[:, cols] * in_all[c, :, cols].astype(f32)).astype(bf16)
            y_ref[:, pl.ds(pl.multiple_of(c * columns + e * part, part), part)] = y
            dbc[1] += dot(lg_all[c, :, cols], p, 1, 1)

    def phase_q(c):
        skip = skip_row(c)
        weight = cwv[:, lanes(c)]
        old = halo[:, lanes(c)].astype(f32)
        heads_of = []
        for e in range(2):
            q = q_all[2 * c + e]
            cols = slice(e * part, (e + 1) * part)
            seen = dot(mapped[:, :n], q, 1, 0)
            dbc[0] += dot(tw_all[c, :, cols], q, 1, 1)
            for j in range(e * part // 128, (e + 1) * part // 128):
                tile = tiles[j]
                own = slice(j * 128 - e * part, (j + 1) * 128 - e * part)
                for rows in strips:
                    g = gv[c, rows, tile].astype(f32)
                    d_w = scale * (da[c, rows, tile] + gt_all[c, rows, tile].astype(f32) * seen[rows, own])
                    d_pre = (d_w + skip[:, tile] * g) * ds_all[c, rows, tile].astype(f32)
                    xp[j, rows] = d_pre
                xp[j, tokens:] = jnp.zeros((8, 128), f32)
                edge = xp[j, 0:8]
                heads_of.append(edge[0 : taps - 1])
                sums = [jnp.zeros((8, 128), f32) for _ in range(taps)]
                for rows in strips:
                    x = xv[c, rows, tile].astype(f32)
                    total = jnp.zeros((STRIP, 128), f32)
                    for k in range(taps):
                        moved = xp[j, pl.ds(taps - 1 - k + rows.start, STRIP)]
                        total = total + weight[k : k + 1, tile] * moved
                        sums[k] = sums[k] + fold(x * moved)
                    at = pl.ds(pl.multiple_of(c * columns + j * 128, 128), 128)
                    gx_ref[rows, at] = total.astype(bf16)
                    if rows.stop == tokens:
                        tails[c, :, tile] = total[STRIP - 16 :]
                for k in range(taps):
                    found = jnp.sum(sums[k], axis=0, keepdims=True)
                    for t in range(taps - 1 - k):
                        at = 16 - (taps - 1 - k) + t
                        found = found + old[at : at + 1, tile] * edge[t : t + 1]
                    row = (j % 2) * taps + k
                    parts[c, row : row + 1, j // 2 * 128 : (j // 2 + 1) * 128] = found

        heads_of.append(jnp.zeros((16 - len(tiles) * (taps - 1), 128), f32))
        edges[c] = jnp.concatenate(heads_of, axis=0).astype(bf16)

        @pl.when(me > 0)
        def _():
            edge_copy(c).start()

        share(c)

    def share(c):
        @pl.when(jnp.logical_not(owner(c)))
        def _():
            core_copy(c).start()

    def ride(c):
        @pl.when(owner(c))
        def _():
            arrived(core_in.at[c], core_recv.at[c], parts.at[c])
            parts[c] = parts[c] + core_in[c]

            @pl.when(me < seq - 1)
            def _():
                ride_copy(c).wait_recv()
                parts[c] = parts[c] + ride_in[c]

            @pl.when(me > 0)
            def _():
                ride_copy(c).start()

            @pl.when(me == 0)
            def _():
                tot[c] = parts[c]
                for move in tot_copies(c):
                    move.start()

    def finish(half):
        other = mapped[:, n:] if half == 0 else mapped[:, :n]
        side = 0 if half == 0 else 1
        cols = slice(half * n, (half + 1) * n)
        whole = dbc[half] + dot(dsim[...].astype(bf16), other, side, 0)
        whole = scale * whole * dsbc[:, cols]
        dbc_out[half] = whole.astype(bf16)
        for o in range(1, heads):
            head_copy(half, o).start()

        @pl.when(me > 0)
        def _():
            for o in range(heads):
                nbc_copy(half, o).start()

        head_in[half, hd] = dbc_out[half]
        for k in range(taps):
            bct[half * taps + k : half * taps + k + 1, :] = jnp.sum(
                whole * bp[pl.ds(first + k, tokens), cols], axis=0, keepdims=True
            )

    g_load(0).wait()
    phase_u(0)

    for load in small[1:]:
        load.wait()

    @pl.when(me > 0)
    def _():
        halo_bc().wait_recv()

    bp[0:8, :] = halo_b[...].astype(f32)[8:]
    bp[8:, :] = bcv[...].astype(f32)
    value, slope = silu_parts(conv_taps(bp, cbcv[...], first, tokens))
    mapped[...] = value.astype(bf16)
    dsbc[...] = slope
    unit = ones_where(iota((tokens, tokens), 0) == iota((tokens, tokens), 1))
    mapped_t[...] = dot(mapped[...], unit, 0, 0).astype(bf16)
    send_u(0, 0)

    @pl.when(back == 0)
    def _():
        for e in range(2):
            advance(e, back, backward, u_all, q_all)

    halves = 2 * groups
    shift = groups - 3 - LAG

    def due(s, base, hops, early=0):
        gap = lax.min(hops, 1) * (shift + 2 - early + LAG * hops)
        c = lax.min(s - base, (s - gap + 4096) // 2 - 2048)
        return c, (c >= 0) & (c < groups) & (lax.max(base + c, 2 * c + gap) == s)

    slots = halves + groups + max(LAG * (seq - 2), RIDE * (seq - 1) - 2)

    both = lax.max(halves + groups - 1, halves + shift + LAG * lax.max(me, back))

    @pl.loop(0, slots)
    def _(s):
        @pl.when(s < groups)
        def _():
            phase_a(s)

        @pl.when((s < groups) & (me == 0))
        def _():
            for e in range(2):
                advance(2 * s + e, me, forward, s_all, p_all)

        @pl.when((s < groups - 1) & (back == 0))
        def _():
            for e in range(2):
                advance(2 * s + 2 + e, back, backward, u_all, q_all)

        @pl.when(s == groups - 1)
        def _():
            setup_b()

        @pl.when((s >= groups) & (s < halves))
        def _():
            phase_b(s - groups)

        cq, has_q = due(s, groups + groups * lax.min(back, 1), back, 1)
        cr, has_r = due(s, groups + 1 + lax.min(back, 1) * (groups - 3 + RIDE * back) - EARLY * lax.max(1 - me, 0), back)
        cp, has_p = due(s, halves, me)

        @pl.when(has_q)
        def _():
            phase_q(cq)

        hf = s - shift - LAG * me
        hb = s - shift + 1 - LAG * back

        @pl.when((me > 0) & (hf >= 0) & (hf < halves))
        def _():
            advance(hf, me, forward, s_all, p_all)

        @pl.when((back > 0) & (hb >= 0) & (hb < halves))
        def _():
            advance(hb, back, backward, u_all, q_all)

        @pl.when(has_q & (cq == groups - 1))
        def _():
            finish(0)

        @pl.when(has_p)
        def _():
            phase_p(cp)

            @pl.when(cp == groups - 1)
            def _():
                finish(1)

        @pl.when(s == both)
        def _():
            bct_in[rank] = bct[...]

            @pl.loop(1, peers)
            def _(o):
                bct_copy(o).start()

        @pl.when(s == groups + 1 + RIDE * back)
        def _():
            ride(groups)

        @pl.when(has_r)
        def _():
            ride(cr)


    @pl.when(me < seq - 1)
    def _():
        at = iota((16, 1), 0)
        for c in range(groups):
            edge_copy(c).wait_recv()
            after = next_x[c].astype(f32)
            for j, tile in enumerate(tiles):
                fixed = tails[c, :, tile]
                lo = c * columns + j * 128
                for r in range(taps - 1):
                    row = jnp.zeros((1, 128), f32)
                    for k in range(r + 1):
                        e = j * (taps - 1) + r - k
                        row = row + cwv[k : k + 1, lo : lo + 128] * after[e : e + 1]
                    fixed = fixed + jnp.where(at == 16 - (taps - 1) + r, row, 0.0)
                gx_ref[tokens - 16 :, lo : lo + 128] = fixed.astype(bf16)

    for half in range(2):
        for o in range(1, heads):
            at = lax.rem(hd + o, heads)
            arrived(head_in.at[half, at], head_recv.at[half, at], dbc_out.at[half])
        cols = slice(half * n, (half + 1) * n)
        full = head_in[half, 0].astype(f32)
        for h in range(1, heads):
            full = full + head_in[half, h].astype(f32)
        dbp[0:tokens, cols] = full

        @pl.when(me == seq - 1)
        def _():
            dbp[tokens:, cols] = jnp.zeros((8, n), f32)

        @pl.when(me < seq - 1)
        def _():
            for h in range(heads):
                arrived(next_bc.at[half, h], nbc_recv.at[half, h], dbc_out.at[half, 0:16])
            rows = next_bc[half, 0].astype(f32)
            for h in range(1, heads):
                rows = rows + next_bc[half, h].astype(f32)
            dbp[tokens:, cols] = rows[0:8]

    grad = jnp.zeros((tokens, 2 * n), f32)
    for k in range(taps):
        grad = grad + cbcv[k : k + 1, :] * dbp[pl.ds(taps - 1 - k, tokens), :]
    gbc_ref[...] = grad.astype(bf16)

    @pl.loop(1, peers)
    def _(o):
        at = lax.rem(rank + o, peers)
        arrived(bct_in.at[at], bct_recv.at[at], bct)

    bsum = bct_in[0]
    for i in range(1, peers):
        bsum = bsum + bct_in[i]
    bsum_ref[...] = bsum

    @pl.loop(0, groups + 1)
    def _(c):
        @pl.when(jnp.logical_not(owner(c) & (me == 0)))
        def _():
            arrived(tot.at[c], tot_recv.at[c], tot.at[c])

    sums_ref[...] = tot[...]

    for half in range(2):
        for o in range(1, heads):
            head_copy(half, o).wait_send()

    @pl.loop(1, peers)
    def _(o):
        bct_copy(o).wait_send()

    @pl.when(me < seq - 1)
    def _():
        halo_bc().wait_send()
        for c in range(groups):
            halo_x(c).wait_send()

        @pl.loop(0, halves)
        def _(h):
            forward(h).wait_send()

    @pl.when(me > 0)
    def _():
        for half in range(2):
            for o in range(heads):
                nbc_copy(half, o).wait_send()

        @pl.loop(0, halves)
        def _(h):
            backward(h).wait_send()

        @pl.loop(0, groups)
        def _(c):
            edge_copy(c).wait_send()

    @pl.loop(0, groups + 1)
    def _(c):
        @pl.when(jnp.logical_not(owner(c)))
        def _():
            core_copy(c).wait_send()

        @pl.when(owner(c) & (me > 0))
        def _():
            ride_copy(c).wait_send()

        @pl.when(owner(c) & (me == 0))
        def _():
            for move in tot_copies(c):
                move.wait_send()


def final_kernel(
    head_dim, norm, pieces, y_in, gx_in, gbc_in, tot, bsum, y_out, gx_out, gbc_out, sums_out, bsum_out,
    skip_out, sums, sums_bc, skips, sem,
):
    tokens = y_in.shape[0]
    groups = tot.shape[0] - 1
    columns = 2 * tot.shape[2]
    taps = sums.shape[0]
    count = skips.shape[1]
    block = tokens // pieces
    moves = []
    for i in range(pieces):
        at = pl.ds(i * block, block)
        moves.append(pltpu.make_async_copy(y_in.at[at], y_out.at[at], sem.at[0, i]))
        moves.append(pltpu.make_async_copy(gx_in.at[at], gx_out.at[at], sem.at[1, i]))
    moves.append(pltpu.make_async_copy(gbc_in, gbc_out, sem.at[2, 0]))
    for move in moves:
        move.start()
    tiles = columns // 128
    for c in range(groups):
        for j in range(tiles):
            lo = c * columns + j * 128
            row = (j % 2) * taps
            sums[:, lo : lo + 128] = norm * tot[
                c, row : row + taps, j // 2 * 128 : (j // 2 + 1) * 128
            ]
    rest = tot[groups, :, 0 : groups * tiles]
    near = 128 // head_dim
    pick = ones_where(
        iota((groups * tiles, count), 0) == iota((groups * tiles, count), 1) // near
    )
    found = jnp.zeros((8, count), f32)
    for _ in range(3):
        piece = rest.astype(bf16)
        rest = rest - piece.astype(f32)
        found = found + dot(piece, pick, 1, 0)
    own = iota((8, count), 1) % near == iota((8, count), 0)
    skips[...] = jnp.sum(jnp.where(own, found, 0.0), axis=0, keepdims=True) * (
        norm * float(head_dim) ** (-0.5)
    )
    half = bsum.shape[1]
    sums_bc[:, :half] = bsum[0:taps] * norm
    sums_bc[:, half:] = bsum[taps:] * norm
    late = [
        pltpu.make_async_copy(src, dst, sem.at[2, i + 1])
        for i, (src, dst) in enumerate(((sums, sums_out), (sums_bc, bsum_out), (skips, skip_out)))
    ]
    for move in late:
        move.start()
    for move in moves + late:
        move.wait()


def local(x_input, bc_input, decays, conv_x, conv_bc, skip_gain, grad_out):
    x = x_input[0]
    bc = bc_input[0]
    d = decays[0]
    g = grad_out[0]
    tokens, channels = x.shape
    taps = conv_x.shape[0]
    count = d.shape[0]
    head_dim = channels // count
    n = bc.shape[1] // 2
    scale = float(n) ** (-0.5)
    seq = lax.axis_size("seq")
    heads = lax.axis_size("head")
    cores = lax.axis_size("dp")
    peers = seq * heads * cores
    width = next(k for k in (8, 4) if count % k == 0)
    groups = count // width
    columns = width * head_dim
    norm = float(tokens * seq * cores) ** (-0.5)
    sizes = (seq, heads, cores)

    held = pltpu.with_memory_space_constraint

    def out(shape, dtype):
        return jax.ShapeDtypeStruct(shape, dtype)

    dma = pltpu.SemaphoreType.DMA
    vmem = pltpu.VMEM
    anywhere = pl.BlockSpec(memory_space=pl.ANY)
    inside = pl.BlockSpec(memory_space=vmem)
    wide = (groups, tokens, columns)
    state = (2 * groups, n, columns // 2)
    part = (groups + 1, 8, columns // 2)
    y, gx, gbc, sums, bsum = pl.pallas_call(
        functools.partial(main_kernel, head_dim, scale, sizes),
        in_specs=[anywhere] * 7,
        out_specs=[inside] * 5,
        out_shape=[
            vmem((tokens, channels), bf16), vmem((tokens, channels), bf16),
            vmem((tokens, 2 * n), bf16), vmem(part, f32), vmem((8, n), f32),
        ],
        scratch_shapes=[
            vmem(wide, bf16), vmem(wide, bf16), vmem((tokens, 2 * n), bf16),
            vmem((count, tokens), f32), vmem((taps, channels), f32), vmem((taps, 2 * n), f32), pltpu.SMEM((count,), f32),
            vmem(wide, bf16), vmem(wide, bf16), vmem(wide, bf16), vmem(wide, bf16),
            vmem(wide, bf16), vmem(wide, bf16), vmem(wide, f32), vmem(wide, f32),
            vmem(state, bf16), vmem((2 * groups + 2, n, columns // 2), bf16), vmem(state, bf16),
            vmem(state, bf16),
            vmem((2 * groups, 1, columns // 2), f32), vmem((2 * tokens, 2 * count), bf16),
            vmem((count, tokens), f32),
            vmem((groups, width, tokens), f32), vmem((groups, tokens, width), f32),
            vmem((16, channels), bf16), vmem((16, 2 * n), bf16),
            vmem((tokens, 2 * n), bf16), vmem((2 * n, tokens), bf16),
            vmem((tokens, 2 * n), f32), vmem((tokens + 8, 2 * n), f32),
            vmem((columns // 128, tokens + 8, 128), f32),
            vmem((tokens, tokens), f32), vmem((tokens, tokens), f32),
            vmem((2, tokens, n), f32),
            vmem((groups, columns // 128, 8, 128), f32),
            vmem((groups, 16, columns), f32), vmem((groups, 16, 128), bf16),
            vmem((groups, 16, 128), bf16), vmem(part, f32), vmem(part, f32), vmem(part, f32),
            vmem(part, f32), vmem((2, tokens, n), bf16), vmem((2, heads, tokens, n), bf16),
            vmem((2, heads, 16, n), bf16), vmem((tokens + 8, 2 * n), f32),
            vmem((8, n), f32), vmem((peers, 8, n), f32),
            dma((groups,)), dma((groups,)), dma((5,)), dma((groups + 1,)), dma((groups + 1,)),
            dma((2 * groups,)), dma((2 * groups,)), dma((2 * groups,)), dma((2 * groups,)),
            dma((groups,)), dma((groups,)), dma((groups + 1,)), dma((groups + 1,)),
            dma((groups + 1,)), dma((groups + 1,)), dma((groups + 1, seq * cores)),
            dma((groups + 1,)),
            dma((2, heads)), dma((2, heads)), dma((2, heads)), dma((2, heads)),
            dma((peers,)), dma((peers,)),
        ],
        compiler_params=pltpu.CompilerParams(
            vmem_limit_bytes=44 * 1024 * 1024, collective_id=0, has_side_effects=True,
        ),
        name="main",
    )(*(held(a, pltpu.HBM) for a in (x, bc, d, conv_x, conv_bc, skip_gain, g)))

    pieces = 4
    y, gx, gbc, taps_x, taps_bc, skips = pl.pallas_call(
        functools.partial(final_kernel, head_dim, norm, pieces),
        in_specs=[inside] * 5,
        out_specs=[anywhere] * 6,
        out_shape=[
            out((tokens, channels), bf16), out((tokens, channels), bf16),
            out((tokens, 2 * n), bf16), out((taps, channels), f32), out((taps, 2 * n), f32),
            out((1, count), f32),
        ],
        scratch_shapes=[
            vmem((taps, channels), f32), vmem((taps, 2 * n), f32), vmem((1, count), f32),
            dma((3, 4)),
        ],
        compiler_params=pltpu.CompilerParams(vmem_limit_bytes=16 * 1024 * 1024),
        name="final",
    )(y, gx, gbc, sums, bsum)
    return y[None], gx[None], gbc[None], taps_x, taps_bc, skips.reshape(count)


def solution(mesh):
    return jax.shard_map(
        local,
        mesh=mesh,
        in_specs=(
            P(("groups", "dp"), "seq", "head"),
            P(("groups", "dp"), "seq", None),
            P(("groups", "dp"), "head", "seq"),
            P(None, "head"),
            P(),
            P("head"),
            P(("groups", "dp"), "seq", "head"),
        ),
        out_specs=(
            P(("groups", "dp"), "seq", "head"),
            P(("groups", "dp"), "seq", "head"),
            P(("groups", "dp"), "seq", None),
            P("groups", "head"),
            P("groups", None),
            P(("groups", "head")),
        ),
        check_vma=False,
    )
```
